128 devices in a mesh: sx: 8 (over z, core), sy: 16 (over y, x).
Axes of the slice: x: 4, y: 4, z: 4, core: 2. Of those that a mesh axis runs over, the one named last changes fastest.
Arguments:
- grid_points: float32 [3, 262144], P(None, ('sx', 'sy')), may hold values from 0 to 16
- weighted_density: float32 [262144], P(('sx', 'sy')), may hold values from -0.15 to 0.15
- point_slot: int32 [262144], P(('sx', 'sy')), may hold values from 0 to 127, as said below
- near_slot: int32 [2048, 64], P(('sx', 'sy')), may hold values from 0 to 127, as said below
- slot_atom: int32 [16384], replicated, may hold values from 0 to 2047, as said below
- atom_pos: float32 [3, 2048], replicated, may hold values from 0 to 16
- decay_rates: float32 [128], replicated, may hold values from 0.5 to 2
- green: float32 [7, 128, 128], replicated, may hold values from -0.5 to 0.5
- moment_table: float32 [3, 128], replicated, may hold values from 0.5 to 5
Outputs:
- potential: float32 [262144], P(('sx', 'sy'))
The draws below stay inside these ranges and needn't reach their ends.
Inputs may be any that keep to these rules, and one draw needn't show every extreme that they name: `slot_atom`: atoms are owned in ranges in device order: devices below 32 own 2 * 16 atoms each, those below 64 own 16, the rest 16 // 2; the 128 atoms listed by one device are distinct; at most 2 of them have one owner, and in every draw one owner has exactly 2 atoms in every device's list. `near_slot`: the 64 entries of one batch are distinct. `point_slot`: each point's entry is one of its batch's near entries.
All inputs are finite; a program needn't handle non-finite values.
Results may differ from the reference program's by a relative error of at most 0.004.
Values may be sent and summed in bfloat16 or wider, within the bound.
A program may use at most 64 MiB of HBM per device.

```python
import math
import jax
import jax.numpy as jnp
import numpy as np
from jax import lax

HARM = 49
NRAD = 128
PTS_DEV = 2048
BATCH_PTS = 128
BATCHES = 16
BATCHES_ALL = 2048
POINTS = 262144
NEAR = 64
SLOTS = 128
OWN_AVG = 16
ATOMS = 2048
N_SX = 8
N_SY = 16
DEVICES = 128


def routing_tables(key):
    devices = DEVICES
    owner_rank = jnp.arange(devices)
    counts = jnp.where(owner_rank < devices // 4, 2 * OWN_AVG, jnp.where(owner_rank < devices // 2, OWN_AVG, OWN_AVG // 2))
    range_ends = jnp.cumsum(counts)
    range_starts = range_ends - counts
    atom_index = jnp.arange(ATOMS)
    owner = jnp.sum((range_ends[None, :] <= atom_index[:, None]).astype(jnp.int32), axis=1)
    capacity = 2 * SLOTS // devices
    half_capacity = SLOTS // devices
    device_index = jnp.arange(devices)
    scores = jax.random.randint(jax.random.fold_in(key, 12), (devices, devices), 0, 4096) * devices + device_index[None, :]
    favoured = jax.random.randint(jax.random.fold_in(key, 13), (), 0, devices)
    scores = jnp.where(device_index[None, :] == favoured, -1, scores)
    choose_rank = jnp.argsort(jnp.argsort(scores, axis=1), axis=1)
    take_count = jnp.where(choose_rank < devices // 4, capacity, jnp.where(choose_rank < 3 * devices // 4, half_capacity, 0))
    shifts = jax.random.randint(jax.random.fold_in(key, 14), (devices, devices), 0, 1 << 20) % counts[None, :]
    local_index = atom_index - range_starts[owner]
    chosen = (local_index[None, :] + shifts[:, owner]) % counts[owner][None, :] < take_count[:, owner]
    order_scores = jax.random.randint(jax.random.fold_in(key, 15), (devices, ATOMS), 0, 4096) * ATOMS + atom_index[None, :]
    order_scores = jnp.where(chosen, order_scores, 1 << 30)
    slot_atom = jnp.argsort(order_scores, axis=1)[:, :SLOTS].astype(jnp.int32).reshape(-1)
    near_scores = jax.random.randint(jax.random.fold_in(key, 16), (BATCHES_ALL, SLOTS), 0, 4096) * SLOTS + jnp.arange(SLOTS)[None, :]
    near_slot = jnp.argsort(near_scores, axis=1)[:, :NEAR].astype(jnp.int32)
    pick_slot = jax.random.randint(jax.random.fold_in(key, 17), (BATCHES_ALL, BATCH_PTS), 0, NEAR)
    point_slot = jnp.take_along_axis(near_slot, pick_slot, axis=1).reshape(-1).astype(jnp.int32)
    return (slot_atom, near_slot, point_slot)


def draw_slot_atom(key, part):
    return routing_tables(key)[0]


def draw_near_slot(key, part):
    return routing_tables(key)[1]


def draw_point_slot(key, part):
    return routing_tables(key)[2]


def block_levels(stream_key, dims, cuts, least, high):
    loudness = 1.0
    for axis_at, shards_of in cuts:
        steps = jax.random.uniform(jax.random.fold_in(jax.random.fold_in(stream_key, 6), axis_at), (shards_of,), jnp.float32, least / len(cuts), high / len(cuts))
        loudness = loudness * jnp.repeat(jnp.exp(steps), dims[axis_at] // shards_of).reshape((-1,) + (1,) * (len(dims) - 1 - axis_at))
    return loudness


def bell_draw(own_key, extent, scale, reach, shards=(), held_as=jnp.bfloat16):
    values = jax.random.normal(own_key, extent, jnp.float32) * scale
    if len(shards) > 0:
        values = block_levels(own_key, extent, shards, -0.22, 0.18) * values
    return jnp.clip(values, min=-reach, max=reach).astype(held_as)


def setup_inputs(seed: int = 0) -> dict:
    streams_of = jax.random.split(jax.random.key(seed), 10)
    grid_points = jnp.clip(16.0 * jax.random.uniform(streams_of[0], (3, POINTS), jnp.float32) ** block_levels(streams_of[0], (3, POINTS), ((1, 128),), -0.2, 0.2), 0.0, 16.0)
    weighted_density = bell_draw(streams_of[1], (POINTS,), 0.025, 0.15, ((0, 128),), jnp.float32)
    point_slot = draw_point_slot(jax.random.fold_in(streams_of[9], 71), 0)
    near_slot = draw_near_slot(jax.random.fold_in(streams_of[9], 71), 0)
    slot_atom = draw_slot_atom(jax.random.fold_in(streams_of[9], 71), 0)
    atom_pos = jnp.clip(jax.random.uniform(streams_of[5], (3, ATOMS), jnp.float32, 0.0, 16.0), 0.0, 16.0)
    decay_rates = jnp.clip(jnp.exp(jax.random.uniform(streams_of[6], (NRAD,), jnp.float32, math.log(0.5), math.log(2.0))), 0.5, 2.0)
    green = bell_draw(streams_of[7], (7, NRAD, NRAD), NRAD ** -0.5, 0.5, (), jnp.float32)
    moment_table = jnp.clip(jnp.exp(jax.random.uniform(streams_of[8], (3, NRAD), jnp.float32, math.log(0.5), math.log(5.0))), 0.5, 5.0)
    return {"grid_points": grid_points, "weighted_density": weighted_density, "point_slot": point_slot, "near_slot": near_slot, "slot_atom": slot_atom, "atom_pos": atom_pos, "decay_rates": decay_rates, "green": green, "moment_table": moment_table}


def harmonic_table(comp_x, comp_y, comp_z, top_degree):
    square = comp_x * comp_x + comp_y * comp_y + comp_z * comp_z
    cosines = [jnp.ones_like(comp_x)]
    sine_terms = [jnp.zeros_like(comp_x)]
    for m in range(1, top_degree + 1):
        cosines.append(cosines[m - 1] * comp_x - sine_terms[m - 1] * comp_y)
        sine_terms.append(cosines[m - 1] * comp_y + sine_terms[m - 1] * comp_x)
    legendre = {}
    for m in range(top_degree + 1):
        legendre[m, m] = float(math.prod(range(1, 2 * m, 2))) * cosines[0]
        if m + 1 <= top_degree:
            legendre[m + 1, m] = (2 * m + 1) * comp_z * legendre[m, m]
        for l in range(m + 2, top_degree + 1):
            legendre[l, m] = ((2 * l - 1) * comp_z * legendre[l - 1, m] - (l + m - 1) * square * legendre[l - 2, m]) / (l - m)
    stacked = []
    for l in range(top_degree + 1):
        for m in range(l + 1):
            factor = math.sqrt((2 * l + 1) / (4 * math.pi) * math.factorial(l - m) / math.factorial(l + m))
            if m == 0:
                stacked.append(factor * legendre[l, 0])
            else:
                factor = factor * math.sqrt(2.0)
                stacked.append(factor * legendre[l, m] * cosines[m])
                stacked.append(factor * legendre[l, m] * sine_terms[m])
    return jnp.stack(stacked)

def soft_geometry(delta):
    distance = jnp.sqrt(lax.optimization_barrier(jnp.sum(delta * delta, axis=0)) + 1.0)
    return (distance, delta / distance)

def shell_layout(decay_rates):
    count = decay_rates.shape[0]
    spacing = 27.0 / (count - 1)
    centres = 1.0 + spacing * jnp.arange(count).astype(decay_rates.dtype)
    return (centres, spacing)

def shell_values(distance, rates, centres, spacing):
    offset = (distance - centres) / spacing
    return jnp.exp(-rates * offset * offset)

def project_points(points, density, slot_of_point, near_list, atom_list, atom_pos, decay_rates):
    batches = near_list.shape[0]
    batch_pts = points.shape[1] // batches
    atom_ids = atom_list[slot_of_point]
    delta = (points - atom_pos[:, atom_ids]).reshape(3, batches, batch_pts)
    distance, unit_vec = soft_geometry(delta)
    harmonics = harmonic_table(unit_vec[0], unit_vec[1], unit_vec[2], 6)
    projected = (density.reshape(1, batches, batch_pts) * harmonics).astype(jnp.bfloat16)
    centres, spacing = shell_layout(decay_rates)
    radial = shell_values(distance[None], decay_rates[:, None, None], centres[:, None, None], spacing).astype(jnp.bfloat16)
    selector = (slot_of_point.reshape(batches, batch_pts)[:, None, :] == near_list[:, :, None]).astype(jnp.bfloat16)
    weighted = selector[:, :, None, :] * jnp.moveaxis(projected, 0, 1)[:, None, :, :]
    terms = jnp.einsum('bjip,kbp->bjik', weighted.astype(jnp.float32), radial.astype(jnp.float32))
    flat = terms.reshape(batches * near_list.shape[1], -1)
    return jax.ops.segment_sum(flat, near_list.reshape(-1), num_segments=atom_list.shape[0])

def apply_green(coefficients, green):
    pieces = []
    for l in range(7):
        pieces.append(jnp.einsum('aik,kn->ain', coefficients[:, l * l:(l + 1) * (l + 1)], green[l], precision=lax.Precision.HIGHEST))
    return jnp.concatenate(pieces, axis=1)

def low_moments(coefficients, moment_table):
    degrees = np.array([0, 1, 1, 1, 2, 2, 2, 2, 2])
    table = moment_table[degrees]
    return jnp.einsum('aik,ik->ia', coefficients[:, :9], table, precision=lax.Precision.HIGHEST)

def near_field(points, near_ids, near_coef, atom_pos, decay_rates):
    batches = near_ids.shape[0]
    batch_pts = points.shape[1] // batches
    grouped = points.reshape(3, batches, batch_pts)
    delta = grouped[:, :, None, :] - atom_pos[:, near_ids][..., None]
    distance, unit_vec = soft_geometry(delta)
    harmonics = harmonic_table(unit_vec[0], unit_vec[1], unit_vec[2], 6)
    centres, spacing = shell_layout(decay_rates)
    radial = shell_values(distance[:, :, None, :], decay_rates[None, None, :, None], centres[None, None, :, None], spacing).astype(jnp.bfloat16)
    values = jnp.einsum('bjik,bjkp->bjip', near_coef.astype(jnp.float32), radial.astype(jnp.float32))
    return lax.optimization_barrier(jnp.sum(values * jnp.moveaxis(harmonics, 0, 2), axis=(1, 2))).reshape(-1)

def far_field(points, near_ids, moments, atom_pos):
    batches = near_ids.shape[0]
    batch_pts = points.shape[1] // batches
    grouped = jnp.moveaxis(points.reshape(3, batches, batch_pts), 1, 0)
    atom_index = jnp.arange(atom_pos.shape[1])

    def one_batch(inputs):
        coords, ids = inputs
        delta = coords[:, :, None] - atom_pos[:, None, :]
        distance, unit_vec = soft_geometry(delta)
        harmonics = harmonic_table(unit_vec[0], unit_vec[1], unit_vec[2], 2)
        inverse = 1.0 / distance
        keep = 1.0 - lax.optimization_barrier(jnp.sum((ids[:, None] == atom_index[None, :]).astype(moments.dtype), axis=0))
        scaled = moments * keep[None, :]
        total = harmonics[0] * scaled[0][None, :] * inverse
        total = total + lax.optimization_barrier(jnp.sum(harmonics[1:4] * scaled[1:4, None, :], axis=0)) * inverse * inverse
        total = total + lax.optimization_barrier(jnp.sum(harmonics[4:9] * scaled[4:9, None, :], axis=0)) * inverse * inverse * inverse
        return lax.optimization_barrier(jnp.sum(total, axis=1))
    return lax.map(one_batch, (grouped, near_ids)).reshape(-1)

def reference(grid_points, weighted_density, point_slot, near_slot, slot_atom, atom_pos, decay_rates, green, moment_table):
    devices = N_SX * N_SY
    points_dev = jnp.moveaxis(grid_points.reshape(3, devices, PTS_DEV), 1, 0)
    density_dev = weighted_density.reshape(devices, PTS_DEV)
    slots_dev = point_slot.reshape(devices, PTS_DEV)
    near_dev = near_slot.reshape(devices, BATCHES, NEAR)
    lists_dev = slot_atom.reshape(devices, SLOTS)

    def project_one(inputs):
        points, density, slot_of_point, near_list, atom_list = inputs
        return project_points(points, density, slot_of_point, near_list, atom_list, atom_pos, decay_rates).astype(jnp.bfloat16)
    partials = lax.map(project_one, (points_dev, density_dev, slots_dev, near_dev, lists_dev))
    width = HARM * NRAD
    coefficients = jax.ops.segment_sum(partials.reshape(-1, width).astype(jnp.float32), slot_atom, num_segments=ATOMS)
    coefficients = coefficients.reshape(ATOMS, HARM, NRAD)
    potential_coefs = apply_green(coefficients, green).astype(jnp.bfloat16)
    moments = low_moments(coefficients, moment_table)

    def evaluate_one(inputs):
        points, near_list, atom_list = inputs
        near_ids = atom_list[near_list]
        near_coef = potential_coefs[near_ids]
        return near_field(points, near_ids, near_coef, atom_pos, decay_rates) + far_field(points, near_ids, moments, atom_pos)
    result = lax.map(evaluate_one, (points_dev, near_dev, lists_dev))
    return result.reshape(-1)
```

```python
import math

import jax
import jax.numpy as jnp
import numpy as np
from jax import lax
from jax.experimental import pallas as pl
from jax.experimental.pallas import tpu as pltpu
from jax.sharding import PartitionSpec as P

HARM = 49
NRAD = 128
OWN_AVG = 16
OWN = 32


def harmonic_table(comp_x, comp_y, comp_z, top_degree):
    square = comp_x * comp_x + comp_y * comp_y + comp_z * comp_z
    cosines = [jnp.ones_like(comp_x)]
    sine_terms = [jnp.zeros_like(comp_x)]
    for m in range(1, top_degree + 1):
        cosines.append(cosines[m - 1] * comp_x - sine_terms[m - 1] * comp_y)
        sine_terms.append(cosines[m - 1] * comp_y + sine_terms[m - 1] * comp_x)
    legendre = {}
    for m in range(top_degree + 1):
        legendre[m, m] = float(math.prod(range(1, 2 * m, 2))) * cosines[0]
        if m + 1 <= top_degree:
            legendre[m + 1, m] = (2 * m + 1) * comp_z * legendre[m, m]
        for l in range(m + 2, top_degree + 1):
            legendre[l, m] = (
                (2 * l - 1) * comp_z * legendre[l - 1, m]
                - (l + m - 1) * square * legendre[l - 2, m]
            ) / (l - m)
    stacked = []
    for l in range(top_degree + 1):
        for m in range(l + 1):
            factor = math.sqrt(
                (2 * l + 1) / (4 * math.pi) * math.factorial(l - m) / math.factorial(l + m)
            )
            if m == 0:
                stacked.append(factor * legendre[l, 0])
            else:
                factor = factor * math.sqrt(2.0)
                stacked.append(factor * legendre[l, m] * cosines[m])
                stacked.append(factor * legendre[l, m] * sine_terms[m])
    return jnp.stack(stacked)


def soft_geometry(delta):
    distance = jnp.sqrt(jnp.sum(delta * delta, axis=0) + 1.0)
    return (distance, delta / distance)


def shell_layout(decay_rates):
    count = decay_rates.shape[0]
    spacing = 27.0 / (count - 1)
    centres = 1.0 + spacing * jnp.arange(count).astype(decay_rates.dtype)
    return (centres, spacing)


def shell_values(distance, rates, centres, spacing):
    offset = (distance - centres) / spacing
    return jnp.exp(-rates * offset * offset)


def project_points(points, density, slot_of_point, atom_list, atom_pos, decay_rates):
    listed = atom_list.shape[0]
    atom_ids = atom_list[slot_of_point]
    delta = points - atom_pos[:, atom_ids]
    distance, unit_vec = soft_geometry(delta)
    harmonics = harmonic_table(unit_vec[0], unit_vec[1], unit_vec[2], 6)
    projected = (density[None, :] * harmonics).astype(jnp.bfloat16)
    centres, spacing = shell_layout(decay_rates)
    radial = shell_values(
        distance[None, :], decay_rates[:, None], centres[:, None], spacing
    ).astype(jnp.bfloat16)
    onehot = (slot_of_point[None, :] == jnp.arange(listed)[:, None]).astype(jnp.bfloat16)
    weighted = onehot[:, None, :] * projected[None, :, :]
    terms = jnp.einsum("tip,kp->tik", weighted, radial, preferred_element_type=jnp.float32)
    return terms.reshape(listed, -1)


def apply_green(coefficients, green):
    pieces = []
    for l in range(7):
        pieces.append(
            jnp.einsum(
                "aik,kn->ain",
                coefficients[:, l * l : (l + 1) * (l + 1)],
                green[l],
                precision=lax.Precision.HIGHEST,
            )
        )
    return jnp.concatenate(pieces, axis=1)


def low_moments(coefficients, moment_table):
    degrees = np.array([0, 1, 1, 1, 2, 2, 2, 2, 2])
    table = moment_table[degrees]
    return jnp.einsum("aik,ik->ia", coefficients[:, :9], table, precision=lax.Precision.HIGHEST)


HP = 64
YR = 56


def y_factor(l, m):
    factor = math.sqrt(
        (2 * l + 1) / (4 * math.pi) * math.factorial(l - m) / math.factorial(l + m)
    )
    return factor if m == 0 else factor * math.sqrt(2.0)


def harmonic_rows(x, y, z, top, emit):
    square = x * x + y * y + z * z
    cos_m, sin_m = None, None
    for m in range(top + 1):
        if m == 1:
            cos_m, sin_m = x, y
        elif m > 1:
            cos_m, sin_m = cos_m * x - sin_m * y, cos_m * y + sin_m * x
        double = float(math.prod(range(1, 2 * m, 2)))
        ladder = {}
        for l in range(m, top + 1):
            if l == m + 1:
                ladder[l] = z * float(2 * m + 1)
            elif l == m + 2:
                ladder[l] = z * ladder[l - 1] * ((2 * l - 1) / 2) - square * ((l + m - 1) / 2)
            elif l > m + 2:
                ladder[l] = z * ladder[l - 1] * ((2 * l - 1) / (l - m)) - square * ladder[l - 2] * (
                    (l + m - 1) / (l - m)
                )
            scale = y_factor(l, m) * double
            part = ladder[l] * scale if l > m else scale
            if m == 0:
                emit(l * l, part if l > m else jnp.full_like(x, part))
            else:
                emit(l * l + 2 * m - 1, cos_m * part)
                emit(l * l + 2 * m, sin_m * part)


def split3(value):
    high = value.astype(jnp.bfloat16).astype(jnp.float32)
    rest = value - high
    middle = rest.astype(jnp.bfloat16).astype(jnp.float32)
    return high, middle, rest - middle


FEATURES = 9
FEATURE_ROWS = 6 * FEATURES + 3
FAR_ROWS = 64


def far_tables(atoms_ref, moments_ref, rows_ref, table_ref):
    atoms = atoms_ref.shape[1]
    ax = atoms_ref[0:1, :] - 8.0
    ay = atoms_ref[1:2, :] - 8.0
    az = atoms_ref[2:3, :] - 8.0
    mom = [moments_ref[i : i + 1, :] for i in range(9)]
    one, nil = jnp.ones_like(ax), jnp.zeros_like(ax)
    n10, n11 = y_factor(1, 0), y_factor(1, 1)
    vx, vy, vz = mom[2] * n11, mom[3] * n11, mom[1] * n10
    f20, f21, f22 = y_factor(2, 0), 3.0 * y_factor(2, 1), 3.0 * y_factor(2, 2)
    qzz = mom[4] * f20
    qxx = mom[7] * f22 - qzz * 0.5
    qyy = -mom[7] * f22 - qzz * 0.5
    qxz, qyz, qxy = mom[5] * f21, mom[6] * f21, mom[8] * (2.0 * f22)
    gx = -(2.0 * qxx * ax + qxy * ay + qxz * az)
    gy = -(qxy * ax + 2.0 * qyy * ay + qyz * az)
    gz = -(qxz * ax + qyz * ay + 2.0 * qzz * az)
    const = -0.5 * (gx * ax + gy * ay + gz * az)
    norm = ax * ax + ay * ay + az * az + 1.0
    plans = [
        ([-2.0 * ax, -2.0 * ay, -2.0 * az, one, one, one, nil, nil, nil], norm),
        ([vx, vy, vz, nil, nil, nil, nil, nil, nil], -(vx * ax + vy * ay + vz * az)),
        ([gx, gy, gz, qxx, qyy, qzz, qxy, qxz, qyz], const),
    ]
    for q, (coefs, fixed) in enumerate(plans):
        columns = pl.ds(q * atoms, atoms)
        for f, coef in enumerate(coefs):
            high, middle, low = split3(coef)
            for r, row in enumerate((high, middle, high, low, high, middle)):
                rows_ref[6 * f + r : 6 * f + r + 1, columns] = row
        for r, row in enumerate(split3(fixed)):
            rows_ref[6 * FEATURES + r : 6 * FEATURES + r + 1, columns] = row
        rows_ref[FEATURE_ROWS:FAR_ROWS, columns] = jnp.zeros(
            (FAR_ROWS - FEATURE_ROWS, atoms), jnp.float32
        )
    table_ref[...] = rows_ref[...].astype(jnp.bfloat16)


def point_features(px, py, pz, rows_ref):
    qx, qy, qz = px - 8.0, py - 8.0, pz - 8.0
    values = [qx, qy, qz, qx * qx, qy * qy, qz * qz, qx * qy, qx * qz, qy * qz]
    for f, value in enumerate(values):
        high, middle, low = split3(value)
        for r, row in enumerate((high, high, middle, high, low, middle)):
            rows_ref[6 * f + r : 6 * f + r + 1, :] = row
    rows_ref[6 * FEATURES : FEATURE_ROWS, :] = jnp.ones((3, qx.shape[1]), jnp.float32)
    rows_ref[FEATURE_ROWS:FAR_ROWS, :] = jnp.zeros(
        (FAR_ROWS - FEATURE_ROWS, qx.shape[1]), jnp.float32
    )
    return rows_ref[...].T.astype(jnp.bfloat16)


def evaluate_kernel(
    near_smem,
    near_ref,
    points_ref,
    slot_table_ref,
    slot_pot_ref,
    atoms_ref,
    moments_ref,
    centre_ref,
    rate_ref,
    out_ref,
    far_rows,
    far_table,
    feat_rows,
    far_acc,
    y_rows,
    rho_rows,
    corr_ref,
):
    b = pl.program_id(0)
    near_count = near_ref.shape[2]
    pts = points_ref.shape[1]
    atoms = atoms_ref.shape[1]

    @pl.when(b == 0)
    def _():
        far_tables(atoms_ref, moments_ref, far_rows, far_table)
        y_rows[...] = jnp.zeros_like(y_rows)

    px, py, pz = points_ref[0:1, :], points_ref[1:2, :], points_ref[2:3, :]

    features = point_features(px, py, pz, feat_rows)
    far_acc[...] = jnp.zeros_like(far_acc)
    chunk = 256

    @pl.loop(0, atoms // chunk)
    def _(c):
        base = pl.multiple_of(c * chunk, chunk)

        def table(q):
            return far_table[:, pl.ds(pl.multiple_of(q * atoms + base, chunk), chunk)]

        square = jnp.dot(features, table(0), preferred_element_type=jnp.float32)
        linear = jnp.dot(features, table(1), preferred_element_type=jnp.float32)
        quad = jnp.dot(features, table(2), preferred_element_type=jnp.float32)
        inv = lax.rsqrt(square)
        inv2 = inv * inv
        level = moments_ref[0:1, pl.ds(base, chunk)] * y_factor(0, 0)
        value = inv * (level + inv2 * (linear + inv2 * quad))
        far_acc[...] += value[:, 0:128] + value[:, 128:256]

    far_row = jnp.sum(far_acc[...].T, axis=0, keepdims=True)

    hot = (
        lax.broadcasted_iota(jnp.int32, (slot_table_ref.shape[0], near_count), 0) == near_ref[0]
    ).astype(jnp.float32)
    info = lax.dot_general(
        hot,
        slot_table_ref[...],
        (((0,), (0,)), ((), ())),
        precision=lax.Precision.HIGHEST,
        preferred_element_type=jnp.float32,
    )
    step = 8
    corr = jnp.zeros((step, pts), jnp.float32)
    for j in range(0, near_count, step):
        part = info[j : j + step, :]
        dx = px - part[:, 0:1]
        dy = py - part[:, 1:2]
        dz = pz - part[:, 2:3]
        square = dx * dx + dy * dy + dz * dz + 1.0
        inv = lax.rsqrt(square)
        rho_rows[j : j + step, :] = square * inv
        low = {}

        def emit(i, value):
            y_rows[pl.ds(j * YR + i, step, stride=YR), :] = value
            if i < 9:
                low[i] = value

        harmonic_rows(dx * inv, dy * inv, dz * inv, 6, emit)
        term = [part[:, 3 + i : 4 + i] * low[i] for i in range(9)]
        degree1 = term[1] + term[2] + term[3]
        degree2 = (term[4] + term[5]) + (term[6] + term[7]) + term[8]
        corr = corr + inv * (term[0] + inv * (degree1 + inv * degree2))
    corr_ref[...] = corr

    centre, rate = centre_ref[...], rate_ref[...]
    unroll = 4

    def pairs(g, total):
        for v in range(unroll):
            j = g * unroll + v
            coefs = slot_pot_ref[near_smem[b, j]]
            t = (rho_rows[pl.ds(j, 1), :] - centre) * rate
            radial = jnp.exp2(-(t * t)).astype(jnp.bfloat16)
            values = jnp.dot(coefs, radial, preferred_element_type=jnp.float32)
            rows = y_rows[pl.ds(pl.multiple_of(j * YR, YR), YR), :]
            total = total + values[0:YR] * rows
        return total

    total = lax.fori_loop(
        0, near_count // unroll, pairs, jnp.zeros((YR, pts), jnp.float32)
    )
    near_row = jnp.sum(total, axis=0, keepdims=True)
    out_ref[0] = near_row + far_row - jnp.sum(corr_ref[...], axis=0, keepdims=True)


def evaluate(points, near_slot, slot_table, slot_pot, atom_pos, moments, decay_rates):
    batches, near_count = near_slot.shape
    pts = points.shape[1] // batches
    atoms = atom_pos.shape[1]
    centres, spacing = shell_layout(decay_rates)
    rate = jnp.sqrt(decay_rates * math.log2(math.e)) / spacing
    centre_full = jnp.broadcast_to(centres[:, None], (NRAD, pts))
    rate_full = jnp.broadcast_to(rate[:, None], (NRAD, pts))

    def whole(shape):
        return pl.BlockSpec(shape, lambda b, near: (0,) * len(shape))

    out = pl.pallas_call(
        evaluate_kernel,
        out_shape=jax.ShapeDtypeStruct((batches, 1, pts), jnp.float32),
        grid_spec=pltpu.PrefetchScalarGridSpec(
            num_scalar_prefetch=1,
            grid=(batches,),
            in_specs=[
                pl.BlockSpec((1, 1, near_count), lambda b, near: (b, 0, 0)),
                pl.BlockSpec((3, pts), lambda b, near: (0, b)),
                whole(slot_table.shape),
                whole(slot_pot.shape),
                whole(atom_pos.shape),
                whole(moments.shape),
                whole((NRAD, pts)),
                whole((NRAD, pts)),
            ],
            out_specs=pl.BlockSpec((1, 1, pts), lambda b, near: (b, 0, 0)),
            scratch_shapes=[
                pltpu.VMEM((FAR_ROWS, 3 * atoms), jnp.float32),
                pltpu.VMEM((FAR_ROWS, 3 * atoms), jnp.bfloat16),
                pltpu.VMEM((FAR_ROWS, pts), jnp.float32),
                pltpu.VMEM((pts, 128), jnp.float32),
                pltpu.VMEM((near_count * YR, pts), jnp.float32),
                pltpu.VMEM((near_count, pts), jnp.float32),
                pltpu.VMEM((8, pts), jnp.float32),
            ],
        ),
        compiler_params=pltpu.CompilerParams(
            dimension_semantics=("arbitrary",), vmem_limit_bytes=40 << 20
        ),
        name="evaluate",
    )(
        near_slot,
        near_slot.reshape(batches, 1, near_count),
        points,
        slot_table,
        slot_pot,
        atom_pos,
        moments,
        centre_full,
        rate_full,
    )
    return out.reshape(-1)


def per_device(
    grid_points,
    weighted_density,
    point_slot,
    near_slot,
    slot_atom,
    atom_pos,
    decay_rates,
    green,
    moment_table,
):
    count_x = lax.axis_size("sx")
    count_y = lax.axis_size("sy")
    devices = count_x * count_y
    myself = lax.axis_index("sx") * count_y + lax.axis_index("sy")
    all_lists = slot_atom.reshape(devices, -1)
    listed = all_lists.shape[1]
    capacity = 2 * listed // devices
    total_atoms = atom_pos.shape[1]
    my_list = all_lists[myself]
    batches = near_slot.shape[0]
    near_count = near_slot.shape[1]
    batch_pts = grid_points.shape[1] // batches
    block = math.gcd(batches, 4)
    groups = batches // block
    group_points = jnp.moveaxis(grid_points.reshape(3, groups, block * batch_pts), 1, 0)
    group_density = weighted_density.reshape(groups, block * batch_pts)
    group_slots = point_slot.reshape(groups, block * batch_pts)
    group_near = near_slot.reshape(groups, block, near_count)
    width = HARM * NRAD

    def project_step(total, inputs):
        points, density, slot_of_point = inputs
        return (
            total + project_points(points, density, slot_of_point, my_list, atom_pos, decay_rates),
            None,
        )

    summed, unused = lax.scan(
        project_step,
        jnp.zeros((listed, width), jnp.float32),
        (group_points, group_density, group_slots),
    )
    partial_value = summed.astype(jnp.bfloat16)
    owner_ids = jnp.arange(devices)
    counts = jnp.where(
        owner_ids < devices // 4,
        2 * OWN_AVG,
        jnp.where(owner_ids < devices // 2, OWN_AVG, OWN_AVG // 2),
    ).astype(jnp.int32)
    range_ends = jnp.cumsum(counts)
    starts = range_ends - counts
    atom_index = jnp.arange(total_atoms)
    owner = jnp.sum((range_ends[None, :] <= atom_index[:, None]).astype(jnp.int32), axis=1)
    owners_all = owner[all_lists]
    my_dest = owners_all[myself]
    slot_index = jnp.arange(listed)
    same_owner = (my_dest[:, None] == my_dest[None, :]) & (
        slot_index[None, :] < slot_index[:, None]
    )
    earlier = jnp.sum(same_owner.astype(jnp.int32), axis=1)
    send_row = my_dest * capacity + earlier
    packing = (jnp.arange(devices * capacity)[:, None] == send_row[None, :]).astype(jnp.bfloat16)
    outgoing = jnp.dot(packing, partial_value, preferred_element_type=jnp.float32).astype(
        jnp.bfloat16
    )
    mine = owners_all == myself
    recv_rank = jnp.cumsum(mine.astype(jnp.int32), axis=1) - 1
    target = jnp.where(mine, owner_ids[:, None] * capacity + recv_rank, devices * capacity)
    local_ids = jnp.where(mine, all_lists - starts[myself], OWN)
    row_owned = (
        jnp.full((devices * capacity + 1,), OWN, jnp.int32)
        .at[target.reshape(-1)]
        .set(local_ids.reshape(-1))[: devices * capacity]
    )
    incoming = lax.all_to_all(outgoing, ("sx", "sy"), split_axis=0, concat_axis=0, tiled=True)
    selector = (row_owned[None, :] == jnp.arange(OWN)[:, None]).astype(jnp.bfloat16)
    coeff_own = jnp.dot(selector, incoming, preferred_element_type=jnp.float32).reshape(
        OWN, HARM, NRAD
    )
    pot_own = apply_green(coeff_own, green).astype(jnp.bfloat16).reshape(OWN, width)
    moments_own = low_moments(coeff_own, moment_table)
    reply = jnp.dot(selector.T, pot_own, preferred_element_type=jnp.float32).astype(jnp.bfloat16)
    returned = lax.all_to_all(reply, ("sx", "sy"), split_axis=0, concat_axis=0, tiled=True)
    gathered = lax.all_gather(moments_own, ("sx", "sy"), axis=1, tiled=True)
    column = owner * OWN + atom_index - starts[owner]
    moments_all = gathered[:, column]
    slot_pot = jnp.dot(packing.T, returned, preferred_element_type=jnp.float32).astype(jnp.bfloat16)
    padded = jnp.pad(slot_pot.reshape(listed, HARM, NRAD), ((0, 0), (0, HP - HARM), (0, 0)))
    slot_table = jnp.concatenate([atom_pos[:, my_list], moments_all[:, my_list]], axis=0).T
    slot_table = jnp.pad(slot_table, ((0, 0), (0, 128 - slot_table.shape[1])))
    return evaluate(
        grid_points, near_slot, slot_table, padded, atom_pos, moments_all, decay_rates
    )


def solution(mesh):
    return jax.shard_map(
        per_device,
        mesh=mesh,
        in_specs=(
            P(None, ("sx", "sy")),
            P(("sx", "sy")),
            P(("sx", "sy")),
            P(("sx", "sy"), None),
            P(),
            P(),
            P(),
            P(),
            P(),
        ),
        out_specs=P(("sx", "sy")),
        check_vma=False,
    )
```

```python
import functools
import math

import jax
import jax.numpy as jnp
from jax import lax
from jax.experimental import pallas as pl
from jax.experimental.pallas import tpu as pltpu
from jax.sharding import PartitionSpec as P

HARM = 49
NRAD = 128


def shell_layout(decay_rates):
    count = decay_rates.shape[0]
    spacing = 27.0 / (count - 1)
    centres = 1.0 + spacing * jnp.arange(count).astype(decay_rates.dtype)
    return (centres, spacing)


HP = 64
YR = 56


def y_factor(l, m):
    factor = math.sqrt(
        (2 * l + 1) / (4 * math.pi) * math.factorial(l - m) / math.factorial(l + m)
    )
    return factor if m == 0 else factor * math.sqrt(2.0)


def harmonic_rows(x, y, z, top, emit):
    square = x * x + y * y + z * z
    cos_m, sin_m = None, None
    for m in range(top + 1):
        if m == 1:
            cos_m, sin_m = x, y
        elif m > 1:
            cos_m, sin_m = cos_m * x - sin_m * y, cos_m * y + sin_m * x
        double = float(math.prod(range(1, 2 * m, 2)))
        ladder = {}
        for l in range(m, top + 1):
            if l == m + 1:
                ladder[l] = z * float(2 * m + 1)
            elif l == m + 2:
                ladder[l] = z * ladder[l - 1] * ((2 * l - 1) / 2) - square * ((l + m - 1) / 2)
            elif l > m + 2:
                ladder[l] = z * ladder[l - 1] * ((2 * l - 1) / (l - m)) - square * ladder[l - 2] * (
                    (l + m - 1) / (l - m)
                )
            scale = y_factor(l, m) * double
            part = ladder[l] * scale if l > m else scale
            if m == 0:
                emit(l * l, part if l > m else jnp.full_like(x, part))
            else:
                emit(l * l + 2 * m - 1, cos_m * part)
                emit(l * l + 2 * m, sin_m * part)


def split3(value):
    high = value.astype(jnp.bfloat16).astype(jnp.float32)
    rest = value - high
    middle = rest.astype(jnp.bfloat16).astype(jnp.float32)
    return high, middle, rest - middle


FEATURES = 9
FEATURE_ROWS = 6 * FEATURES + 3
FAR_ROWS = 64


def far_tables(atoms_ref, moments_ref, rows_ref, table_ref):
    atoms = atoms_ref.shape[1]
    ax = atoms_ref[0:1, :] - 8.0
    ay = atoms_ref[1:2, :] - 8.0
    az = atoms_ref[2:3, :] - 8.0
    mom = [moments_ref[i : i + 1, :] for i in range(9)]
    one, nil = jnp.ones_like(ax), jnp.zeros_like(ax)
    n10, n11 = y_factor(1, 0), y_factor(1, 1)
    vx, vy, vz = mom[2] * n11, mom[3] * n11, mom[1] * n10
    f20, f21, f22 = y_factor(2, 0), 3.0 * y_factor(2, 1), 3.0 * y_factor(2, 2)
    qzz = mom[4] * f20
    qxx = mom[7] * f22 - qzz * 0.5
    qyy = -mom[7] * f22 - qzz * 0.5
    qxz, qyz, qxy = mom[5] * f21, mom[6] * f21, mom[8] * (2.0 * f22)
    gx = -(2.0 * qxx * ax + qxy * ay + qxz * az)
    gy = -(qxy * ax + 2.0 * qyy * ay + qyz * az)
    gz = -(qxz * ax + qyz * ay + 2.0 * qzz * az)
    const = -0.5 * (gx * ax + gy * ay + gz * az)
    norm = ax * ax + ay * ay + az * az + 1.0
    plans = [
        ([-2.0 * ax, -2.0 * ay, -2.0 * az, one, one, one, nil, nil, nil], norm),
        ([vx, vy, vz, nil, nil, nil, nil, nil, nil], -(vx * ax + vy * ay + vz * az)),
        ([gx, gy, gz, qxx, qyy, qzz, qxy, qxz, qyz], const),
    ]
    for q, (coefs, fixed) in enumerate(plans):
        columns = pl.ds(q * atoms, atoms)
        for f, coef in enumerate(coefs):
            high, middle, low = split3(coef)
            for r, row in enumerate((high, middle, high, low, high, middle)):
                rows_ref[6 * f + r : 6 * f + r + 1, columns] = row
        for r, row in enumerate(split3(fixed)):
            rows_ref[6 * FEATURES + r : 6 * FEATURES + r + 1, columns] = row
        rows_ref[FEATURE_ROWS:FAR_ROWS, columns] = jnp.zeros(
            (FAR_ROWS - FEATURE_ROWS, atoms), jnp.float32
        )
    table_ref[...] = rows_ref[...].astype(jnp.bfloat16)


def point_features(px, py, pz, rows_ref):
    qx, qy, qz = px - 8.0, py - 8.0, pz - 8.0
    values = [qx, qy, qz, qx * qx, qy * qy, qz * qz, qx * qy, qx * qz, qy * qz]
    for f, value in enumerate(values):
        high, middle, low = split3(value)
        for r, row in enumerate((high, high, middle, high, low, middle)):
            rows_ref[6 * f + r : 6 * f + r + 1, :] = row
    rows_ref[6 * FEATURES : FEATURE_ROWS, :] = jnp.ones((3, qx.shape[1]), jnp.float32)
    rows_ref[FEATURE_ROWS:FAR_ROWS, :] = jnp.zeros(
        (FAR_ROWS - FEATURE_ROWS, qx.shape[1]), jnp.float32
    )
    return rows_ref[...].T.astype(jnp.bfloat16)


def evaluate_kernel(
    near_smem,
    near_ref,
    points_ref,
    slot_table_ref,
    slot_pot_ref,
    atoms_ref,
    moments_ref,
    centre_ref,
    rate_ref,
    out_ref,
    far_rows,
    far_table,
    feat_rows,
    far_acc,
    y_rows,
    rho_rows,
    corr_ref,
):
    b = pl.program_id(0)
    near_count = near_ref.shape[2]
    pts = points_ref.shape[1]
    atoms = atoms_ref.shape[1]

    @pl.when(b == 0)
    def _():
        far_tables(atoms_ref, moments_ref, far_rows, far_table)
        y_rows[...] = jnp.zeros_like(y_rows)

    px, py, pz = points_ref[0:1, :], points_ref[1:2, :], points_ref[2:3, :]

    features = point_features(px, py, pz, feat_rows)
    far_acc[...] = jnp.zeros_like(far_acc)
    chunk = 256

    @pl.loop(0, atoms // chunk)
    def _(c):
        base = pl.multiple_of(c * chunk, chunk)

        def table(q):
            return far_table[:, pl.ds(pl.multiple_of(q * atoms + base, chunk), chunk)]

        square = jnp.dot(features, table(0), preferred_element_type=jnp.float32)
        linear = jnp.dot(features, table(1), preferred_element_type=jnp.float32)
        quad = jnp.dot(features, table(2), preferred_element_type=jnp.float32)
        inv = lax.rsqrt(square)
        inv2 = inv * inv
        level = moments_ref[0:1, pl.ds(base, chunk)] * y_factor(0, 0)
        value = inv * (level + inv2 * (linear + inv2 * quad))
        far_acc[...] += value[:, 0:128] + value[:, 128:256]

    far_row = jnp.sum(far_acc[...].T, axis=0, keepdims=True)

    hot = (
        lax.broadcasted_iota(jnp.int32, (slot_table_ref.shape[0], near_count), 0) == near_ref[0]
    ).astype(jnp.float32)
    info = lax.dot_general(
        hot,
        slot_table_ref[...],
        (((0,), (0,)), ((), ())),
        precision=lax.Precision.HIGHEST,
        preferred_element_type=jnp.float32,
    )
    step = 8
    corr = jnp.zeros((step, pts), jnp.float32)
    for j in range(0, near_count, step):
        part = info[j : j + step, :]
        dx = px - part[:, 0:1]
        dy = py - part[:, 1:2]
        dz = pz - part[:, 2:3]
        square = dx * dx + dy * dy + dz * dz + 1.0
        inv = lax.rsqrt(square)
        rho_rows[j : j + step, :] = square * inv
        low = {}

        def emit(i, value):
            y_rows[pl.ds(j * YR + i, step, stride=YR), :] = value
            if i < 9:
                low[i] = value

        harmonic_rows(dx * inv, dy * inv, dz * inv, 6, emit)
        term = [part[:, 3 + i : 4 + i] * low[i] for i in range(9)]
        degree1 = term[1] + term[2] + term[3]
        degree2 = (term[4] + term[5]) + (term[6] + term[7]) + term[8]
        corr = corr + inv * (term[0] + inv * (degree1 + inv * degree2))
    corr_ref[...] = corr

    centre, rate = centre_ref[...], rate_ref[...]
    unroll = 4

    def pairs(g, total):
        for v in range(unroll):
            j = g * unroll + v
            coefs = slot_pot_ref[near_smem[b, j]]
            t = (rho_rows[pl.ds(j, 1), :] - centre) * rate
            radial = jnp.exp2(-(t * t)).astype(jnp.bfloat16)
            values = jnp.dot(coefs, radial, preferred_element_type=jnp.float32)
            rows = y_rows[pl.ds(pl.multiple_of(j * YR, YR), YR), :]
            total = total + values[0:YR] * rows
        return total

    total = lax.fori_loop(
        0, near_count // unroll, pairs, jnp.zeros((YR, pts), jnp.float32)
    )
    near_row = jnp.sum(total, axis=0, keepdims=True)
    out_ref[0] = near_row + far_row - jnp.sum(corr_ref[...], axis=0, keepdims=True)


def evaluate(points, near_slot, slot_table, slot_pot, atom_pos, moments, decay_rates):
    batches, near_count = near_slot.shape
    pts = points.shape[1] // batches
    atoms = atom_pos.shape[1]
    centres, spacing = shell_layout(decay_rates)
    rate = jnp.sqrt(decay_rates * math.log2(math.e)) / spacing
    centre_full = jnp.broadcast_to(centres[:, None], (NRAD, pts))
    rate_full = jnp.broadcast_to(rate[:, None], (NRAD, pts))

    def whole(shape):
        return pl.BlockSpec(shape, lambda b, near: (0,) * len(shape))

    out = pl.pallas_call(
        evaluate_kernel,
        out_shape=jax.ShapeDtypeStruct((batches, 1, pts), jnp.float32),
        grid_spec=pltpu.PrefetchScalarGridSpec(
            num_scalar_prefetch=1,
            grid=(batches,),
            in_specs=[
                pl.BlockSpec((1, 1, near_count), lambda b, near: (b, 0, 0)),
                pl.BlockSpec((3, pts), lambda b, near: (0, b)),
                whole(slot_table.shape),
                whole(slot_pot.shape),
                whole(atom_pos.shape),
                whole(moments.shape),
                whole((NRAD, pts)),
                whole((NRAD, pts)),
            ],
            out_specs=pl.BlockSpec((1, 1, pts), lambda b, near: (b, 0, 0)),
            scratch_shapes=[
                pltpu.VMEM((FAR_ROWS, 3 * atoms), jnp.float32),
                pltpu.VMEM((FAR_ROWS, 3 * atoms), jnp.bfloat16),
                pltpu.VMEM((FAR_ROWS, pts), jnp.float32),
                pltpu.VMEM((pts, 128), jnp.float32),
                pltpu.VMEM((near_count * YR, pts), jnp.float32),
                pltpu.VMEM((near_count, pts), jnp.float32),
                pltpu.VMEM((8, pts), jnp.float32),
            ],
        ),
        compiler_params=pltpu.CompilerParams(
            dimension_semantics=("arbitrary",), vmem_limit_bytes=40 << 20
        ),
        name="evaluate",
    )(
        near_slot,
        near_slot.reshape(batches, 1, near_count),
        points,
        slot_table,
        slot_pot,
        atom_pos,
        moments,
        centre_full,
        rate_full,
    )
    return out.reshape(-1)


def point_blocks_kernel(
    points_ref,
    density_ref,
    slots_ref,
    places_ref,
    centre_ref,
    rate_ref,
    table_ref,
    out_ref,
    four_ref,
    q_rows,
):
    listed = places_ref.shape[1]
    pts = centre_ref.shape[1]
    blocks = points_ref.shape[1] // pts
    slot_rows = lax.broadcasted_iota(jnp.int32, (listed, pts), 0)
    lane = lax.broadcasted_iota(jnp.int32, (listed, pts), 1)
    earlier = (slot_rows < lane).astype(jnp.bfloat16)
    counts = jnp.zeros((listed, 1), jnp.float32)
    ranks, hots = [], []
    for g in range(blocks):
        at = pl.ds(g * pts, pts)
        same = slot_rows == slots_ref[:, at]
        hot = same.astype(jnp.float32)
        inside = jnp.dot(hot.astype(jnp.bfloat16), earlier, preferred_element_type=jnp.float32)
        ranks.append(jnp.sum(hot * (inside + counts), axis=0, keepdims=True))
        counts = counts + jnp.sum(hot, axis=1, keepdims=True)
    below = (lax.broadcasted_iota(jnp.int32, (listed, listed), 1) < lax.broadcasted_iota(
        jnp.int32, (listed, listed), 0
    )).astype(jnp.float32)
    counts_full = jnp.broadcast_to(counts, (listed, listed))
    starts_full = jnp.dot(
        below, counts_full, precision=lax.Precision.HIGHEST, preferred_element_type=jnp.float32
    )
    starts = starts_full[:, 0:1]
    packed = starts_full * 4096.0 + counts_full
    rows64 = lax.broadcasted_iota(jnp.int32, (4 * blocks, pts), 0) // 4
    sorted_rows = jnp.zeros((4 * blocks, pts), jnp.float32)
    moments = jnp.zeros((16, listed), jnp.float32)
    q_rows[...] = jnp.zeros_like(q_rows)
    for g in range(blocks):
        at = pl.ds(g * pts, pts)
        hot = (slot_rows == slots_ref[:, at]).astype(jnp.float32)
        place = ranks[g] + jnp.sum(hot * starts, axis=0, keepdims=True)
        place = place.astype(jnp.int32)
        atom = jnp.dot(
            places_ref[...], hot, precision=lax.Precision.HIGHEST, preferred_element_type=jnp.float32
        )
        dx = points_ref[0:1, at] - atom[0:1]
        dy = points_ref[1:2, at] - atom[1:2]
        dz = points_ref[2:3, at] - atom[2:3]
        weight = density_ref[:, at]
        for r in range(2):
            for c, value in enumerate((dx, dy, dz, weight)):
                four_ref[4 * r + c : 4 * r + c + 1, :] = value
        tiled = jnp.concatenate([four_ref[...]] * (blocks // 2), axis=0)
        masked = jnp.where(rows64 == place // pts, tiled, 0.0)
        target = (slot_rows == place % pts).astype(jnp.bfloat16)
        for piece in split3(masked):
            sorted_rows = sorted_rows + lax.dot_general(
                piece.astype(jnp.bfloat16),
                target,
                (((1,), (1,)), ((), ())),
                preferred_element_type=jnp.float32,
            )
        square = dx * dx + dy * dy + dz * dz + 1.0
        inv = lax.rsqrt(square)
        rho = square * inv
        t = (rho - centre_ref[...]) * rate_ref[...]
        radial = jnp.exp2(-(t * t))
        levels = jnp.dot(
            table_ref[...], radial, precision=lax.Precision.HIGHEST, preferred_element_type=jnp.float32
        )

        def emit(i, value):
            degree = (0, 1, 1, 1, 2, 2, 2, 2, 2)[i]
            q_rows[i : i + 1, :] = value * weight * levels[degree : degree + 1]

        harmonic_rows(dx * inv, dy * inv, dz * inv, 2, emit)
        moments = moments + lax.dot_general(
            q_rows[...],
            hot,
            (((1,), (1,)), ((), ())),
            precision=lax.Precision.HIGHEST,
            preferred_element_type=jnp.float32,
        )
    out_ref[0 : 4 * blocks, :] = sorted_rows
    out_ref[4 * blocks : 4 * blocks + 1, :] = packed.T[0:1, :]
    out_ref[4 * blocks + 1 : 4 * blocks + 10, :] = moments[0:9]
    out_ref[4 * blocks + 10 : 4 * blocks + 12, :] = jnp.zeros((2, listed), jnp.float32)


def radial_tables(decay_rates, width):
    centres, spacing = shell_layout(decay_rates)
    rate = jnp.sqrt(decay_rates * math.log2(math.e)) / spacing
    shape = (decay_rates.shape[0], width)
    return jnp.broadcast_to(centres[:, None], shape), jnp.broadcast_to(rate[:, None], shape)


def point_blocks(points, density, slots, places, tables, moment_table):
    count = points.shape[1]
    pts = tables[0].shape[1]
    rows = 4 * (count // pts) + 12
    out = pl.pallas_call(
        point_blocks_kernel,
        out_shape=jax.ShapeDtypeStruct((rows, pts), jnp.float32),
        scratch_shapes=[pltpu.VMEM((8, pts), jnp.float32), pltpu.VMEM((16, pts), jnp.float32)],
        compiler_params=pltpu.CompilerParams(vmem_limit_bytes=40 << 20),
        name="point_blocks",
    )(
        points,
        density.reshape(1, count),
        slots.reshape(1, count),
        jnp.pad(places, ((0, 5), (0, 0))),
        *tables,
        jnp.pad(moment_table, ((0, 5), (0, 0))),
    )
    return out.reshape(rows // 4, 4, pts)


MESH = pl.DeviceIdType.MESH
SIDE = 4


def gather_kernel(cuts, mine_ref, all_ref, local_sem, send_sems, recv_sems, swap_send, swap_recv):
    row, column = lax.axis_index("sx"), lax.axis_index("sy")
    core = lax.rem(row, 2)
    here = {"z": row // 2, "y": column // SIDE, "x": lax.rem(column, SIDE)}

    def device(place, on_core):
        return (place["z"] * 2 + on_core, place["y"] * SIDE + place["x"])

    def moved(axis, offset):
        place = dict(here)
        place[axis] = lax.rem(here[axis] + offset, SIDE)
        return place

    def region(place, whole, part):
        index = [pl.ds(0, SIDE) if a in whole else place[a] for a in ("z", "y", "x")]
        return all_ref.at[index[0], core, index[1], index[2], part]

    barrier = pltpu.get_barrier_semaphore()
    for axis in ("z", "y", "x"):
        for offset in range(1, SIDE):
            pl.semaphore_signal(
                barrier, inc=1, device_id=device(moved(axis, offset), core), device_id_type=MESH
            )
    pl.semaphore_signal(barrier, inc=1, device_id=device(here, 1 - core), device_id_type=MESH)
    pl.semaphore_wait(barrier, 3 * (SIDE - 1) + 1)

    local = pltpu.make_async_copy(mine_ref, region(here, "", pl.ds(0, cuts[-1])), local_sem)
    local.start()
    orders = ("xyz", "yzx", "zxy")
    parts = [pl.ds(cuts[c], cuts[c + 1] - cuts[c]) for c in range(3)]
    hops = {}
    swaps = []

    def send(c, phase):
        axis = orders[c][phase]
        whole = orders[c][:phase]
        for offset in range(1, SIDE):
            place = region(here, whole, parts[c])
            copy = pltpu.make_async_remote_copy(
                src_ref=mine_ref.at[parts[c]] if phase == 0 else place,
                dst_ref=place,
                send_sem=send_sems.at[c, phase, offset],
                recv_sem=recv_sems.at[c, phase, offset],
                device_id=device(moved(axis, offset), core),
                device_id_type=MESH,
            )
            copy.start()
            hops[c, phase, offset] = copy

    def swap(c, slot, place):
        area = region(place, orders[c][:2], parts[c])
        copy = pltpu.make_async_remote_copy(
            src_ref=area,
            dst_ref=area,
            send_sem=swap_send.at[c, slot],
            recv_sem=swap_recv.at[c, slot],
            device_id=device(here, 1 - core),
            device_id_type=MESH,
        )
        copy.start()
        swaps.append(copy)

    for c in range(3):
        send(c, 0)
    local.wait()
    for phase in (1, 2):
        for c in range(3):
            for offset in range(1, SIDE):
                hops[c, phase - 1, offset].wait_recv()
            send(c, phase)
    for c in range(3):
        swap(c, 0, here)
    for offset in range(1, SIDE):
        for c in range(3):
            hops[c, 2, offset].wait_recv()
            swap(c, offset, moved(orders[c][2], SIDE - offset))
    for copy in hops.values():
        copy.wait_send()
    for copy in swaps:
        copy.wait()


def gather_blocks(mine):
    blocks = mine.shape[0]
    cuts = (0, blocks // 3, 2 * blocks // 3, blocks)
    return pl.pallas_call(
        functools.partial(gather_kernel, cuts),
        out_shape=jax.ShapeDtypeStruct((SIDE, 2, SIDE, SIDE) + mine.shape, mine.dtype),
        in_specs=[pl.BlockSpec(memory_space=pl.ANY)],
        out_specs=pl.BlockSpec(memory_space=pl.ANY),
        scratch_shapes=[
            pltpu.SemaphoreType.DMA,
            pltpu.SemaphoreType.DMA((3, 3, SIDE)),
            pltpu.SemaphoreType.DMA((3, 3, SIDE)),
            pltpu.SemaphoreType.DMA((3, SIDE)),
            pltpu.SemaphoreType.DMA((3, SIDE)),
        ],
        compiler_params=pltpu.CompilerParams(collective_id=0, has_side_effects=True),
        name="gather_blocks",
    )(mine)


CHUNK = 32
PER = 4
FLUSH = 8


def project_kernel(
    counts_ref,
    codes_ref,
    runs_ref,
    blocks_ref,
    centre_ref,
    rate_ref,
    green_ref,
    pot_ref,
    buffer,
    owner_ref,
    used_ref,
    y_rows,
    rho_rows,
    coefs_ref,
):
    listed = counts_ref.shape[0]
    pts = centre_ref.shape[1]
    coefs_ref[...] = jnp.zeros_like(coefs_ref)
    y_rows[...] = jnp.zeros_like(y_rows)
    lane = lax.broadcasted_iota(jnp.int32, (4, pts), 1)
    used_ref[0] = 0
    for f in range(FLUSH):
        owner_ref[f] = 0

    def flush():
        def component(c):
            return buffer[pl.ds(c, FLUSH, stride=4), :]

        dx, dy, dz, weight = (component(c) for c in range(4))
        square = dx * dx + dy * dy + dz * dz + 1.0
        inv = lax.rsqrt(square)
        rho_rows[...] = square * inv

        def emit(i, value):
            y_rows[pl.ds(i, FLUSH, stride=HP), :] = value * weight

        harmonic_rows(dx * inv, dy * inv, dz * inv, 6, emit)
        sums = []
        for f in range(FLUSH):
            t = (rho_rows[f : f + 1, :] - centre_ref[...]) * rate_ref[...]
            radial = jnp.exp2(-(t * t)).astype(jnp.bfloat16)
            rows = y_rows[f * HP : (f + 1) * HP, :].astype(jnp.bfloat16)
            sums.append(
                lax.dot_general(
                    rows, radial, (((1,), (1,)), ((), ())), preferred_element_type=jnp.float32
                )
            )
        for f in range(FLUSH):
            at = pl.ds(owner_ref[f], YR, stride=listed)
            coefs_ref[at, :] = coefs_ref[at, :] + sums[f][0:YR]
        buffer[...] = jnp.zeros_like(buffer)
        used_ref[0] = 0

    buffer[...] = jnp.zeros_like(buffer)

    def window(device, start):
        at = lax.shift_right_logical(start, 7)
        off = lax.bitwise_and(start, 127)
        first = blocks_ref[device, at]
        second = blocks_ref[device, at + 1]
        return jnp.where(lane >= off, first, second), off

    def piece(device, start, length, position):
        value, off = window(device, start)
        left = position * CHUNK
        moved = pltpu.roll(value, lax.bitwise_and(left - off + 128, 127), 1)
        keep = (lane >= left) & (lane < left + length)
        return jnp.where(keep, moved, 0.0)

    def put(j, value):
        row = used_ref[0]
        buffer[pl.ds(row * 4, 4), :] = value
        owner_ref[row] = j
        used_ref[0] = row + 1

        @pl.when(row + 1 == FLUSH)
        def _():
            flush()

    @pl.loop(0, listed)
    def _(j):
        count = counts_ref[j]

        @pl.loop(0, lax.shift_right_logical(count + (PER - 1), 2))
        def _(g):
            total = jnp.zeros((4, pts), jnp.float32)
            longest = jnp.int32(0)
            entries = []
            for v in range(PER):
                r = g * PER + v
                code = codes_ref[r, j]
                device = lax.shift_right_logical(code, 7)
                run = runs_ref[device, lax.bitwise_and(code, 127)]
                length = jnp.where(r < count, lax.bitwise_and(run, 4095), 0)
                start = lax.shift_right_logical(run, 12)
                entries.append((device, start, length))
                longest = jnp.maximum(longest, length)
                total = total + piece(device, start, jnp.minimum(length, CHUNK), v)
            put(j, total)

            @pl.when(longest > CHUNK)
            def _():
                for device, start, length in entries:

                    @pl.loop(1, (length + (CHUNK - 1)) // CHUNK)
                    def _(c):
                        put(
                            j,
                            piece(
                                device,
                                start + c * CHUNK,
                                jnp.minimum(length - c * CHUNK, CHUNK),
                                0,
                            ),
                        )

    flush()
    for l in range(7):
        top = green_ref[l]
        high = top.astype(jnp.bfloat16)
        low = (top - high.astype(jnp.float32)).astype(jnp.bfloat16)
        half = jnp.concatenate([high, low], axis=1)
        table = jnp.concatenate([half, half], axis=0)
        for i in range(l * l, (l + 1) * (l + 1)):
            rows = coefs_ref[i * listed : (i + 1) * listed, :]
            big = rows.astype(jnp.bfloat16)
            small = (rows - big.astype(jnp.float32)).astype(jnp.bfloat16)
            both = jnp.dot(
                jnp.concatenate([big, small], axis=1), table, preferred_element_type=jnp.float32
            )
            coefs_ref[i * listed : (i + 1) * listed, :] = both[:, 0:128] + both[:, 128:256]

    @pl.loop(0, listed)
    def _(j):
        rows = coefs_ref[pl.ds(j, YR, stride=listed), :]
        pot_ref[j] = jnp.concatenate(
            [rows, jnp.zeros((HP - YR, rows.shape[1]), jnp.float32)], axis=0
        ).astype(jnp.bfloat16)


def project(counts, codes, runs, blocks, tables, green):
    listed = counts.shape[0]
    pts = tables[0].shape[1]
    smem = pl.BlockSpec(memory_space=pltpu.SMEM)
    vmem = pl.BlockSpec(memory_space=pltpu.VMEM)
    return pl.pallas_call(
        project_kernel,
        out_shape=jax.ShapeDtypeStruct((listed, HP, NRAD), jnp.bfloat16),
        in_specs=[smem, smem, smem, vmem, vmem, vmem, vmem],
        out_specs=vmem,
        scratch_shapes=[
            pltpu.VMEM((FLUSH * 4, pts), jnp.float32),
            pltpu.SMEM((FLUSH,), jnp.int32),
            pltpu.SMEM((1,), jnp.int32),
            pltpu.VMEM((FLUSH * HP, pts), jnp.float32),
            pltpu.VMEM((FLUSH, pts), jnp.float32),
            pltpu.VMEM((YR * listed, NRAD), jnp.float32),
        ],
        compiler_params=pltpu.CompilerParams(vmem_limit_bytes=40 << 20),
        name="project",
    )(counts, codes, runs, blocks, *tables, green)


def scatter_kernel(blocks_ref, lists_ref, rows_at, out_ref, acc_ref):
    devices, _, _, listed = blocks_ref.shape
    wide = 256
    acc_ref[...] = jnp.zeros_like(acc_ref)
    column = lax.broadcasted_iota(jnp.int32, (wide, listed), 0)
    groups = acc_ref.shape[0] // 16

    @pl.loop(0, devices // 4)
    def _(g):
        total = acc_ref[...]
        for v in range(4):
            q = g * 4 + v
            ids = lists_ref[pl.ds(q, 1), :]
            target = (column == lax.bitwise_and(ids, wide - 1)).astype(jnp.bfloat16)
            group = lax.shift_right_logical(ids, 8)
            tiles = [blocks_ref[q, rows_at + m] for m in range(3)]
            mom = jnp.concatenate(tiles + [jnp.zeros((4, listed), jnp.float32)], axis=0)
            masked = jnp.concatenate(
                [jnp.where(group == h, mom, 0.0) for h in range(groups)], axis=0
            )
            high = masked.astype(jnp.bfloat16)
            low = (masked - high.astype(jnp.float32)).astype(jnp.bfloat16)
            for part in (high, low):
                total = total + lax.dot_general(
                    part, target, (((1,), (1,)), ((), ())), preferred_element_type=jnp.float32
                )
        acc_ref[...] = total

    for h in range(groups):
        out_ref[:, h * wide : (h + 1) * wide] = acc_ref[h * 16 + 1 : h * 16 + 10, :]


def scatter_moments(blocks, lists, atoms):
    return pl.pallas_call(
        lambda b, l, o, a: scatter_kernel(b, l, blocks.shape[1] - 3, o, a),
        out_shape=jax.ShapeDtypeStruct((9, atoms), jnp.float32),
        scratch_shapes=[pltpu.VMEM((atoms // 256 * 16, 256), jnp.float32)],
        compiler_params=pltpu.CompilerParams(vmem_limit_bytes=40 << 20),
        name="scatter_moments",
    )(blocks, lists)


def entry_tables(lists, my_list):
    devices, listed = lists.shape
    same = lists[:, :, None] == my_list[None, None, :]
    slot = jnp.arange(1, listed + 1, dtype=jnp.int32)[None, :, None]
    held = jnp.sum(jnp.where(same, slot, 0), axis=1)
    present = held > 0
    order = jnp.arange(devices)
    rank = jnp.dot(
        (order[None, :] < order[:, None]).astype(jnp.bfloat16),
        present.astype(jnp.bfloat16),
        preferred_element_type=jnp.float32,
    ).astype(jnp.int32)
    rank = jnp.where(present, rank, devices)
    code = order[:, None].astype(jnp.int32) * listed + held - 1
    picked = rank[None, :, :] == order[:, None, None]
    codes = jnp.sum(jnp.where(picked, code[None], 0), axis=1)
    return jnp.sum(present.astype(jnp.int32), axis=0), codes


def per_device(
    grid_points,
    weighted_density,
    point_slot,
    near_slot,
    slot_atom,
    atom_pos,
    decay_rates,
    green,
    moment_table,
):
    count_y = lax.axis_size("sy")
    devices = lax.axis_size("sx") * count_y
    myself = lax.axis_index("sx") * count_y + lax.axis_index("sy")
    lists = slot_atom.reshape(devices, -1)
    my_list = lists[myself]
    atoms = atom_pos.shape[1]
    pts = grid_points.shape[1] // near_slot.shape[0]
    tables = radial_tables(decay_rates, pts)
    places = atom_pos[:, my_list]
    mine = point_blocks(grid_points, weighted_density, point_slot, places, tables, moment_table)
    gathered = gather_blocks(mine)
    blocks = gathered.reshape((devices,) + mine.shape)
    counts, codes = entry_tables(lists, my_list)
    runs = blocks[:, mine.shape[0] - 3, 0, :].astype(jnp.int32)
    slot_pot = project(counts, codes, runs, blocks, tables, green)
    moments = scatter_moments(blocks, lists, atoms)
    slot_table = jnp.concatenate([places, moments[:, my_list]], axis=0).T
    slot_table = jnp.pad(slot_table, ((0, 0), (0, 128 - slot_table.shape[1])))
    return evaluate(
        grid_points, near_slot, slot_table, slot_pot, atom_pos, moments, decay_rates
    )


def solution(mesh):
    return jax.shard_map(
        per_device,
        mesh=mesh,
        in_specs=(
            P(None, ("sx", "sy")),
            P(("sx", "sy")),
            P(("sx", "sy")),
            P(("sx", "sy"), None),
            P(),
            P(),
            P(),
            P(),
            P(),
        ),
        out_specs=P(("sx", "sy")),
        check_vma=False,
    )
```

```python
import functools
import math

import jax
import jax.numpy as jnp
from jax import lax
from jax.experimental import pallas as pl
from jax.experimental.pallas import tpu as pltpu
from jax.sharding import PartitionSpec as P

HARM = 49
NRAD = 128


def shell_layout(decay_rates):
    count = decay_rates.shape[0]
    spacing = 27.0 / (count - 1)
    centres = 1.0 + spacing * jnp.arange(count).astype(decay_rates.dtype)
    return (centres, spacing)


HP = 64
YR = 56


def y_factor(l, m):
    factor = math.sqrt(
        (2 * l + 1) / (4 * math.pi) * math.factorial(l - m) / math.factorial(l + m)
    )
    return factor if m == 0 else factor * math.sqrt(2.0)


def harmonic_rows(x, y, z, top, emit):
    square = x * x + y * y + z * z
    cos_m, sin_m = None, None
    for m in range(top + 1):
        if m == 1:
            cos_m, sin_m = x, y
        elif m > 1:
            cos_m, sin_m = cos_m * x - sin_m * y, cos_m * y + sin_m * x
        double = float(math.prod(range(1, 2 * m, 2)))
        ladder = {}
        for l in range(m, top + 1):
            if l == m + 1:
                ladder[l] = z * float(2 * m + 1)
            elif l == m + 2:
                ladder[l] = z * ladder[l - 1] * ((2 * l - 1) / 2) - square * ((l + m - 1) / 2)
            elif l > m + 2:
                ladder[l] = z * ladder[l - 1] * ((2 * l - 1) / (l - m)) - square * ladder[l - 2] * (
                    (l + m - 1) / (l - m)
                )
            scale = y_factor(l, m) * double
            part = ladder[l] * scale if l > m else scale
            if m == 0:
                emit(l * l, part if l > m else jnp.full_like(x, part))
            else:
                emit(l * l + 2 * m - 1, cos_m * part)
                emit(l * l + 2 * m, sin_m * part)


def split3(value):
    high = value.astype(jnp.bfloat16).astype(jnp.float32)
    rest = value - high
    middle = rest.astype(jnp.bfloat16).astype(jnp.float32)
    return high, middle, rest - middle


SPACING = 27.0 / (NRAD - 1)
SHELL_ROWS = 16


def radial_values(rho, first_ref, rate_ref, dtype=jnp.bfloat16):
    rows, pts = first_ref.shape[0], rho.shape[1]
    base = jnp.broadcast_to(rho, (rows, pts)) - first_ref[...]
    pieces = []
    for k in range(0, NRAD, rows):
        e = base - (SPACING * k)
        power = (e * e) * rate_ref[k : k + rows, :]
        pieces.append(jnp.exp2(power.astype(dtype)))
    return jnp.concatenate(pieces, axis=0)


def radial_tables(decay_rates, width):
    centres, spacing = shell_layout(decay_rates)
    factor = decay_rates * (-math.log2(math.e) / spacing**2)
    return (
        jnp.broadcast_to(centres[:SHELL_ROWS, None], (SHELL_ROWS, width)),
        jnp.broadcast_to(factor[:, None], (decay_rates.shape[0], width)),
    )


FARC = 8
FEATURES = 9
FEATURE_ROWS = 6 * FEATURES + 3
FAR_ROWS = 64


def far_tables(atoms_ref, moments_ref, rows_ref, table_ref):
    atoms = atoms_ref.shape[1]
    ax = atoms_ref[0:1, :] - 8.0
    ay = atoms_ref[1:2, :] - 8.0
    az = atoms_ref[2:3, :] - 8.0
    mom = [moments_ref[i : i + 1, :] for i in range(9)]
    one, nil = jnp.ones_like(ax), jnp.zeros_like(ax)
    n10, n11 = y_factor(1, 0), y_factor(1, 1)
    vx, vy, vz = mom[2] * n11, mom[3] * n11, mom[1] * n10
    f20, f21, f22 = y_factor(2, 0), 3.0 * y_factor(2, 1), 3.0 * y_factor(2, 2)
    qzz = mom[4] * f20
    qxx = mom[7] * f22 - qzz * 0.5
    qyy = -mom[7] * f22 - qzz * 0.5
    qxz, qyz, qxy = mom[5] * f21, mom[6] * f21, mom[8] * (2.0 * f22)
    gx = -(2.0 * qxx * ax + qxy * ay + qxz * az)
    gy = -(qxy * ax + 2.0 * qyy * ay + qyz * az)
    gz = -(qxz * ax + qyz * ay + 2.0 * qzz * az)
    const = -0.5 * (gx * ax + gy * ay + gz * az)
    norm = ax * ax + ay * ay + az * az + 1.0
    plans = [
        ([-2.0 * ax, -2.0 * ay, -2.0 * az, one, one, one, nil, nil, nil], norm),
        ([vx, vy, vz, nil, nil, nil, nil, nil, nil], -(vx * ax + vy * ay + vz * az)),
        ([gx, gy, gz, qxx, qyy, qzz, qxy, qxz, qyz], const),
    ]
    for q, (coefs, fixed) in enumerate(plans):
        columns = pl.ds(q * atoms, atoms)
        for f, coef in enumerate(coefs):
            high, middle, low = split3(coef)
            for r, row in enumerate((high, middle, high, low, high, middle)):
                rows_ref[6 * f + r : 6 * f + r + 1, columns] = row
        for r, row in enumerate(split3(fixed)):
            rows_ref[6 * FEATURES + r : 6 * FEATURES + r + 1, columns] = row
        rows_ref[FEATURE_ROWS:FAR_ROWS, columns] = jnp.zeros(
            (FAR_ROWS - FEATURE_ROWS, atoms), jnp.float32
        )
    table_ref[...] = rows_ref[...].astype(jnp.bfloat16)


def point_features(px, py, pz, rows_ref):
    qx, qy, qz = px - 8.0, py - 8.0, pz - 8.0
    values = [qx, qy, qz, qx * qx, qy * qy, qz * qz, qx * qy, qx * qz, qy * qz]
    for f, value in enumerate(values):
        high, middle, low = split3(value)
        for r, row in enumerate((high, high, middle, high, low, middle)):
            rows_ref[6 * f + r : 6 * f + r + 1, :] = row
    rows_ref[6 * FEATURES : FEATURE_ROWS, :] = jnp.ones((3, qx.shape[1]), jnp.float32)
    rows_ref[FEATURE_ROWS:FAR_ROWS, :] = jnp.zeros(
        (FAR_ROWS - FEATURE_ROWS, qx.shape[1]), jnp.float32
    )
    return rows_ref[...].T.astype(jnp.bfloat16)


def evaluate_kernel(
    near_smem,
    near_ref,
    points_ref,
    slot_table_ref,
    slot_pot_ref,
    atoms_ref,
    moments_ref,
    first_ref,
    rate_ref,
    out_ref,
    far_rows,
    far_table,
    feat_rows,
    far_acc,
    y_rows,
    rho_rows,
    corr_ref,
):
    b = pl.program_id(0)
    near_count = near_ref.shape[2]
    pts = points_ref.shape[1]
    atoms = atoms_ref.shape[1]

    @pl.when(b == 0)
    def _():
        far_tables(atoms_ref, moments_ref, far_rows, far_table)
        y_rows[...] = jnp.zeros_like(y_rows)

    px, py, pz = points_ref[0:1, :], points_ref[1:2, :], points_ref[2:3, :]

    features = point_features(px, py, pz, feat_rows)
    far_acc[...] = jnp.zeros_like(far_acc)
    chunk = 256

    for c in range(FARC):
        base = c * chunk

        def table(q):
            return far_table[:, q * atoms + base : q * atoms + base + chunk]

        square = jnp.dot(features, table(0), preferred_element_type=jnp.float32)
        linear = jnp.dot(features, table(1), preferred_element_type=jnp.float32)
        quad = jnp.dot(features, table(2), preferred_element_type=jnp.float32)
        inv = lax.rsqrt(square)
        inv2 = inv * inv
        level = moments_ref[0:1, pl.ds(base, chunk)] * y_factor(0, 0)
        value = inv * (level + inv2 * (linear + inv2 * quad))
        far_acc[...] += value[:, 0:128] + value[:, 128:256]

    far_row = jnp.sum(far_acc[...].T, axis=0, keepdims=True)

    hot = (
        lax.broadcasted_iota(jnp.int32, (slot_table_ref.shape[0], near_count), 0) == near_ref[0]
    ).astype(jnp.float32)
    info = lax.dot_general(
        hot,
        slot_table_ref[...],
        (((0,), (0,)), ((), ())),
        precision=lax.Precision.HIGHEST,
        preferred_element_type=jnp.float32,
    )
    step = 8
    corr = jnp.zeros((step, pts), jnp.float32)
    for j in range(0, near_count, step):
        part = info[j : j + step, :]
        dx = px - part[:, 0:1]
        dy = py - part[:, 1:2]
        dz = pz - part[:, 2:3]
        square = dx * dx + dy * dy + dz * dz + 1.0
        inv = lax.rsqrt(square)
        rho_rows[j : j + step, :] = square * inv
        low = {}

        def emit(i, value):
            y_rows[pl.ds(j * YR + i, step, stride=YR), :] = value
            if i < 9:
                low[i] = value

        harmonic_rows(dx * inv, dy * inv, dz * inv, 6, emit)
        term = [part[:, 3 + i : 4 + i] * low[i] for i in range(9)]
        degree1 = term[1] + term[2] + term[3]
        degree2 = (term[4] + term[5]) + (term[6] + term[7]) + term[8]
        corr = corr + inv * (term[0] + inv * (degree1 + inv * degree2))
    corr_ref[...] = corr

    unroll = 32

    def pairs(g, total):
        for v in range(unroll):
            j = g * unroll + v
            coefs = slot_pot_ref[near_smem[b, j]]
            radial = radial_values(rho_rows[pl.ds(j, 1), :], first_ref, rate_ref)
            values = jnp.dot(coefs, radial, preferred_element_type=jnp.float32)
            rows = y_rows[pl.ds(pl.multiple_of(j * YR, YR), YR), :]
            total = total + values[0:YR] * rows
        return total

    total = lax.fori_loop(
        0, near_count // unroll, pairs, jnp.zeros((YR, pts), jnp.float32)
    )
    near_row = jnp.sum(total, axis=0, keepdims=True)
    out_ref[0] = near_row + far_row - jnp.sum(corr_ref[...], axis=0, keepdims=True)


def evaluate(points, near_slot, slot_table, slot_pot, atom_pos, moments, decay_rates):
    batches, near_count = near_slot.shape
    pts = points.shape[1] // batches
    atoms = atom_pos.shape[1]
    first, factor = radial_tables(decay_rates, pts)

    def whole(shape):
        return pl.BlockSpec(shape, lambda b, near: (0,) * len(shape))

    out = pl.pallas_call(
        evaluate_kernel,
        out_shape=jax.ShapeDtypeStruct((batches, 1, pts), jnp.float32),
        grid_spec=pltpu.PrefetchScalarGridSpec(
            num_scalar_prefetch=1,
            grid=(batches,),
            in_specs=[
                pl.BlockSpec((1, 1, near_count), lambda b, near: (b, 0, 0)),
                pl.BlockSpec((3, pts), lambda b, near: (0, b)),
                whole(slot_table.shape),
                whole(slot_pot.shape),
                whole(atom_pos.shape),
                whole(moments.shape),
                whole(first.shape),
                whole(factor.shape),
            ],
            out_specs=pl.BlockSpec((1, 1, pts), lambda b, near: (b, 0, 0)),
            scratch_shapes=[
                pltpu.VMEM((FAR_ROWS, 3 * atoms), jnp.float32),
                pltpu.VMEM((FAR_ROWS, 3 * atoms), jnp.bfloat16),
                pltpu.VMEM((FAR_ROWS, pts), jnp.float32),
                pltpu.VMEM((pts, 128), jnp.float32),
                pltpu.VMEM((near_count * YR, pts), jnp.float32),
                pltpu.VMEM((near_count, pts), jnp.float32),
                pltpu.VMEM((8, pts), jnp.float32),
            ],
        ),
        compiler_params=pltpu.CompilerParams(
            dimension_semantics=("arbitrary",), vmem_limit_bytes=40 << 20
        ),
        name="evaluate",
    )(
        near_slot,
        near_slot.reshape(batches, 1, near_count),
        points,
        slot_table,
        slot_pot,
        atom_pos,
        moments,
        first,
        factor,
    )
    return out.reshape(-1)


def point_blocks_kernel(
    points_ref,
    density_ref,
    slots_ref,
    places_ref,
    first_ref,
    rate_ref,
    table_ref,
    out_ref,
    four_ref,
    q_rows,
):
    listed = places_ref.shape[1]
    pts = first_ref.shape[1]
    blocks = points_ref.shape[1] // pts
    slot_rows = lax.broadcasted_iota(jnp.int32, (listed, pts), 0)
    lane = lax.broadcasted_iota(jnp.int32, (listed, pts), 1)
    earlier = (slot_rows < lane).astype(jnp.bfloat16)
    counts = jnp.zeros((listed, 1), jnp.float32)
    ranks, hots = [], []
    for g in range(blocks):
        at = pl.ds(g * pts, pts)
        same = slot_rows == slots_ref[:, at]
        hot = same.astype(jnp.float32)
        inside = jnp.dot(hot.astype(jnp.bfloat16), earlier, preferred_element_type=jnp.float32)
        ranks.append(jnp.sum(hot * (inside + counts), axis=0, keepdims=True))
        counts = counts + jnp.sum(hot, axis=1, keepdims=True)
    below = (lax.broadcasted_iota(jnp.int32, (listed, listed), 1) < lax.broadcasted_iota(
        jnp.int32, (listed, listed), 0
    )).astype(jnp.float32)
    counts_full = jnp.broadcast_to(counts, (listed, listed))
    starts_full = jnp.dot(
        below, counts_full, precision=lax.Precision.HIGHEST, preferred_element_type=jnp.float32
    )
    starts = starts_full[:, 0:1]
    packed = starts_full * 4096.0 + counts_full
    rows64 = lax.broadcasted_iota(jnp.int32, (4 * blocks, pts), 0) // 4
    sorted_rows = jnp.zeros((4 * blocks, pts), jnp.float32)
    moments = jnp.zeros((16, listed), jnp.float32)
    q_rows[...] = jnp.zeros_like(q_rows)
    for g in range(blocks):
        at = pl.ds(g * pts, pts)
        hot = (slot_rows == slots_ref[:, at]).astype(jnp.float32)
        place = ranks[g] + jnp.sum(hot * starts, axis=0, keepdims=True)
        place = place.astype(jnp.int32)
        atom = jnp.dot(
            places_ref[...], hot, precision=lax.Precision.HIGHEST, preferred_element_type=jnp.float32
        )
        dx = points_ref[0:1, at] - atom[0:1]
        dy = points_ref[1:2, at] - atom[1:2]
        dz = points_ref[2:3, at] - atom[2:3]
        weight = density_ref[:, at]
        for r in range(2):
            for c, value in enumerate((dx, dy, dz, weight)):
                four_ref[4 * r + c : 4 * r + c + 1, :] = value
        tiled = jnp.concatenate([four_ref[...]] * (blocks // 2), axis=0)
        masked = jnp.where(rows64 == place // pts, tiled, 0.0)
        target = (slot_rows == place % pts).astype(jnp.bfloat16)
        for piece in split3(masked):
            sorted_rows = sorted_rows + lax.dot_general(
                piece.astype(jnp.bfloat16),
                target,
                (((1,), (1,)), ((), ())),
                preferred_element_type=jnp.float32,
            )
        square = dx * dx + dy * dy + dz * dz + 1.0
        inv = lax.rsqrt(square)
        rho = square * inv
        radial = radial_values(rho, first_ref, rate_ref, jnp.float32)
        levels = jnp.dot(
            table_ref[...], radial, precision=lax.Precision.HIGHEST, preferred_element_type=jnp.float32
        )

        def emit(i, value):
            degree = (0, 1, 1, 1, 2, 2, 2, 2, 2)[i]
            q_rows[i : i + 1, :] = value * weight * levels[degree : degree + 1]

        harmonic_rows(dx * inv, dy * inv, dz * inv, 2, emit)
        moments = moments + lax.dot_general(
            q_rows[...],
            hot,
            (((1,), (1,)), ((), ())),
            precision=lax.Precision.HIGHEST,
            preferred_element_type=jnp.float32,
        )
    out_ref[0 : 4 * blocks, :] = sorted_rows
    out_ref[4 * blocks : 4 * blocks + 1, :] = packed.T[0:1, :]
    out_ref[4 * blocks + 1 : 4 * blocks + 10, :] = moments[0:9]
    out_ref[4 * blocks + 10 : 4 * blocks + 12, :] = jnp.zeros((2, listed), jnp.float32)


def point_blocks(points, density, slots, places, tables, moment_table):
    count = points.shape[1]
    pts = tables[0].shape[1]
    rows = 4 * (count // pts) + 12
    out = pl.pallas_call(
        point_blocks_kernel,
        out_shape=jax.ShapeDtypeStruct((rows, pts), jnp.float32),
        scratch_shapes=[pltpu.VMEM((8, pts), jnp.float32), pltpu.VMEM((16, pts), jnp.float32)],
        compiler_params=pltpu.CompilerParams(vmem_limit_bytes=40 << 20),
        name="point_blocks",
    )(
        points,
        density.reshape(1, count),
        slots.reshape(1, count),
        jnp.pad(places, ((0, 5), (0, 0))),
        *tables,
        jnp.pad(moment_table, ((0, 5), (0, 0))),
    )
    return out.reshape(rows // 4, 4, pts)


MESH = pl.DeviceIdType.MESH
SIDE = 4


def gather_kernel(cuts, mine_ref, all_ref, local_sem, send_sems, recv_sems, swap_send, swap_recv):
    row, column = lax.axis_index("sx"), lax.axis_index("sy")
    core = lax.rem(row, 2)
    here = {"z": row // 2, "y": column // SIDE, "x": lax.rem(column, SIDE)}

    def device(place, on_core):
        return (place["z"] * 2 + on_core, place["y"] * SIDE + place["x"])

    def moved(axis, offset):
        place = dict(here)
        place[axis] = lax.rem(here[axis] + offset, SIDE)
        return place

    def region(place, whole, part):
        index = [pl.ds(0, SIDE) if a in whole else place[a] for a in ("z", "y", "x")]
        return all_ref.at[index[0], core, index[1], index[2], part]

    barrier = pltpu.get_barrier_semaphore()
    for axis in ("z", "y", "x"):
        for offset in range(1, SIDE):
            pl.semaphore_signal(
                barrier, inc=1, device_id=device(moved(axis, offset), core), device_id_type=MESH
            )
    pl.semaphore_signal(barrier, inc=1, device_id=device(here, 1 - core), device_id_type=MESH)
    pl.semaphore_wait(barrier, 3 * (SIDE - 1) + 1)

    local = pltpu.make_async_copy(mine_ref, region(here, "", pl.ds(0, cuts[-1])), local_sem)
    local.start()
    orders = ("xyz", "yzx", "zxy")
    parts = [pl.ds(cuts[c], cuts[c + 1] - cuts[c]) for c in range(3)]
    hops = {}
    swaps = []

    def send(c, phase):
        axis = orders[c][phase]
        whole = orders[c][:phase]
        for offset in range(1, SIDE):
            place = region(here, whole, parts[c])
            copy = pltpu.make_async_remote_copy(
                src_ref=mine_ref.at[parts[c]] if phase == 0 else place,
                dst_ref=place,
                send_sem=send_sems.at[c, phase, offset],
                recv_sem=recv_sems.at[c, phase, offset],
                device_id=device(moved(axis, offset), core),
                device_id_type=MESH,
            )
            copy.start()
            hops[c, phase, offset] = copy

    def swap(c, slot, place):
        area = region(place, orders[c][:2], parts[c])
        copy = pltpu.make_async_remote_copy(
            src_ref=area,
            dst_ref=area,
            send_sem=swap_send.at[c, slot],
            recv_sem=swap_recv.at[c, slot],
            device_id=device(here, 1 - core),
            device_id_type=MESH,
        )
        copy.start()
        swaps.append(copy)

    for c in range(3):
        send(c, 0)
    local.wait()
    for phase in (1, 2):
        for c in range(3):
            for offset in range(1, SIDE):
                hops[c, phase - 1, offset].wait_recv()
            send(c, phase)
    for c in range(3):
        swap(c, 0, here)
    for offset in range(1, SIDE):
        for c in range(3):
            hops[c, 2, offset].wait_recv()
            swap(c, offset, moved(orders[c][2], SIDE - offset))
    for copy in hops.values():
        copy.wait_send()
    for copy in swaps:
        copy.wait()


def gather_blocks(mine):
    blocks = mine.shape[0]
    cuts = (0, blocks // 3, 2 * blocks // 3, blocks)
    return pl.pallas_call(
        functools.partial(gather_kernel, cuts),
        out_shape=jax.ShapeDtypeStruct((SIDE, 2, SIDE, SIDE) + mine.shape, mine.dtype),
        in_specs=[pl.BlockSpec(memory_space=pl.ANY)],
        out_specs=pl.BlockSpec(memory_space=pl.ANY),
        scratch_shapes=[
            pltpu.SemaphoreType.DMA,
            pltpu.SemaphoreType.DMA((3, 3, SIDE)),
            pltpu.SemaphoreType.DMA((3, 3, SIDE)),
            pltpu.SemaphoreType.DMA((3, SIDE)),
            pltpu.SemaphoreType.DMA((3, SIDE)),
        ],
        compiler_params=pltpu.CompilerParams(collective_id=0, has_side_effects=True),
        name="gather_blocks",
    )(mine)


CHUNK = 32
PER = 4
GROUP = 8


def project_kernel(
    total_ref,
    plan_ref,
    counts_ref,
    codes_ref,
    runs_ref,
    blocks_ref,
    first_ref,
    rate_ref,
    green_ref,
    pot_ref,
    buffer,
    owner_ref,
    extra_ref,
    extra_run,
    extra_from,
    y_rows,
    rho_rows,
    coefs_ref,
):
    listed = counts_ref.shape[0]
    pts = first_ref.shape[1]
    coefs_ref[...] = jnp.zeros_like(coefs_ref)
    y_rows[...] = jnp.zeros_like(y_rows)
    buffer[...] = jnp.zeros_like(buffer)
    for f in range(2 * GROUP):
        owner_ref[f] = 0
    extra_ref[0] = 0
    lane = lax.broadcasted_iota(jnp.int32, (4, pts), 1)

    def piece(device, start, length, position):
        at = lax.shift_right_logical(start, 7)
        off = lax.bitwise_and(start, 127)
        value = jnp.where(lane >= off, blocks_ref[device, at], blocks_ref[device, at + 1])
        left = position * CHUNK
        moved = pltpu.roll(value, lax.bitwise_and(left - off + 128, 127), 1)
        keep = (lane >= left) & (lane < left + length)
        return jnp.where(keep, moved, 0.0)

    def collect(g, half):
        owners, values, runs = [], [], []
        longest = jnp.int32(0)
        for f in range(GROUP):
            plan = plan_ref[g * GROUP + f]
            j = lax.shift_right_logical(plan, 12)
            r = lax.bitwise_and(plan, 4095)
            count = jnp.where(g * GROUP + f < total_ref[0], counts_ref[j], 0)
            owners.append(j)
            value = None
            for v in range(PER):
                code = codes_ref[r + v, j]
                device = lax.shift_right_logical(code, 7)
                run = runs_ref[device, lax.bitwise_and(code, 127)]
                length = jnp.where(r + v < count, lax.bitwise_and(run, 4095), 0)
                start = lax.shift_right_logical(run, 12)
                longest = jnp.maximum(longest, length)
                part = piece(device, start, jnp.minimum(length, CHUNK), v)
                value = part if value is None else value + part
                runs.append((device, start, length, j))
            values.append(value)
        for f in range(GROUP):
            row = half * GROUP + f
            buffer[pl.ds(row * 4, 4), :] = values[f]
            owner_ref[row] = owners[f]
        return longest, runs

    def note(longest, runs):
        @pl.when(longest > CHUNK)
        def _():
            for device, start, length, j in runs:

                @pl.when(length > CHUNK)
                def _():
                    at = extra_ref[0]
                    extra_run[at] = start * 4096 + length
                    extra_from[at] = device * 4096 + j
                    extra_ref[0] = at + 1

    def flush(half):
        def component(c):
            return buffer[pl.ds(half * (4 * GROUP) + c, GROUP, stride=4), :]

        dx, dy, dz, weight = (component(c) for c in range(4))
        square = dx * dx + dy * dy + dz * dz + 1.0
        inv = lax.rsqrt(square)
        rho_rows[...] = square * inv

        def emit(i, value):
            y_rows[pl.ds(i, GROUP, stride=HP), :] = value * weight

        harmonic_rows(dx * inv, dy * inv, dz * inv, 6, emit)
        sums = []
        for f in range(GROUP):
            radial = radial_values(rho_rows[f : f + 1, :], first_ref, rate_ref)
            rows = y_rows[f * HP : (f + 1) * HP, :].astype(jnp.bfloat16)
            sums.append(
                lax.dot_general(
                    rows, radial, (((1,), (1,)), ((), ())), preferred_element_type=jnp.float32
                )
            )
        for f in range(GROUP):
            at = pl.ds(pl.multiple_of(owner_ref[half * GROUP + f] * YR, 8), YR)
            coefs_ref[at, :] = coefs_ref[at, :] + sums[f][0:YR]

    groups = (total_ref[0] + (GROUP - 1)) // GROUP
    note(*collect(0, 0))

    @pl.loop(0, groups)
    def _(g):
        half = lax.bitwise_and(g, 1)
        later = jnp.minimum(g + 1, groups - 1)
        longest, runs = collect(later, 1 - half)
        flush(half)
        note(jnp.where(later > g, longest, 0), runs)

    @pl.when(extra_ref[0] > 0)
    def _():
        buffer[...] = jnp.zeros_like(buffer)
        extra_ref[1] = 0

        @pl.loop(0, extra_ref[0])
        def _(n):
            run, source = extra_run[n], extra_from[n]
            device, j = lax.shift_right_logical(source, 12), lax.bitwise_and(source, 4095)
            start = lax.shift_right_logical(run, 12) + CHUNK
            length = lax.bitwise_and(run, 4095) - CHUNK

            @pl.loop(0, lax.shift_right_logical(length + (pts - 1), 7))
            def _(c):
                row = extra_ref[1]
                part = piece(device, start + c * pts, jnp.minimum(length - c * pts, pts), 0)
                buffer[pl.ds(row * 4, 4), :] = part
                owner_ref[row] = j
                extra_ref[1] = row + 1

                @pl.when(row + 1 == GROUP)
                def _():
                    flush(0)
                    buffer[...] = jnp.zeros_like(buffer)
                    extra_ref[1] = 0

        flush(0)

    for l in range(7):
        top = green_ref[l]
        high = top.astype(jnp.bfloat16)
        low = (top - high.astype(jnp.float32)).astype(jnp.bfloat16)
        half = jnp.concatenate([high, low], axis=1)
        table = jnp.concatenate([half, half], axis=0)
        for i in range(l * l, (l + 1) * (l + 1)):
            at = pl.ds(i, listed, stride=YR)
            rows = coefs_ref[at, :]
            big = rows.astype(jnp.bfloat16)
            small = (rows - big.astype(jnp.float32)).astype(jnp.bfloat16)
            both = jnp.dot(
                jnp.concatenate([big, small], axis=1), table, preferred_element_type=jnp.float32
            )
            coefs_ref[at, :] = both[:, 0:128] + both[:, 128:256]

    @pl.loop(0, listed // 8)
    def _(g):
        for v in range(8):
            j = g * 8 + v
            rows = coefs_ref[pl.ds(pl.multiple_of(j * YR, 8), YR), :]
            pot_ref[j] = jnp.concatenate(
                [rows, jnp.zeros((HP - YR, rows.shape[1]), jnp.float32)], axis=0
            ).astype(jnp.bfloat16)


def block_plan(counts, devices):
    listed = counts.shape[0]
    index = jnp.arange(listed)
    needed = (counts + (PER - 1)) // PER
    ends = jnp.sum(jnp.where(index[None, :] <= index[:, None], needed[None, :], 0), axis=1)
    starts = ends - needed
    most = listed * (devices // PER) + GROUP
    block = jnp.arange(most)[:, None]
    inside = (block >= starts[None, :]) & (block < ends[None, :])
    value = index[None, :] * 4096 + (block - starts[None, :]) * PER
    plan = jnp.sum(jnp.where(inside, value, 0), axis=1)
    total = ends[listed - 1]
    return total.reshape(1).astype(jnp.int32), plan.astype(jnp.int32)


def project(counts, codes, runs, blocks, tables, green):
    listed = counts.shape[0]
    pts = tables[0].shape[1]
    smem = pl.BlockSpec(memory_space=pltpu.SMEM)
    vmem = pl.BlockSpec(memory_space=pltpu.VMEM)
    total, plan = block_plan(counts, codes.shape[0])
    return pl.pallas_call(
        project_kernel,
        out_shape=jax.ShapeDtypeStruct((listed, HP, NRAD), jnp.bfloat16),
        in_specs=[smem] * 5 + [vmem] * 4,
        out_specs=vmem,
        scratch_shapes=[
            pltpu.VMEM((2 * GROUP * 4, pts), jnp.float32),
            pltpu.SMEM((2 * GROUP,), jnp.int32),
            pltpu.SMEM((2,), jnp.int32),
            pltpu.SMEM((codes.size,), jnp.int32),
            pltpu.SMEM((codes.size,), jnp.int32),
            pltpu.VMEM((GROUP * HP, pts), jnp.float32),
            pltpu.VMEM((GROUP, pts), jnp.float32),
            pltpu.VMEM((YR * listed, NRAD), jnp.float32),
        ],
        compiler_params=pltpu.CompilerParams(vmem_limit_bytes=40 << 20),
        name="project",
    )(total, plan, counts, codes, runs, blocks, *tables, green)


def scatter_kernel(blocks_ref, lists_ref, rows_at, out_ref, acc_ref):
    devices, _, _, listed = blocks_ref.shape
    wide = 256
    acc_ref[...] = jnp.zeros_like(acc_ref)
    column = lax.broadcasted_iota(jnp.int32, (wide, listed), 0)
    groups = acc_ref.shape[0] // 32

    steps = 8

    @pl.loop(0, devices // steps)
    def _(g):
        total = acc_ref[...]
        for v in range(0, steps, 2):
            targets, parts = [], []
            for q in (g * steps + v, g * steps + v + 1):
                ids = lists_ref[pl.ds(q, 1), :]
                targets.append(
                    (column == lax.bitwise_and(ids, wide - 1)).astype(jnp.bfloat16)
                )
                group = lax.shift_right_logical(ids, 8)
                tiles = [blocks_ref[q, rows_at + m] for m in range(3)]
                mom = jnp.concatenate(tiles + [jnp.zeros((4, listed), jnp.float32)], axis=0)
                top = mom.astype(jnp.bfloat16).astype(jnp.float32)
                both = [
                    jnp.where(group == h, half, 0.0)
                    for h in range(groups)
                    for half in (top, mom - top)
                ]
                parts.append(jnp.concatenate(both, axis=0).astype(jnp.bfloat16))
            total = total + lax.dot_general(
                jnp.concatenate(parts, axis=1),
                jnp.concatenate(targets, axis=1),
                (((1,), (1,)), ((), ())),
                preferred_element_type=jnp.float32,
            )
        acc_ref[...] = total

    for h in range(groups):
        out_ref[:, h * wide : (h + 1) * wide] = (
            acc_ref[h * 32 + 1 : h * 32 + 10, :] + acc_ref[h * 32 + 17 : h * 32 + 26, :]
        )


def scatter_moments(blocks, lists, atoms):
    return pl.pallas_call(
        lambda b, l, o, a: scatter_kernel(b, l, blocks.shape[1] - 3, o, a),
        out_shape=jax.ShapeDtypeStruct((9, atoms), jnp.float32),
        scratch_shapes=[pltpu.VMEM((atoms // 256 * 32, 256), jnp.float32)],
        compiler_params=pltpu.CompilerParams(vmem_limit_bytes=40 << 20),
        name="scatter_moments",
    )(blocks, lists)


def entry_tables(lists, my_list):
    devices, listed = lists.shape
    same = lists[:, :, None] == my_list[None, None, :]
    slot = jnp.arange(1, listed + 1, dtype=jnp.int32)[None, :, None]
    held = jnp.sum(jnp.where(same, slot, 0), axis=1)
    present = held > 0
    order = jnp.arange(devices)
    rank = jnp.dot(
        (order[None, :] < order[:, None]).astype(jnp.bfloat16),
        present.astype(jnp.bfloat16),
        preferred_element_type=jnp.float32,
    ).astype(jnp.int32)
    rank = jnp.where(present, rank, devices)
    code = order[:, None].astype(jnp.int32) * listed + held - 1
    picked = rank[None, :, :] == order[:, None, None]
    codes = jnp.sum(jnp.where(picked, code[None], 0), axis=1)
    return jnp.sum(present.astype(jnp.int32), axis=0), codes


def per_device(
    grid_points,
    weighted_density,
    point_slot,
    near_slot,
    slot_atom,
    atom_pos,
    decay_rates,
    green,
    moment_table,
):
    count_y = lax.axis_size("sy")
    devices = lax.axis_size("sx") * count_y
    myself = lax.axis_index("sx") * count_y + lax.axis_index("sy")
    lists = slot_atom.reshape(devices, -1)
    my_list = lists[myself]
    atoms = atom_pos.shape[1]
    pts = grid_points.shape[1] // near_slot.shape[0]
    tables = radial_tables(decay_rates, pts)
    places = atom_pos[:, my_list]
    mine = point_blocks(grid_points, weighted_density, point_slot, places, tables, moment_table)
    gathered = gather_blocks(mine)
    blocks = gathered.reshape((devices,) + mine.shape)
    counts, codes = entry_tables(lists, my_list)
    runs = blocks[:, mine.shape[0] - 3, 0, :].astype(jnp.int32)
    slot_pot = project(counts, codes, runs, blocks, tables, green)
    moments = scatter_moments(blocks, lists, atoms)
    slot_table = jnp.concatenate([places, moments[:, my_list]], axis=0).T
    slot_table = jnp.pad(slot_table, ((0, 0), (0, 128 - slot_table.shape[1])))
    return evaluate(
        grid_points, near_slot, slot_table, slot_pot, atom_pos, moments, decay_rates
    )


def solution(mesh):
    return jax.shard_map(
        per_device,
        mesh=mesh,
        in_specs=(
            P(None, ("sx", "sy")),
            P(("sx", "sy")),
            P(("sx", "sy")),
            P(("sx", "sy"), None),
            P(),
            P(),
            P(),
            P(),
            P(),
        ),
        out_specs=P(("sx", "sy")),
        check_vma=False,
    )
```

```python
import functools
import math

import jax
import jax.numpy as jnp
from jax import lax
from jax.experimental import pallas as pl
from jax.experimental.pallas import tpu as pltpu
from jax.sharding import PartitionSpec as P

HARM = 49
NRAD = 128


def shell_layout(decay_rates):
    count = decay_rates.shape[0]
    spacing = 27.0 / (count - 1)
    centres = 1.0 + spacing * jnp.arange(count).astype(decay_rates.dtype)
    return (centres, spacing)


HP = 64
YR = 56


def y_factor(l, m):
    factor = math.sqrt(
        (2 * l + 1) / (4 * math.pi) * math.factorial(l - m) / math.factorial(l + m)
    )
    return factor if m == 0 else factor * math.sqrt(2.0)


def harmonic_rows(x, y, z, top, emit):
    square = x * x + y * y + z * z
    cos_m, sin_m = None, None
    for m in range(top + 1):
        if m == 1:
            cos_m, sin_m = x, y
        elif m > 1:
            cos_m, sin_m = cos_m * x - sin_m * y, cos_m * y + sin_m * x
        double = float(math.prod(range(1, 2 * m, 2)))
        ladder = {}
        for l in range(m, top + 1):
            if l == m + 1:
                ladder[l] = z * float(2 * m + 1)
            elif l == m + 2:
                ladder[l] = z * ladder[l - 1] * ((2 * l - 1) / 2) - square * ((l + m - 1) / 2)
            elif l > m + 2:
                ladder[l] = z * ladder[l - 1] * ((2 * l - 1) / (l - m)) - square * ladder[l - 2] * (
                    (l + m - 1) / (l - m)
                )
            scale = y_factor(l, m) * double
            part = ladder[l] * scale if l > m else scale
            if m == 0:
                emit(l * l, part if l > m else jnp.full_like(x, part))
            else:
                emit(l * l + 2 * m - 1, cos_m * part)
                emit(l * l + 2 * m, sin_m * part)


def split3(value):
    high = value.astype(jnp.bfloat16).astype(jnp.float32)
    rest = value - high
    middle = rest.astype(jnp.bfloat16).astype(jnp.float32)
    return high, middle, rest - middle


SPACING = 27.0 / (NRAD - 1)
SHELL_ROWS = 16


def radial_values(rho, first_ref, rate_ref, dtype=jnp.bfloat16):
    rows, pts = first_ref.shape[0], rho.shape[1]
    base = jnp.broadcast_to(rho, (rows, pts)) - first_ref[...]
    pieces = []
    for k in range(0, NRAD, rows):
        e = base - (SPACING * k)
        power = (e * e) * rate_ref[k : k + rows, :]
        pieces.append(jnp.exp2(power.astype(dtype)))
    return jnp.concatenate(pieces, axis=0)


def radial_tables(decay_rates, width):
    centres, spacing = shell_layout(decay_rates)
    factor = decay_rates * (-math.log2(math.e) / spacing**2)
    return (
        jnp.broadcast_to(centres[:SHELL_ROWS, None], (SHELL_ROWS, width)),
        jnp.broadcast_to(factor[:, None], (decay_rates.shape[0], width)),
    )


FARC = 8
FEATURES = 9
FEATURE_ROWS = 6 * FEATURES + 3
FAR_ROWS = 64


def far_tables(atoms_ref, moments_ref, rows_ref, table_ref):
    atoms = atoms_ref.shape[1]
    ax = atoms_ref[0:1, :] - 8.0
    ay = atoms_ref[1:2, :] - 8.0
    az = atoms_ref[2:3, :] - 8.0
    mom = [moments_ref[i : i + 1, :] for i in range(9)]
    one, nil = jnp.ones_like(ax), jnp.zeros_like(ax)
    n10, n11 = y_factor(1, 0), y_factor(1, 1)
    vx, vy, vz = mom[2] * n11, mom[3] * n11, mom[1] * n10
    f20, f21, f22 = y_factor(2, 0), 3.0 * y_factor(2, 1), 3.0 * y_factor(2, 2)
    qzz = mom[4] * f20
    qxx = mom[7] * f22 - qzz * 0.5
    qyy = -mom[7] * f22 - qzz * 0.5
    qxz, qyz, qxy = mom[5] * f21, mom[6] * f21, mom[8] * (2.0 * f22)
    gx = -(2.0 * qxx * ax + qxy * ay + qxz * az)
    gy = -(qxy * ax + 2.0 * qyy * ay + qyz * az)
    gz = -(qxz * ax + qyz * ay + 2.0 * qzz * az)
    const = -0.5 * (gx * ax + gy * ay + gz * az)
    norm = ax * ax + ay * ay + az * az + 1.0
    plans = [
        ([-2.0 * ax, -2.0 * ay, -2.0 * az, one, one, one, nil, nil, nil], norm),
        ([vx, vy, vz, nil, nil, nil, nil, nil, nil], -(vx * ax + vy * ay + vz * az)),
        ([gx, gy, gz, qxx, qyy, qzz, qxy, qxz, qyz], const),
    ]
    for q, (coefs, fixed) in enumerate(plans):
        columns = pl.ds(q * atoms, atoms)
        for f, coef in enumerate(coefs):
            high, middle, low = split3(coef)
            for r, row in enumerate((high, middle, high, low, high, middle)):
                rows_ref[6 * f + r : 6 * f + r + 1, columns] = row
        for r, row in enumerate(split3(fixed)):
            rows_ref[6 * FEATURES + r : 6 * FEATURES + r + 1, columns] = row
        rows_ref[FEATURE_ROWS:FAR_ROWS, columns] = jnp.zeros(
            (FAR_ROWS - FEATURE_ROWS, atoms), jnp.float32
        )
    table_ref[...] = rows_ref[...].astype(jnp.bfloat16)


def point_features(px, py, pz, rows_ref):
    qx, qy, qz = px - 8.0, py - 8.0, pz - 8.0
    values = [qx, qy, qz, qx * qx, qy * qy, qz * qz, qx * qy, qx * qz, qy * qz]
    for f, value in enumerate(values):
        high, middle, low = split3(value)
        for r, row in enumerate((high, high, middle, high, low, middle)):
            rows_ref[6 * f + r : 6 * f + r + 1, :] = row
    rows_ref[6 * FEATURES : FEATURE_ROWS, :] = jnp.ones((3, qx.shape[1]), jnp.float32)
    rows_ref[FEATURE_ROWS:FAR_ROWS, :] = jnp.zeros(
        (FAR_ROWS - FEATURE_ROWS, qx.shape[1]), jnp.float32
    )
    return rows_ref[...].T.astype(jnp.bfloat16)


def evaluate_kernel(
    near_smem,
    near_ref,
    points_ref,
    slot_table_ref,
    slot_pot_ref,
    atoms_ref,
    moments_ref,
    first_ref,
    rate_ref,
    out_ref,
    far_rows,
    far_table,
    feat_rows,
    far_acc,
    y_rows,
    rho_rows,
    corr_ref,
):
    b = pl.program_id(0)
    near_count = near_ref.shape[2]
    pts = points_ref.shape[1]
    atoms = atoms_ref.shape[1]

    @pl.when(b == 0)
    def _():
        far_tables(atoms_ref, moments_ref, far_rows, far_table)
        y_rows[...] = jnp.zeros_like(y_rows)

    px, py, pz = points_ref[0:1, :], points_ref[1:2, :], points_ref[2:3, :]

    features = point_features(px, py, pz, feat_rows)
    far_acc[...] = jnp.zeros_like(far_acc)
    chunk = 256

    for c in range(FARC):
        base = c * chunk

        def table(q):
            return far_table[:, q * atoms + base : q * atoms + base + chunk]

        square = jnp.dot(features, table(0), preferred_element_type=jnp.float32)
        linear = jnp.dot(features, table(1), preferred_element_type=jnp.float32)
        quad = jnp.dot(features, table(2), preferred_element_type=jnp.float32)
        inv = lax.rsqrt(square)
        inv2 = inv * inv
        level = moments_ref[0:1, pl.ds(base, chunk)] * y_factor(0, 0)
        value = inv * (level + inv2 * (linear + inv2 * quad))
        far_acc[...] += value[:, 0:128] + value[:, 128:256]

    far_row = jnp.sum(far_acc[...].T, axis=0, keepdims=True)

    hot = (
        lax.broadcasted_iota(jnp.int32, (slot_table_ref.shape[1], near_count), 0) == near_ref[0]
    ).astype(jnp.float32)
    info = lax.dot_general(
        hot,
        slot_table_ref[...],
        (((0,), (1,)), ((), ())),
        precision=lax.Precision.HIGHEST,
        preferred_element_type=jnp.float32,
    )
    step = 8
    corr = jnp.zeros((step, pts), jnp.float32)
    for j in range(0, near_count, step):
        part = info[j : j + step, :]
        dx = px - part[:, 0:1]
        dy = py - part[:, 1:2]
        dz = pz - part[:, 2:3]
        square = dx * dx + dy * dy + dz * dz + 1.0
        inv = lax.rsqrt(square)
        rho_rows[j : j + step, :] = square * inv
        low = {}

        def emit(i, value):
            y_rows[pl.ds(j * YR + i, step, stride=YR), :] = value
            if i < 9:
                low[i] = value

        harmonic_rows(dx * inv, dy * inv, dz * inv, 6, emit)
        term = [part[:, 3 + i : 4 + i] * low[i] for i in range(9)]
        degree1 = term[1] + term[2] + term[3]
        degree2 = (term[4] + term[5]) + (term[6] + term[7]) + term[8]
        corr = corr + inv * (term[0] + inv * (degree1 + inv * degree2))
    corr_ref[...] = corr

    unroll = 32

    def pairs(g, total):
        for v in range(unroll):
            j = g * unroll + v
            coefs = slot_pot_ref[near_smem[b, j]]
            radial = radial_values(rho_rows[pl.ds(j, 1), :], first_ref, rate_ref)
            values = jnp.dot(coefs, radial, preferred_element_type=jnp.float32)
            rows = y_rows[pl.ds(pl.multiple_of(j * YR, YR), YR), :]
            total = total + values[0:YR] * rows
        return total

    total = lax.fori_loop(
        0, near_count // unroll, pairs, jnp.zeros((YR, pts), jnp.float32)
    )
    near_row = jnp.sum(total, axis=0, keepdims=True)
    out_ref[0] = near_row + far_row - jnp.sum(corr_ref[...], axis=0, keepdims=True)


def evaluate(points, near_slot, slot_table, slot_pot, atom_pos, moments, decay_rates):
    batches, near_count = near_slot.shape
    pts = points.shape[1] // batches
    atoms = atom_pos.shape[1]
    first, factor = radial_tables(decay_rates, pts)

    def whole(shape):
        return pl.BlockSpec(shape, lambda b, near: (0,) * len(shape))

    out = pl.pallas_call(
        evaluate_kernel,
        out_shape=jax.ShapeDtypeStruct((batches, 1, pts), jnp.float32),
        grid_spec=pltpu.PrefetchScalarGridSpec(
            num_scalar_prefetch=1,
            grid=(batches,),
            in_specs=[
                pl.BlockSpec((1, 1, near_count), lambda b, near: (b, 0, 0)),
                pl.BlockSpec((3, pts), lambda b, near: (0, b)),
                whole(slot_table.shape),
                whole(slot_pot.shape),
                whole(atom_pos.shape),
                whole(moments.shape),
                whole(first.shape),
                whole(factor.shape),
            ],
            out_specs=pl.BlockSpec((1, 1, pts), lambda b, near: (b, 0, 0)),
            scratch_shapes=[
                pltpu.VMEM((FAR_ROWS, 3 * atoms), jnp.float32),
                pltpu.VMEM((FAR_ROWS, 3 * atoms), jnp.bfloat16),
                pltpu.VMEM((FAR_ROWS, pts), jnp.float32),
                pltpu.VMEM((pts, 128), jnp.float32),
                pltpu.VMEM((near_count * YR, pts), jnp.float32),
                pltpu.VMEM((near_count, pts), jnp.float32),
                pltpu.VMEM((8, pts), jnp.float32),
            ],
        ),
        compiler_params=pltpu.CompilerParams(
            dimension_semantics=("arbitrary",), vmem_limit_bytes=40 << 20
        ),
        name="evaluate",
    )(
        near_slot,
        near_slot.reshape(batches, 1, near_count),
        points,
        slot_table,
        slot_pot,
        atom_pos,
        moments,
        first,
        factor,
    )
    return out.reshape(-1)


def point_blocks_kernel(
    points_ref,
    density_ref,
    slots_ref,
    places_ref,
    first_ref,
    rate_ref,
    table_ref,
    out_ref,
    four_ref,
    q_rows,
):
    listed = places_ref.shape[1]
    pts = first_ref.shape[1]
    blocks = points_ref.shape[1] // pts
    slot_rows = lax.broadcasted_iota(jnp.int32, (listed, pts), 0)
    lane = lax.broadcasted_iota(jnp.int32, (listed, pts), 1)
    earlier = (slot_rows < lane).astype(jnp.bfloat16)
    counts = jnp.zeros((listed, 1), jnp.float32)
    ranks, hots = [], []
    for g in range(blocks):
        at = pl.ds(g * pts, pts)
        same = slot_rows == slots_ref[:, at]
        hot = same.astype(jnp.float32)
        inside = jnp.dot(hot.astype(jnp.bfloat16), earlier, preferred_element_type=jnp.float32)
        ranks.append(jnp.sum(hot * (inside + counts), axis=0, keepdims=True))
        counts = counts + jnp.sum(hot, axis=1, keepdims=True)
    below = (lax.broadcasted_iota(jnp.int32, (listed, listed), 1) < lax.broadcasted_iota(
        jnp.int32, (listed, listed), 0
    )).astype(jnp.float32)
    counts_full = jnp.broadcast_to(counts, (listed, listed))
    starts_full = jnp.dot(
        below, counts_full, precision=lax.Precision.HIGHEST, preferred_element_type=jnp.float32
    )
    starts = starts_full[:, 0:1]
    packed = starts_full * 4096.0 + counts_full
    rows64 = lax.broadcasted_iota(jnp.int32, (4 * blocks, pts), 0) // 4
    sorted_rows = jnp.zeros((4 * blocks, pts), jnp.float32)
    moments = jnp.zeros((16, listed), jnp.float32)
    q_rows[...] = jnp.zeros_like(q_rows)
    for g in range(blocks):
        at = pl.ds(g * pts, pts)
        hot = (slot_rows == slots_ref[:, at]).astype(jnp.float32)
        place = ranks[g] + jnp.sum(hot * starts, axis=0, keepdims=True)
        place = place.astype(jnp.int32)
        atom = jnp.dot(
            places_ref[...], hot, precision=lax.Precision.HIGHEST, preferred_element_type=jnp.float32
        )
        dx = points_ref[0:1, at] - atom[0:1]
        dy = points_ref[1:2, at] - atom[1:2]
        dz = points_ref[2:3, at] - atom[2:3]
        weight = density_ref[:, at]
        for r in range(2):
            for c, value in enumerate((dx, dy, dz, weight)):
                four_ref[4 * r + c : 4 * r + c + 1, :] = value
        tiled = jnp.concatenate([four_ref[...]] * (blocks // 2), axis=0)
        masked = jnp.where(rows64 == place // pts, tiled, 0.0)
        target = (slot_rows == place % pts).astype(jnp.bfloat16)
        for piece in split3(masked):
            sorted_rows = sorted_rows + lax.dot_general(
                piece.astype(jnp.bfloat16),
                target,
                (((1,), (1,)), ((), ())),
                preferred_element_type=jnp.float32,
            )
        square = dx * dx + dy * dy + dz * dz + 1.0
        inv = lax.rsqrt(square)
        rho = square * inv
        radial = radial_values(rho, first_ref, rate_ref, jnp.float32)
        levels = jnp.dot(
            table_ref[...], radial, precision=lax.Precision.HIGHEST, preferred_element_type=jnp.float32
        )

        def emit(i, value):
            degree = (0, 1, 1, 1, 2, 2, 2, 2, 2)[i]
            q_rows[i : i + 1, :] = value * weight * levels[degree : degree + 1]

        harmonic_rows(dx * inv, dy * inv, dz * inv, 2, emit)
        moments = moments + lax.dot_general(
            q_rows[...],
            hot,
            (((1,), (1,)), ((), ())),
            precision=lax.Precision.HIGHEST,
            preferred_element_type=jnp.float32,
        )
    out_ref[0 : 4 * blocks, :] = sorted_rows
    out_ref[4 * blocks : 4 * blocks + 1, :] = packed.T[0:1, :]
    out_ref[4 * blocks + 1 : 4 * blocks + 10, :] = moments[0:9]
    out_ref[4 * blocks + 10 : 4 * blocks + 12, :] = jnp.zeros((2, listed), jnp.float32)


def point_blocks(points, density, slots, places, tables, moment_table):
    count = points.shape[1]
    pts = tables[0].shape[1]
    rows = 4 * (count // pts) + 12
    out = pl.pallas_call(
        point_blocks_kernel,
        out_shape=jax.ShapeDtypeStruct((rows, pts), jnp.float32),
        scratch_shapes=[pltpu.VMEM((8, pts), jnp.float32), pltpu.VMEM((16, pts), jnp.float32)],
        compiler_params=pltpu.CompilerParams(vmem_limit_bytes=40 << 20),
        name="point_blocks",
    )(
        points,
        density.reshape(1, count),
        slots.reshape(1, count),
        places,
        *tables,
        moment_table,
    )
    return out.reshape(rows // 4, 4, pts)


MESH = pl.DeviceIdType.MESH
SIDE = 4


def gather_kernel(cuts, mine_ref, all_ref, local_sem, send_sems, recv_sems, swap_send, swap_recv):
    row, column = lax.axis_index("sx"), lax.axis_index("sy")
    core = lax.rem(row, 2)
    here = {"z": row // 2, "y": column // SIDE, "x": lax.rem(column, SIDE)}

    def device(place, on_core):
        return (place["z"] * 2 + on_core, place["y"] * SIDE + place["x"])

    def moved(axis, offset):
        place = dict(here)
        place[axis] = lax.rem(here[axis] + offset, SIDE)
        return place

    def region(place, whole, part):
        index = [pl.ds(0, SIDE) if a in whole else place[a] for a in ("z", "y", "x")]
        return all_ref.at[index[0], core, index[1], index[2], part]

    barrier = pltpu.get_barrier_semaphore()
    for axis in ("z", "y", "x"):
        for offset in range(1, SIDE):
            pl.semaphore_signal(
                barrier, inc=1, device_id=device(moved(axis, offset), core), device_id_type=MESH
            )
    pl.semaphore_signal(barrier, inc=1, device_id=device(here, 1 - core), device_id_type=MESH)
    pl.semaphore_wait(barrier, 3 * (SIDE - 1) + 1)

    local = pltpu.make_async_copy(mine_ref, region(here, "", pl.ds(0, cuts[-1])), local_sem)
    local.start()
    orders = ("xyz", "yzx", "zxy")
    parts = [pl.ds(cuts[c], cuts[c + 1] - cuts[c]) for c in range(3)]
    hops = {}
    swaps = []

    def send(c, phase):
        axis = orders[c][phase]
        whole = orders[c][:phase]
        for offset in range(1, SIDE):
            place = region(here, whole, parts[c])
            copy = pltpu.make_async_remote_copy(
                src_ref=mine_ref.at[parts[c]] if phase == 0 else place,
                dst_ref=place,
                send_sem=send_sems.at[c, phase, offset],
                recv_sem=recv_sems.at[c, phase, offset],
                device_id=device(moved(axis, offset), core),
                device_id_type=MESH,
            )
            copy.start()
            hops[c, phase, offset] = copy

    def swap(c, slot, place):
        area = region(place, orders[c][:2], parts[c])
        copy = pltpu.make_async_remote_copy(
            src_ref=area,
            dst_ref=area,
            send_sem=swap_send.at[c, slot],
            recv_sem=swap_recv.at[c, slot],
            device_id=device(here, 1 - core),
            device_id_type=MESH,
        )
        copy.start()
        swaps.append(copy)

    for c in range(3):
        send(c, 0)
    local.wait()
    for phase in (1, 2):
        for c in range(3):
            for offset in range(1, SIDE):
                hops[c, phase - 1, offset].wait_recv()
            send(c, phase)
    for c in range(3):
        swap(c, 0, here)
    for offset in range(1, SIDE):
        for c in range(3):
            hops[c, 2, offset].wait_recv()
            swap(c, offset, moved(orders[c][2], SIDE - offset))
    for copy in hops.values():
        copy.wait_send()
    for copy in swaps:
        copy.wait()


def gather_blocks(mine):
    blocks = mine.shape[0]
    cuts = (0, blocks // 3, 2 * blocks // 3, blocks)
    return pl.pallas_call(
        functools.partial(gather_kernel, cuts),
        out_shape=jax.ShapeDtypeStruct((SIDE, 2, SIDE, SIDE) + mine.shape, mine.dtype),
        in_specs=[pl.BlockSpec(memory_space=pl.ANY)],
        out_specs=pl.BlockSpec(memory_space=pl.ANY),
        scratch_shapes=[
            pltpu.SemaphoreType.DMA,
            pltpu.SemaphoreType.DMA((3, 3, SIDE)),
            pltpu.SemaphoreType.DMA((3, 3, SIDE)),
            pltpu.SemaphoreType.DMA((3, SIDE)),
            pltpu.SemaphoreType.DMA((3, SIDE)),
        ],
        compiler_params=pltpu.CompilerParams(collective_id=0, has_side_effects=True),
        name="gather_blocks",
    )(mine)


CHUNK = 32
PER = 4
LONG = 64
GROUP = 16


def project_kernel(
    lists,
    total_ref,
    plan_ref,
    codes_ref,
    words_ref,
    runs_ref,
    blocks_ref,
    first_ref,
    rate_ref,
    green_ref,
    pot_ref,
    buffer,
    owner_ref,
    extra_ref,
    extra_code,
    extra_owner,
    y_rows,
    rho_rows,
    coefs_ref,
):
    listed = codes_ref.shape[1]
    pts = first_ref.shape[1]
    coefs_ref[...] = jnp.zeros_like(coefs_ref)
    y_rows[...] = jnp.zeros_like(y_rows)
    buffer[...] = jnp.zeros_like(buffer)
    for f in range(2 * GROUP):
        owner_ref[f] = 0
    extra_ref[0] = 0
    lane = lax.broadcasted_iota(jnp.int32, (4, pts), 1)
    held = blocks_ref.shape[0] // lists

    def window(tile, off, left):
        value = jnp.where(lane >= off, blocks_ref[tile], blocks_ref[tile + 1])
        return pltpu.roll(value, lax.bitwise_and(left + 128 - off, 127), 1)

    def collect(g, half):
        owners, values, codes = [], [], []
        marks = jnp.int32(0)
        for f in range(GROUP):
            plan = plan_ref[g * GROUP + f]
            j = lax.shift_right_logical(plan, 12)
            r = lax.bitwise_and(plan, 4095)
            owners.append(j)
            value = jnp.zeros((4, pts), jnp.float32)
            for v in range(PER):
                code = codes_ref[r + v, j]
                word = words_ref[code]
                left = v * CHUNK
                moved = window(
                    lax.shift_right_logical(word, 16),
                    lax.bitwise_and(lax.shift_right_logical(word, 8), 127),
                    left,
                )
                right = left + lax.bitwise_and(word, 63)
                fresh = jnp.where(lane < right, moved, 0.0)
                value = fresh if v == 0 else jnp.where(lane < left, value, fresh)
                marks = lax.bitwise_or(marks, word)
                codes.append(code)
            values.append(value)
        for f in range(GROUP):
            row = half * GROUP + f
            buffer[pl.ds(row * 4, 4), :] = values[f]
            owner_ref[row] = owners[f]
        return marks, codes, owners

    def note(fresh, marks, codes, owners):
        @pl.when(fresh & (lax.bitwise_and(marks, LONG) > 0))
        def _():
            for n, code in enumerate(codes):

                @pl.when(lax.bitwise_and(words_ref[code], LONG) > 0)
                def _():
                    at = extra_ref[0]
                    extra_code[at] = code
                    extra_owner[at] = owners[n // PER]
                    extra_ref[0] = at + 1

    def flush(half):
        def component(c):
            return buffer[pl.ds(half * (4 * GROUP) + c, GROUP, stride=4), :]

        dx, dy, dz, weight = (component(c) for c in range(4))
        square = dx * dx + dy * dy + dz * dz + 1.0
        inv = lax.rsqrt(square)
        rho_rows[...] = square * inv

        def emit(i, value):
            y_rows[pl.ds(i, GROUP, stride=HP), :] = value * weight

        harmonic_rows(dx * inv, dy * inv, dz * inv, 6, emit)
        sums = []
        for f in range(GROUP):
            radial = radial_values(rho_rows[f : f + 1, :], first_ref, rate_ref)
            rows = y_rows[f * HP : (f + 1) * HP, :].astype(jnp.bfloat16)
            sums.append(
                lax.dot_general(
                    rows, radial, (((1,), (1,)), ((), ())), preferred_element_type=jnp.float32
                )
            )
        for f in range(GROUP):
            at = pl.ds(pl.multiple_of(owner_ref[half * GROUP + f] * YR, 8), YR)
            coefs_ref[at, :] = coefs_ref[at, :] + sums[f][0:YR]

    groups = (total_ref[0] + (GROUP - 1)) // GROUP
    note(groups > 0, *collect(0, 0))

    @pl.loop(0, groups)
    def _(g):
        half = lax.bitwise_and(g, 1)
        later = jnp.minimum(g + 1, groups - 1)
        found = collect(later, 1 - half)
        flush(half)
        note(later > g, *found)

    @pl.when(extra_ref[0] > 0)
    def _():
        buffer[...] = jnp.zeros_like(buffer)
        extra_ref[1] = 0

        @pl.loop(0, extra_ref[0])
        def _(n):
            code = extra_code[n]
            device = lax.shift_right_logical(code, 7)
            run = runs_ref[device, lax.bitwise_and(code, 127)]
            start = lax.shift_right_logical(run, 12) + CHUNK
            length = lax.bitwise_and(run, 4095) - CHUNK

            @pl.loop(0, lax.shift_right_logical(length + (pts - 1), 7))
            def _(c):
                row = extra_ref[1]
                place = start + c * pts
                tile = device * held + lax.shift_right_logical(place, 7)
                moved = window(tile, lax.bitwise_and(place, 127), 0)
                buffer[pl.ds(row * 4, 4), :] = jnp.where(lane < length - c * pts, moved, 0.0)
                owner_ref[row] = extra_owner[n]
                extra_ref[1] = row + 1

                @pl.when(row + 1 == GROUP)
                def _():
                    flush(0)
                    buffer[...] = jnp.zeros_like(buffer)
                    extra_ref[1] = 0

        flush(0)

    for l in range(7):
        top = green_ref[l]
        high = top.astype(jnp.bfloat16)
        low = (top - high.astype(jnp.float32)).astype(jnp.bfloat16)
        half = jnp.concatenate([high, low], axis=1)
        table = jnp.concatenate([half, half], axis=0)
        for i in range(l * l, (l + 1) * (l + 1)):
            at = pl.ds(i, listed, stride=YR)
            rows = coefs_ref[at, :]
            big = rows.astype(jnp.bfloat16)
            small = (rows - big.astype(jnp.float32)).astype(jnp.bfloat16)
            both = jnp.dot(
                jnp.concatenate([big, small], axis=1), table, preferred_element_type=jnp.float32
            )
            coefs_ref[at, :] = both[:, 0:128] + both[:, 128:256]

    @pl.loop(0, listed // 8)
    def _(g):
        for v in range(8):
            j = g * 8 + v
            rows = coefs_ref[pl.ds(pl.multiple_of(j * YR, 8), YR), :]
            pot_ref[j] = jnp.concatenate(
                [rows, jnp.zeros((HP - YR, rows.shape[1]), jnp.float32)], axis=0
            ).astype(jnp.bfloat16)


def block_plan(counts, devices):
    listed = counts.shape[0]
    index = jnp.arange(listed)
    needed = (counts + (PER - 1)) // PER
    ends = jnp.sum(jnp.where(index[None, :] <= index[:, None], needed[None, :], 0), axis=1)
    starts = ends - needed
    most = listed * (devices // PER) + GROUP
    block = jnp.arange(most)[:, None]
    inside = (block >= starts[None, :]) & (block < ends[None, :])
    value = index[None, :] * 4096 + (block - starts[None, :]) * PER
    plan = jnp.sum(jnp.where(inside, value, 0), axis=1)
    total = ends[listed - 1]
    plan = jnp.where(block[:, 0] < total, plan, devices)
    return total.reshape(1).astype(jnp.int32), plan.astype(jnp.int32)


def project(counts, codes, words, runs, blocks, tables, green):
    lists, listed = runs.shape
    pts = tables[0].shape[1]
    smem = pl.BlockSpec(memory_space=pltpu.SMEM)
    vmem = pl.BlockSpec(memory_space=pltpu.VMEM)
    total, plan = block_plan(counts, lists)
    return pl.pallas_call(
        functools.partial(project_kernel, lists),
        out_shape=jax.ShapeDtypeStruct((listed, HP, NRAD), jnp.bfloat16),
        in_specs=[smem] * 5 + [vmem] * 4,
        out_specs=vmem,
        scratch_shapes=[
            pltpu.VMEM((2 * GROUP * 4, pts), jnp.float32),
            pltpu.SMEM((2 * GROUP,), jnp.int32),
            pltpu.SMEM((2,), jnp.int32),
            pltpu.SMEM((codes.size,), jnp.int32),
            pltpu.SMEM((codes.size,), jnp.int32),
            pltpu.VMEM((GROUP * HP, pts), jnp.float32),
            pltpu.VMEM((GROUP, pts), jnp.float32),
            pltpu.VMEM((YR * listed, NRAD), jnp.float32),
        ],
        compiler_params=pltpu.CompilerParams(vmem_limit_bytes=40 << 20),
        name="project",
    )(total, plan, codes, words.reshape(-1), runs, blocks, *tables, green)


def scatter_kernel(
    lists_ref, blocks_ref, atoms_ref, mine_ref, places_ref, out_ref, info_ref, words_ref, runs_ref, acc_ref
):
    devices, listed = atoms_ref.shape
    held = blocks_ref.shape[0] // lists_ref
    wide = 256
    acc_ref[...] = jnp.zeros_like(acc_ref)
    column = lax.broadcasted_iota(jnp.int32, (wide, listed), 0)
    groups = acc_ref.shape[0] // 32
    steps = 8

    @pl.loop(0, devices // steps)
    def _(g):
        total = acc_ref[...]
        packed = []
        for v in range(0, steps, 2):
            targets, parts = [], []
            for q in (g * steps + v, g * steps + v + 1):
                ids = atoms_ref[pl.ds(q, 1), :]
                targets.append(
                    (column == lax.bitwise_and(ids, wide - 1)).astype(jnp.bfloat16)
                )
                group = lax.shift_right_logical(ids, 8)
                tiles = [blocks_ref[(q + 1) * held - 3 + m] for m in range(3)]
                packed.append(tiles[0][0:1])
                mom = jnp.concatenate(tiles + [jnp.zeros((4, listed), jnp.float32)], axis=0)
                top = mom.astype(jnp.bfloat16).astype(jnp.float32)
                both = [
                    jnp.where(group == h, half, 0.0)
                    for h in range(groups)
                    for half in (top, mom - top)
                ]
                parts.append(jnp.concatenate(both, axis=0).astype(jnp.bfloat16))
            total = total + lax.dot_general(
                jnp.concatenate(parts, axis=1),
                jnp.concatenate(targets, axis=1),
                (((1,), (1,)), ((), ())),
                preferred_element_type=jnp.float32,
            )
        acc_ref[...] = total
        at = pl.ds(pl.multiple_of(g * steps, steps), steps)
        run = jnp.concatenate(packed, axis=0).astype(jnp.int32)
        runs_ref[at, :] = run
        start, length = lax.shift_right_logical(run, 12), lax.bitwise_and(run, 4095)
        device = g * steps + lax.broadcasted_iota(jnp.int32, (steps, listed), 0)
        tile = device * held + lax.shift_right_logical(start, 7)
        word = tile * 65536 + lax.bitwise_and(start, 127) * 256 + jnp.minimum(length, CHUNK)
        words_ref[at, :] = word + jnp.where(length > CHUNK, LONG, 0)

    words_ref[devices : devices + 8, :] = jnp.zeros((8, listed), jnp.int32)
    mine = jnp.zeros((16, listed), jnp.float32)
    for h in range(groups):
        both = acc_ref[h * 32 : h * 32 + 16, :] + acc_ref[h * 32 + 16 : h * 32 + 32, :]
        out_ref[:, h * wide : (h + 1) * wide] = both[1:10]
        mine = mine + jnp.dot(
            both,
            (column + h * wide == mine_ref[...]).astype(jnp.float32),
            precision=lax.Precision.HIGHEST,
            preferred_element_type=jnp.float32,
        )
    info_ref[...] = jnp.zeros_like(info_ref)
    info_ref[0:3, :] = places_ref[...]
    info_ref[3:12, :] = mine[1:10]


def scatter_moments(blocks, lists, my_list, places, atoms):
    devices, listed = lists.shape
    return pl.pallas_call(
        functools.partial(scatter_kernel, devices),
        out_shape=(
            jax.ShapeDtypeStruct((9, atoms), jnp.float32),
            jax.ShapeDtypeStruct((16, listed), jnp.float32),
            jax.ShapeDtypeStruct((devices + 8, listed), jnp.int32),
            jax.ShapeDtypeStruct((devices, listed), jnp.int32),
        ),
        scratch_shapes=[pltpu.VMEM((atoms // 256 * 32, 256), jnp.float32)],
        compiler_params=pltpu.CompilerParams(vmem_limit_bytes=40 << 20),
        name="scatter_moments",
    )(blocks, lists, my_list.reshape(1, listed), places)


def entry_tables(lists, my_list):
    devices, listed = lists.shape
    same = lists[:, :, None] == my_list[None, None, :]
    slot = jnp.arange(1, listed + 1, dtype=jnp.int32)[None, :, None]
    held = jnp.sum(jnp.where(same, slot, 0), axis=1)
    present = held > 0
    order = jnp.arange(devices)
    rank = jnp.dot(
        (order[None, :] < order[:, None]).astype(jnp.bfloat16),
        present.astype(jnp.bfloat16),
        preferred_element_type=jnp.float32,
    ).astype(jnp.int32)
    rank = jnp.where(present, rank, devices)
    code = order[:, None].astype(jnp.int32) * listed + held - 1
    row = jnp.arange(devices + 8)
    picked = rank[None, :, :] == row[:, None, None]
    picked = picked & present[None, :, :]
    none = devices * listed
    codes = none + jnp.sum(jnp.where(picked, code[None] - none, 0), axis=1)
    return jnp.sum(present.astype(jnp.int32), axis=0), codes


def per_device(
    grid_points,
    weighted_density,
    point_slot,
    near_slot,
    slot_atom,
    atom_pos,
    decay_rates,
    green,
    moment_table,
):
    count_y = lax.axis_size("sy")
    devices = lax.axis_size("sx") * count_y
    myself = lax.axis_index("sx") * count_y + lax.axis_index("sy")
    lists = slot_atom.reshape(devices, -1)
    my_list = lists[myself]
    atoms = atom_pos.shape[1]
    pts = grid_points.shape[1] // near_slot.shape[0]
    tables = radial_tables(decay_rates, pts)
    places = atom_pos[:, my_list]
    mine = point_blocks(grid_points, weighted_density, point_slot, places, tables, moment_table)
    gathered = gather_blocks(mine)
    blocks = gathered.reshape((devices * mine.shape[0],) + mine.shape[1:])
    counts, codes = entry_tables(lists, my_list)
    moments, slot_table, words, runs = scatter_moments(blocks, lists, my_list, places, atoms)
    slot_pot = project(counts, codes, words, runs, blocks, tables, green)
    return evaluate(
        grid_points, near_slot, slot_table, slot_pot, atom_pos, moments, decay_rates
    )


def solution(mesh):
    return jax.shard_map(
        per_device,
        mesh=mesh,
        in_specs=(
            P(None, ("sx", "sy")),
            P(("sx", "sy")),
            P(("sx", "sy")),
            P(("sx", "sy"), None),
            P(),
            P(),
            P(),
            P(),
            P(),
        ),
        out_specs=P(("sx", "sy")),
        check_vma=False,
    )
```

```python
import functools
import math

import jax
import jax.numpy as jnp
from jax import lax
from jax.experimental import pallas as pl
from jax.experimental.pallas import tpu as pltpu
from jax.sharding import PartitionSpec as P

HARM = 49
NRAD = 128


def shell_layout(decay_rates):
    count = decay_rates.shape[0]
    spacing = 27.0 / (count - 1)
    centres = 1.0 + spacing * jnp.arange(count).astype(decay_rates.dtype)
    return (centres, spacing)


HP = 64
YR = 56


def y_factor(l, m):
    factor = math.sqrt(
        (2 * l + 1) / (4 * math.pi) * math.factorial(l - m) / math.factorial(l + m)
    )
    return factor if m == 0 else factor * math.sqrt(2.0)


def harmonic_rows(x, y, z, top, emit):
    square = x * x + y * y + z * z
    cos_m, sin_m = None, None
    for m in range(top + 1):
        if m == 1:
            cos_m, sin_m = x, y
        elif m > 1:
            cos_m, sin_m = cos_m * x - sin_m * y, cos_m * y + sin_m * x
        double = float(math.prod(range(1, 2 * m, 2)))
        ladder = {}
        for l in range(m, top + 1):
            if l == m + 1:
                ladder[l] = z * float(2 * m + 1)
            elif l == m + 2:
                ladder[l] = z * ladder[l - 1] * ((2 * l - 1) / 2) - square * ((l + m - 1) / 2)
            elif l > m + 2:
                ladder[l] = z * ladder[l - 1] * ((2 * l - 1) / (l - m)) - square * ladder[l - 2] * (
                    (l + m - 1) / (l - m)
                )
            scale = y_factor(l, m) * double
            part = ladder[l] * scale if l > m else scale
            if m == 0:
                emit(l * l, part if l > m else jnp.full_like(x, part))
            else:
                emit(l * l + 2 * m - 1, cos_m * part)
                emit(l * l + 2 * m, sin_m * part)


def split3(value):
    high = value.astype(jnp.bfloat16).astype(jnp.float32)
    rest = value - high
    middle = rest.astype(jnp.bfloat16).astype(jnp.float32)
    return high, middle, rest - middle


SPACING = 27.0 / (NRAD - 1)
SHELL_ROWS = 16


def radial_values(rho, first_ref, rate_ref, dtype=jnp.bfloat16):
    rows, pts = first_ref.shape[0], rho.shape[1]
    base = jnp.broadcast_to(rho, (rows, pts)) - first_ref[...]
    pieces = []
    for k in range(0, NRAD, rows):
        e = base - (SPACING * k)
        power = (e * e) * rate_ref[k : k + rows, :]
        pieces.append(jnp.exp2(power.astype(dtype)))
    return jnp.concatenate(pieces, axis=0)


def radial_tables(decay_rates, width):
    centres, spacing = shell_layout(decay_rates)
    factor = decay_rates * (-math.log2(math.e) / spacing**2)
    return (
        jnp.broadcast_to(centres[:SHELL_ROWS, None], (SHELL_ROWS, width)),
        jnp.broadcast_to(factor[:, None], (decay_rates.shape[0], width)),
    )


FARC = 8
FEATURES = 9
FEATURE_ROWS = 6 * FEATURES + 3
FAR_ROWS = 64


def far_tables(atoms_ref, moments_ref, rows_ref, table_ref):
    atoms = atoms_ref.shape[1]
    ax = atoms_ref[0:1, :] - 8.0
    ay = atoms_ref[1:2, :] - 8.0
    az = atoms_ref[2:3, :] - 8.0
    mom = [moments_ref[i : i + 1, :] for i in range(9)]
    one, nil = jnp.ones_like(ax), jnp.zeros_like(ax)
    n10, n11 = y_factor(1, 0), y_factor(1, 1)
    vx, vy, vz = mom[2] * n11, mom[3] * n11, mom[1] * n10
    f20, f21, f22 = y_factor(2, 0), 3.0 * y_factor(2, 1), 3.0 * y_factor(2, 2)
    qzz = mom[4] * f20
    qxx = mom[7] * f22 - qzz * 0.5
    qyy = -mom[7] * f22 - qzz * 0.5
    qxz, qyz, qxy = mom[5] * f21, mom[6] * f21, mom[8] * (2.0 * f22)
    gx = -(2.0 * qxx * ax + qxy * ay + qxz * az)
    gy = -(qxy * ax + 2.0 * qyy * ay + qyz * az)
    gz = -(qxz * ax + qyz * ay + 2.0 * qzz * az)
    const = -0.5 * (gx * ax + gy * ay + gz * az)
    norm = ax * ax + ay * ay + az * az + 1.0
    plans = [
        ([-2.0 * ax, -2.0 * ay, -2.0 * az, one, one, one, nil, nil, nil], norm),
        ([vx, vy, vz, nil, nil, nil, nil, nil, nil], -(vx * ax + vy * ay + vz * az)),
        ([gx, gy, gz, qxx, qyy, qzz, qxy, qxz, qyz], const),
    ]
    for q, (coefs, fixed) in enumerate(plans):
        columns = pl.ds(q * atoms, atoms)
        for f, coef in enumerate(coefs):
            high, middle, low = split3(coef)
            for r, row in enumerate((high, middle, high, low, high, middle)):
                rows_ref[6 * f + r : 6 * f + r + 1, columns] = row
        for r, row in enumerate(split3(fixed)):
            rows_ref[6 * FEATURES + r : 6 * FEATURES + r + 1, columns] = row
        rows_ref[FEATURE_ROWS:FAR_ROWS, columns] = jnp.zeros(
            (FAR_ROWS - FEATURE_ROWS, atoms), jnp.float32
        )
    table_ref[...] = rows_ref[...].astype(jnp.bfloat16)


def point_features(px, py, pz, rows_ref):
    qx, qy, qz = px - 8.0, py - 8.0, pz - 8.0
    values = [qx, qy, qz, qx * qx, qy * qy, qz * qz, qx * qy, qx * qz, qy * qz]
    for f, value in enumerate(values):
        high, middle, low = split3(value)
        for r, row in enumerate((high, high, middle, high, low, middle)):
            rows_ref[6 * f + r : 6 * f + r + 1, :] = row
    rows_ref[6 * FEATURES : FEATURE_ROWS, :] = jnp.ones((3, qx.shape[1]), jnp.float32)
    rows_ref[FEATURE_ROWS:FAR_ROWS, :] = jnp.zeros(
        (FAR_ROWS - FEATURE_ROWS, qx.shape[1]), jnp.float32
    )
    return rows_ref[...].T.astype(jnp.bfloat16)


def evaluate_kernel(
    near_smem,
    near_ref,
    points_ref,
    slot_table_ref,
    slot_pot_ref,
    atoms_ref,
    moments_ref,
    first_ref,
    rate_ref,
    out_ref,
    far_rows,
    far_table,
    feat_rows,
    far_acc,
    y_rows,
    rho_rows,
    corr_ref,
):
    b = pl.program_id(0)
    near_count = near_ref.shape[2]
    pts = points_ref.shape[1]
    atoms = atoms_ref.shape[1]

    @pl.when(b == 0)
    def _():
        far_tables(atoms_ref, moments_ref, far_rows, far_table)
        y_rows[...] = jnp.zeros_like(y_rows)

    px, py, pz = points_ref[0:1, :], points_ref[1:2, :], points_ref[2:3, :]

    features = point_features(px, py, pz, feat_rows)
    far_acc[...] = jnp.zeros_like(far_acc)
    chunk = 256

    for c in range(FARC):
        base = c * chunk

        def table(q):
            return far_table[:, q * atoms + base : q * atoms + base + chunk]

        square = jnp.dot(features, table(0), preferred_element_type=jnp.float32)
        linear = jnp.dot(features, table(1), preferred_element_type=jnp.float32)
        quad = jnp.dot(features, table(2), preferred_element_type=jnp.float32)
        inv = lax.rsqrt(square)
        inv2 = inv * inv
        level = moments_ref[0:1, pl.ds(base, chunk)] * y_factor(0, 0)
        value = inv * (level + inv2 * (linear + inv2 * quad))
        far_acc[...] += value[:, 0:128] + value[:, 128:256]

    far_row = jnp.sum(far_acc[...].T, axis=0, keepdims=True)

    hot = (
        lax.broadcasted_iota(jnp.int32, (slot_table_ref.shape[1], near_count), 0) == near_ref[0]
    ).astype(jnp.float32)
    info = lax.dot_general(
        hot,
        slot_table_ref[...],
        (((0,), (1,)), ((), ())),
        precision=lax.Precision.HIGHEST,
        preferred_element_type=jnp.float32,
    )
    step = 8
    corr = jnp.zeros((step, pts), jnp.float32)
    for j in range(0, near_count, step):
        part = info[j : j + step, :]
        dx = px - part[:, 0:1]
        dy = py - part[:, 1:2]
        dz = pz - part[:, 2:3]
        square = dx * dx + dy * dy + dz * dz + 1.0
        inv = lax.rsqrt(square)
        rho_rows[j : j + step, :] = square * inv
        low = {}

        def emit(i, value):
            y_rows[pl.ds(j * YR + i, step, stride=YR), :] = value
            if i < 9:
                low[i] = value

        harmonic_rows(dx * inv, dy * inv, dz * inv, 6, emit)
        term = [part[:, 3 + i : 4 + i] * low[i] for i in range(9)]
        degree1 = term[1] + term[2] + term[3]
        degree2 = (term[4] + term[5]) + (term[6] + term[7]) + term[8]
        corr = corr + inv * (term[0] + inv * (degree1 + inv * degree2))
    corr_ref[...] = corr

    unroll = 32

    def pairs(g, total):
        for v in range(unroll):
            j = g * unroll + v
            coefs = slot_pot_ref[near_smem[b, j]]
            radial = radial_values(rho_rows[pl.ds(j, 1), :], first_ref, rate_ref)
            values = jnp.dot(coefs, radial, preferred_element_type=jnp.float32)
            rows = y_rows[pl.ds(pl.multiple_of(j * YR, YR), YR), :]
            total = total + values[0:YR] * rows
        return total

    total = lax.fori_loop(
        0, near_count // unroll, pairs, jnp.zeros((YR, pts), jnp.float32)
    )
    near_row = jnp.sum(total, axis=0, keepdims=True)
    out_ref[0] = near_row + far_row - jnp.sum(corr_ref[...], axis=0, keepdims=True)


def evaluate(points, near_slot, slot_table, slot_pot, atom_pos, moments, decay_rates):
    batches, near_count = near_slot.shape
    pts = points.shape[1] // batches
    atoms = atom_pos.shape[1]
    first, factor = radial_tables(decay_rates, pts)

    def whole(shape):
        return pl.BlockSpec(shape, lambda b, near: (0,) * len(shape))

    out = pl.pallas_call(
        evaluate_kernel,
        out_shape=jax.ShapeDtypeStruct((batches, 1, pts), jnp.float32),
        grid_spec=pltpu.PrefetchScalarGridSpec(
            num_scalar_prefetch=1,
            grid=(batches,),
            in_specs=[
                pl.BlockSpec((1, 1, near_count), lambda b, near: (b, 0, 0)),
                pl.BlockSpec((3, pts), lambda b, near: (0, b)),
                whole(slot_table.shape),
                whole(slot_pot.shape),
                whole(atom_pos.shape),
                whole(moments.shape),
                whole(first.shape),
                whole(factor.shape),
            ],
            out_specs=pl.BlockSpec((1, 1, pts), lambda b, near: (b, 0, 0)),
            scratch_shapes=[
                pltpu.VMEM((FAR_ROWS, 3 * atoms), jnp.float32),
                pltpu.VMEM((FAR_ROWS, 3 * atoms), jnp.bfloat16),
                pltpu.VMEM((FAR_ROWS, pts), jnp.float32),
                pltpu.VMEM((pts, 128), jnp.float32),
                pltpu.VMEM((near_count * YR, pts), jnp.float32),
                pltpu.VMEM((near_count, pts), jnp.float32),
                pltpu.VMEM((8, pts), jnp.float32),
            ],
        ),
        compiler_params=pltpu.CompilerParams(
            dimension_semantics=("arbitrary",), vmem_limit_bytes=40 << 20
        ),
        name="evaluate",
    )(
        near_slot,
        near_slot.reshape(batches, 1, near_count),
        points,
        slot_table,
        slot_pot,
        atom_pos,
        moments,
        first,
        factor,
    )
    return out.reshape(-1)


def entry_tables(lists_ref, mine_ref, codes_ref, plan_ref, held_ref):
    devices, listed = lists_ref.shape
    shape = (listed, listed)
    row = lax.broadcasted_iota(jnp.int32, shape, 0)
    column = lax.broadcasted_iota(jnp.int32, shape, 1)
    turned = lists_ref[...].astype(jnp.float32).T
    mine = mine_ref[...].astype(jnp.float32)
    slot = (row + 1).astype(jnp.float32)
    for q in range(devices):
        same = turned[:, q : q + 1] == mine
        held_ref[q : q + 1, :] = jnp.sum(jnp.where(same, slot, 0.0), axis=0, keepdims=True)
    held = held_ref[...]
    present = jnp.where(held > 0.0, 1.0, 0.0).astype(jnp.bfloat16)
    rank = jnp.dot(
        (column < row).astype(jnp.bfloat16), present, preferred_element_type=jnp.float32
    )
    rank = jnp.where(held > 0.0, rank, 4096.0)
    none = float(devices * listed)
    code = (row * listed).astype(jnp.float32) + held - (1.0 + none)
    for r in range(codes_ref.shape[0]):
        picked = jnp.sum(jnp.where(rank == float(r), code, 0.0), axis=0, keepdims=True)
        codes_ref[r : r + 1, :] = (picked + none).astype(jnp.int32)
    counts = lax.dot_general(
        present,
        jnp.ones(shape, jnp.bfloat16),
        (((0,), (0,)), ((), ())),
        preferred_element_type=jnp.float32,
    ).astype(jnp.int32)
    needed = lax.shift_right_logical(counts + (PER - 1), 2)
    ends = jnp.dot(
        (column <= row).astype(jnp.bfloat16),
        needed.astype(jnp.float32).astype(jnp.bfloat16),
        preferred_element_type=jnp.float32,
    ).astype(jnp.int32)
    starts = ends - needed
    total = ends[listed - 1 : listed, :]
    last = plan_ref.shape[0] - 1
    for m in range(last):
        block = column + m * listed
        inside = (block >= starts) & (block < ends)
        value = jnp.sum(
            jnp.where(inside, row * 4096 + (block - starts) * PER, 0), axis=0, keepdims=True
        )
        plan_ref[m : m + 1, :] = value + jnp.where(block[0:1, :] >= total, devices, 0)
    plan_ref[last : last + 1, :] = total


def point_blocks_kernel(
    points_ref,
    density_ref,
    slots_ref,
    places_ref,
    first_ref,
    rate_ref,
    table_ref,
    lists_ref,
    mine_ref,
    out_ref,
    codes_ref,
    plan_ref,
    four_ref,
    q_rows,
    held_ref,
    sorted_ref,
):
    listed = places_ref.shape[1]
    pts = first_ref.shape[1]
    blocks = points_ref.shape[1] // pts
    slot_rows = lax.broadcasted_iota(jnp.int32, (listed, pts), 0)
    lane = lax.broadcasted_iota(jnp.int32, (listed, pts), 1)
    earlier = (slot_rows < lane).astype(jnp.bfloat16)
    counts = jnp.zeros((listed, 1), jnp.float32)
    ranks, hots = [], []
    for g in range(blocks):
        at = pl.ds(g * pts, pts)
        same = slot_rows == slots_ref[:, at]
        hot = same.astype(jnp.float32)
        inside = jnp.dot(hot.astype(jnp.bfloat16), earlier, preferred_element_type=jnp.float32)
        ranks.append(jnp.sum(hot * (inside + counts), axis=0, keepdims=True))
        counts = counts + jnp.sum(hot, axis=1, keepdims=True)
    below = (lax.broadcasted_iota(jnp.int32, (listed, listed), 1) < lax.broadcasted_iota(
        jnp.int32, (listed, listed), 0
    )).astype(jnp.float32)
    counts_full = jnp.broadcast_to(counts, (listed, listed))
    starts_full = jnp.dot(
        below, counts_full, precision=lax.Precision.HIGHEST, preferred_element_type=jnp.float32
    )
    starts = starts_full[:, 0:1]
    packed = starts_full * 4096.0 + counts_full
    rows64 = lax.broadcasted_iota(jnp.int32, (4 * blocks, pts), 0) // 4
    sorted_rows = jnp.zeros((4 * blocks, pts), jnp.float32)
    moments = jnp.zeros((16, listed), jnp.float32)
    q_rows[...] = jnp.zeros_like(q_rows)
    for g in range(blocks):
        at = pl.ds(g * pts, pts)
        hot = (slot_rows == slots_ref[:, at]).astype(jnp.float32)
        place = ranks[g] + jnp.sum(hot * starts, axis=0, keepdims=True)
        place = place.astype(jnp.int32)
        atom = jnp.dot(
            places_ref[...], hot, precision=lax.Precision.HIGHEST, preferred_element_type=jnp.float32
        )
        dx = points_ref[0:1, at] - atom[0:1]
        dy = points_ref[1:2, at] - atom[1:2]
        dz = points_ref[2:3, at] - atom[2:3]
        weight = density_ref[:, at]
        for r in range(2):
            for c, value in enumerate((dx, dy, dz, weight)):
                four_ref[4 * r + c : 4 * r + c + 1, :] = value
        tiled = jnp.concatenate([four_ref[...]] * (blocks // 2), axis=0)
        masked = jnp.where(rows64 == place // pts, tiled, 0.0)
        target = (slot_rows == place % pts).astype(jnp.bfloat16)
        for piece in split3(masked):
            sorted_rows = sorted_rows + lax.dot_general(
                piece.astype(jnp.bfloat16),
                target,
                (((1,), (1,)), ((), ())),
                preferred_element_type=jnp.float32,
            )
        square = dx * dx + dy * dy + dz * dz + 1.0
        inv = lax.rsqrt(square)
        rho = square * inv
        radial = radial_values(rho, first_ref, rate_ref, jnp.float32)
        levels = jnp.dot(
            table_ref[...], radial, precision=lax.Precision.HIGHEST, preferred_element_type=jnp.float32
        )

        def emit(i, value):
            degree = (0, 1, 1, 1, 2, 2, 2, 2, 2)[i]
            q_rows[i : i + 1, :] = value * weight * levels[degree : degree + 1]

        harmonic_rows(dx * inv, dy * inv, dz * inv, 2, emit)
        moments = moments + lax.dot_general(
            q_rows[...],
            hot,
            (((1,), (1,)), ((), ())),
            precision=lax.Precision.HIGHEST,
            preferred_element_type=jnp.float32,
        )
    sorted_ref[0 : 4 * blocks, :] = sorted_rows
    sorted_ref[4 * blocks : 4 * blocks + 1, :] = packed.T[0:1, :]
    sorted_ref[4 * blocks + 1 : 4 * blocks + 10, :] = moments[0:9]
    sorted_ref[4 * blocks + 10 : 4 * blocks + 12, :] = jnp.zeros((2, listed), jnp.float32)
    for m in range(blocks + 3):
        out_ref[m] = sorted_ref[4 * m : 4 * m + 4, :]
    entry_tables(lists_ref, mine_ref, codes_ref, plan_ref, held_ref)


def point_blocks(points, density, slots, places, tables, moment_table, lists, my_list):
    count = points.shape[1]
    devices, listed = lists.shape
    pts = tables[0].shape[1]
    tiles = count // pts + 3
    plans = (listed * (devices // PER) + GROUP + listed - 1) // listed + 1
    return pl.pallas_call(
        point_blocks_kernel,
        out_shape=(
            jax.ShapeDtypeStruct((tiles, 4, pts), jnp.float32),
            jax.ShapeDtypeStruct((devices + 8, listed), jnp.int32),
            jax.ShapeDtypeStruct((plans, listed), jnp.int32),
        ),
        scratch_shapes=[
            pltpu.VMEM((8, pts), jnp.float32),
            pltpu.VMEM((16, pts), jnp.float32),
            pltpu.VMEM((devices, listed), jnp.float32),
            pltpu.VMEM((4 * tiles, pts), jnp.float32),
        ],
        compiler_params=pltpu.CompilerParams(vmem_limit_bytes=40 << 20),
        name="point_blocks",
    )(
        points,
        density.reshape(1, count),
        slots.reshape(1, count),
        places,
        *tables,
        moment_table,
        lists,
        my_list.reshape(1, listed),
    )


MESH = pl.DeviceIdType.MESH
SIDE = 4


def gather_kernel(cuts, mine_ref, all_ref, local_sem, send_sems, recv_sems, swap_send, swap_recv):
    row, column = lax.axis_index("sx"), lax.axis_index("sy")
    core = lax.rem(row, 2)
    here = {"z": row // 2, "y": column // SIDE, "x": lax.rem(column, SIDE)}

    def device(place, on_core):
        return (place["z"] * 2 + on_core, place["y"] * SIDE + place["x"])

    def moved(axis, offset):
        place = dict(here)
        place[axis] = lax.rem(here[axis] + offset, SIDE)
        return place

    def region(place, whole, part):
        index = [pl.ds(0, SIDE) if a in whole else place[a] for a in ("z", "y", "x")]
        return all_ref.at[index[0], core, index[1], index[2], part]

    barrier = pltpu.get_barrier_semaphore()
    for axis in ("z", "y", "x"):
        for offset in range(1, SIDE):
            pl.semaphore_signal(
                barrier, inc=1, device_id=device(moved(axis, offset), core), device_id_type=MESH
            )
    pl.semaphore_signal(barrier, inc=1, device_id=device(here, 1 - core), device_id_type=MESH)
    pl.semaphore_wait(barrier, 3 * (SIDE - 1) + 1)

    local = pltpu.make_async_copy(mine_ref, region(here, "", pl.ds(0, cuts[-1])), local_sem)
    local.start()
    orders = ("xyz", "yzx", "zxy")
    parts = [pl.ds(cuts[c], cuts[c + 1] - cuts[c]) for c in range(3)]
    hops = {}
    swaps = []

    def send(c, phase):
        axis = orders[c][phase]
        whole = orders[c][:phase]
        for offset in range(1, SIDE):
            place = region(here, whole, parts[c])
            copy = pltpu.make_async_remote_copy(
                src_ref=mine_ref.at[parts[c]] if phase == 0 else place,
                dst_ref=place,
                send_sem=send_sems.at[c, phase, offset],
                recv_sem=recv_sems.at[c, phase, offset],
                device_id=device(moved(axis, offset), core),
                device_id_type=MESH,
            )
            copy.start()
            hops[c, phase, offset] = copy

    def swap(c, slot, place):
        area = region(place, orders[c][:2], parts[c])
        copy = pltpu.make_async_remote_copy(
            src_ref=area,
            dst_ref=area,
            send_sem=swap_send.at[c, slot],
            recv_sem=swap_recv.at[c, slot],
            device_id=device(here, 1 - core),
            device_id_type=MESH,
        )
        copy.start()
        swaps.append(copy)

    for c in range(3):
        send(c, 0)
    local.wait()
    for phase in (1, 2):
        for c in range(3):
            for offset in range(1, SIDE):
                hops[c, phase - 1, offset].wait_recv()
            send(c, phase)
    for c in range(3):
        swap(c, 0, here)
    for offset in range(1, SIDE):
        for c in range(3):
            hops[c, 2, offset].wait_recv()
            swap(c, offset, moved(orders[c][2], SIDE - offset))
    for copy in hops.values():
        copy.wait_send()
    for copy in swaps:
        copy.wait()


def gather_blocks(mine):
    blocks = mine.shape[0]
    cuts = (0, blocks // 3, 2 * blocks // 3, blocks)
    return pl.pallas_call(
        functools.partial(gather_kernel, cuts),
        out_shape=jax.ShapeDtypeStruct((SIDE, 2, SIDE, SIDE) + mine.shape, mine.dtype),
        in_specs=[pl.BlockSpec(memory_space=pl.ANY)],
        out_specs=pl.BlockSpec(memory_space=pl.ANY),
        scratch_shapes=[
            pltpu.SemaphoreType.DMA,
            pltpu.SemaphoreType.DMA((3, 3, SIDE)),
            pltpu.SemaphoreType.DMA((3, 3, SIDE)),
            pltpu.SemaphoreType.DMA((3, SIDE)),
            pltpu.SemaphoreType.DMA((3, SIDE)),
        ],
        compiler_params=pltpu.CompilerParams(collective_id=0, has_side_effects=True),
        name="gather_blocks",
    )(mine)


CHUNK = 32
PER = 4
LONG = 64
GROUP = 32


def project_kernel(
    lists,
    plan_ref,
    codes_ref,
    words_ref,
    runs_ref,
    blocks_ref,
    first_ref,
    rate_ref,
    green_ref,
    pot_ref,
    buffer,
    owner_ref,
    extra_ref,
    extra_code,
    extra_owner,
    y_rows,
    rho_rows,
    coefs_ref,
):
    listed = codes_ref.shape[1]
    pts = first_ref.shape[1]
    coefs_ref[...] = jnp.zeros_like(coefs_ref)
    y_rows[...] = jnp.zeros_like(y_rows)
    buffer[...] = jnp.zeros_like(buffer)
    for f in range(2 * GROUP):
        owner_ref[f] = 0
    extra_ref[0] = 0
    lane = lax.broadcasted_iota(jnp.int32, (4, pts), 1)
    held = blocks_ref.shape[0] // lists

    def window(tile, off, left):
        value = jnp.where(lane >= off, blocks_ref[tile], blocks_ref[tile + 1])
        return pltpu.roll(value, lax.bitwise_and(left + 128 - off, 127), 1)

    def collect(g, half):
        owners, values, codes = [], [], []
        marks = jnp.int32(0)
        for f in range(GROUP):
            plan = plan_ref[g * GROUP + f]
            j = lax.shift_right_logical(plan, 12)
            r = lax.bitwise_and(plan, 4095)
            owners.append(j)
            value = jnp.zeros((4, pts), jnp.float32)
            for v in range(PER):
                code = codes_ref[r + v, j]
                word = words_ref[code]
                left = v * CHUNK
                moved = window(
                    lax.shift_right_logical(word, 16),
                    lax.bitwise_and(lax.shift_right_logical(word, 8), 127),
                    left,
                )
                right = left + lax.bitwise_and(word, 63)
                fresh = jnp.where(lane < right, moved, 0.0)
                value = fresh if v == 0 else jnp.where(lane < left, value, fresh)
                marks = lax.bitwise_or(marks, word)
                codes.append(code)
            values.append(value)
        for f in range(GROUP):
            row = half * GROUP + f
            buffer[pl.ds(row * 4, 4), :] = values[f]
            owner_ref[row] = owners[f]
        return marks, codes, owners

    def note(fresh, marks, codes, owners):
        @pl.when(fresh & (lax.bitwise_and(marks, LONG) > 0))
        def _():
            for n, code in enumerate(codes):

                @pl.when(lax.bitwise_and(words_ref[code], LONG) > 0)
                def _():
                    at = extra_ref[0]
                    extra_code[at] = code
                    extra_owner[at] = owners[n // PER]
                    extra_ref[0] = at + 1

    def flush(half):
        def component(c):
            return buffer[pl.ds(half * (4 * GROUP) + c, GROUP, stride=4), :]

        dx, dy, dz, weight = (component(c) for c in range(4))
        square = dx * dx + dy * dy + dz * dz + 1.0
        inv = lax.rsqrt(square)
        rho_rows[...] = square * inv

        def emit(i, value):
            y_rows[pl.ds(i, GROUP, stride=HP), :] = value * weight

        harmonic_rows(dx * inv, dy * inv, dz * inv, 6, emit)
        sums = []
        for f in range(GROUP):
            radial = radial_values(rho_rows[f : f + 1, :], first_ref, rate_ref)
            rows = y_rows[f * HP : (f + 1) * HP, :].astype(jnp.bfloat16)
            sums.append(
                lax.dot_general(
                    rows, radial, (((1,), (1,)), ((), ())), preferred_element_type=jnp.float32
                )
            )
        for f in range(GROUP):
            at = pl.ds(pl.multiple_of(owner_ref[half * GROUP + f] * YR, 8), YR)
            coefs_ref[at, :] = coefs_ref[at, :] + sums[f][0:YR]

    groups = (plan_ref[plan_ref.shape[0] - first_ref.shape[1]] + (GROUP - 1)) // GROUP
    note(groups > 0, *collect(0, 0))

    @pl.loop(0, groups)
    def _(g):
        half = lax.bitwise_and(g, 1)
        later = jnp.minimum(g + 1, groups - 1)
        found = collect(later, 1 - half)
        flush(half)
        note(later > g, *found)

    @pl.when(extra_ref[0] > 0)
    def _():
        buffer[...] = jnp.zeros_like(buffer)
        extra_ref[1] = 0

        @pl.loop(0, extra_ref[0])
        def _(n):
            code = extra_code[n]
            device = lax.shift_right_logical(code, 7)
            run = runs_ref[device, lax.bitwise_and(code, 127)]
            start = lax.shift_right_logical(run, 12) + CHUNK
            length = lax.bitwise_and(run, 4095) - CHUNK

            @pl.loop(0, lax.shift_right_logical(length + (pts - 1), 7))
            def _(c):
                row = extra_ref[1]
                place = start + c * pts
                tile = device * held + lax.shift_right_logical(place, 7)
                moved = window(tile, lax.bitwise_and(place, 127), 0)
                buffer[pl.ds(row * 4, 4), :] = jnp.where(lane < length - c * pts, moved, 0.0)
                owner_ref[row] = extra_owner[n]
                extra_ref[1] = row + 1

                @pl.when(row + 1 == GROUP)
                def _():
                    flush(0)
                    buffer[...] = jnp.zeros_like(buffer)
                    extra_ref[1] = 0

        flush(0)

    for l in range(7):
        top = green_ref[l]
        high = top.astype(jnp.bfloat16)
        low = (top - high.astype(jnp.float32)).astype(jnp.bfloat16)
        half = jnp.concatenate([high, low], axis=1)
        table = jnp.concatenate([half, half], axis=0)
        for i in range(l * l, (l + 1) * (l + 1)):
            at = pl.ds(i, listed, stride=YR)
            rows = coefs_ref[at, :]
            big = rows.astype(jnp.bfloat16)
            small = (rows - big.astype(jnp.float32)).astype(jnp.bfloat16)
            both = jnp.dot(
                jnp.concatenate([big, small], axis=1), table, preferred_element_type=jnp.float32
            )
            coefs_ref[at, :] = both[:, 0:128] + both[:, 128:256]

    @pl.loop(0, listed // 8)
    def _(g):
        for v in range(8):
            j = g * 8 + v
            rows = coefs_ref[pl.ds(pl.multiple_of(j * YR, 8), YR), :]
            pot_ref[j] = jnp.concatenate(
                [rows, jnp.zeros((HP - YR, rows.shape[1]), jnp.float32)], axis=0
            ).astype(jnp.bfloat16)


def project(plan, codes, words, runs, blocks, tables, green):
    lists, listed = runs.shape
    pts = tables[0].shape[1]
    smem = pl.BlockSpec(memory_space=pltpu.SMEM)
    vmem = pl.BlockSpec(memory_space=pltpu.VMEM)
    return pl.pallas_call(
        functools.partial(project_kernel, lists),
        out_shape=jax.ShapeDtypeStruct((listed, HP, NRAD), jnp.bfloat16),
        in_specs=[smem] * 4 + [vmem] * 4,
        out_specs=vmem,
        scratch_shapes=[
            pltpu.VMEM((2 * GROUP * 4, pts), jnp.float32),
            pltpu.SMEM((2 * GROUP,), jnp.int32),
            pltpu.SMEM((2,), jnp.int32),
            pltpu.SMEM((codes.size,), jnp.int32),
            pltpu.SMEM((codes.size,), jnp.int32),
            pltpu.VMEM((GROUP * HP, pts), jnp.float32),
            pltpu.VMEM((GROUP, pts), jnp.float32),
            pltpu.VMEM((YR * listed, NRAD), jnp.float32),
        ],
        compiler_params=pltpu.CompilerParams(vmem_limit_bytes=40 << 20),
        name="project",
    )(plan.reshape(-1), codes, words.reshape(-1), runs, blocks, *tables, green)


def scatter_kernel(
    lists_ref, blocks_ref, atoms_ref, mine_ref, places_ref, out_ref, info_ref, words_ref, runs_ref, acc_ref
):
    devices, listed = atoms_ref.shape
    held = blocks_ref.shape[0] // lists_ref
    wide = 256
    acc_ref[...] = jnp.zeros_like(acc_ref)
    column = lax.broadcasted_iota(jnp.int32, (wide, listed), 0)
    groups = acc_ref.shape[0] // 32
    steps = 8

    @pl.loop(0, devices // steps)
    def _(g):
        total = acc_ref[...]
        packed = []
        for v in range(0, steps, 2):
            targets, parts = [], []
            for q in (g * steps + v, g * steps + v + 1):
                ids = atoms_ref[pl.ds(q, 1), :]
                targets.append(
                    (column == lax.bitwise_and(ids, wide - 1)).astype(jnp.bfloat16)
                )
                group = lax.shift_right_logical(ids, 8)
                tiles = [blocks_ref[(q + 1) * held - 3 + m] for m in range(3)]
                packed.append(tiles[0][0:1])
                mom = jnp.concatenate(tiles + [jnp.zeros((4, listed), jnp.float32)], axis=0)
                top = mom.astype(jnp.bfloat16).astype(jnp.float32)
                both = [
                    jnp.where(group == h, half, 0.0)
                    for h in range(groups)
                    for half in (top, mom - top)
                ]
                parts.append(jnp.concatenate(both, axis=0).astype(jnp.bfloat16))
            total = total + lax.dot_general(
                jnp.concatenate(parts, axis=1),
                jnp.concatenate(targets, axis=1),
                (((1,), (1,)), ((), ())),
                preferred_element_type=jnp.float32,
            )
        acc_ref[...] = total
        at = pl.ds(pl.multiple_of(g * steps, steps), steps)
        run = jnp.concatenate(packed, axis=0).astype(jnp.int32)
        runs_ref[at, :] = run
        start, length = lax.shift_right_logical(run, 12), lax.bitwise_and(run, 4095)
        device = g * steps + lax.broadcasted_iota(jnp.int32, (steps, listed), 0)
        tile = device * held + lax.shift_right_logical(start, 7)
        word = tile * 65536 + lax.bitwise_and(start, 127) * 256 + jnp.minimum(length, CHUNK)
        words_ref[at, :] = word + jnp.where(length > CHUNK, LONG, 0)

    words_ref[devices : devices + 8, :] = jnp.zeros((8, listed), jnp.int32)
    mine = jnp.zeros((16, listed), jnp.float32)
    for h in range(groups):
        both = acc_ref[h * 32 : h * 32 + 16, :] + acc_ref[h * 32 + 16 : h * 32 + 32, :]
        out_ref[:, h * wide : (h + 1) * wide] = both[1:10]
        mine = mine + jnp.dot(
            both,
            (column + h * wide == mine_ref[...]).astype(jnp.float32),
            precision=lax.Precision.HIGHEST,
            preferred_element_type=jnp.float32,
        )
    info_ref[...] = jnp.zeros_like(info_ref)
    info_ref[0:3, :] = places_ref[...]
    info_ref[3:12, :] = mine[1:10]


def scatter_moments(blocks, lists, my_list, places, atoms):
    devices, listed = lists.shape
    return pl.pallas_call(
        functools.partial(scatter_kernel, devices),
        out_shape=(
            jax.ShapeDtypeStruct((9, atoms), jnp.float32),
            jax.ShapeDtypeStruct((16, listed), jnp.float32),
            jax.ShapeDtypeStruct((devices + 8, listed), jnp.int32),
            jax.ShapeDtypeStruct((devices, listed), jnp.int32),
        ),
        scratch_shapes=[pltpu.VMEM((atoms // 256 * 32, 256), jnp.float32)],
        compiler_params=pltpu.CompilerParams(vmem_limit_bytes=40 << 20),
        name="scatter_moments",
    )(blocks, lists, my_list.reshape(1, listed), places)


def per_device(
    grid_points,
    weighted_density,
    point_slot,
    near_slot,
    slot_atom,
    atom_pos,
    decay_rates,
    green,
    moment_table,
):
    count_y = lax.axis_size("sy")
    devices = lax.axis_size("sx") * count_y
    myself = lax.axis_index("sx") * count_y + lax.axis_index("sy")
    lists = slot_atom.reshape(devices, -1)
    my_list = lists[myself]
    atoms = atom_pos.shape[1]
    pts = grid_points.shape[1] // near_slot.shape[0]
    tables = radial_tables(decay_rates, pts)
    places = atom_pos[:, my_list]
    mine, codes, plan = point_blocks(
        grid_points, weighted_density, point_slot, places, tables, moment_table, lists, my_list
    )
    gathered = gather_blocks(mine)
    blocks = gathered.reshape((devices * mine.shape[0],) + mine.shape[1:])
    moments, slot_table, words, runs = scatter_moments(blocks, lists, my_list, places, atoms)
    slot_pot = project(plan, codes, words, runs, blocks, tables, green)
    return evaluate(
        grid_points, near_slot, slot_table, slot_pot, atom_pos, moments, decay_rates
    )


def solution(mesh):
    return jax.shard_map(
        per_device,
        mesh=mesh,
        in_specs=(
            P(None, ("sx", "sy")),
            P(("sx", "sy")),
            P(("sx", "sy")),
            P(("sx", "sy"), None),
            P(),
            P(),
            P(),
            P(),
            P(),
        ),
        out_specs=P(("sx", "sy")),
        check_vma=False,
    )
```

```python
import functools
import math

import jax
import jax.numpy as jnp
from jax import lax
from jax.experimental import pallas as pl
from jax.experimental.pallas import tpu as pltpu
from jax.sharding import PartitionSpec as P

HARM = 49
NRAD = 128


HP = 64
YR = 56


def y_factor(l, m):
    factor = math.sqrt(
        (2 * l + 1) / (4 * math.pi) * math.factorial(l - m) / math.factorial(l + m)
    )
    return factor if m == 0 else factor * math.sqrt(2.0)


def harmonic_rows(x, y, z, top, emit):
    square = x * x + y * y + z * z
    cos_m, sin_m = None, None
    for m in range(top + 1):
        if m == 1:
            cos_m, sin_m = x, y
        elif m > 1:
            cos_m, sin_m = cos_m * x - sin_m * y, cos_m * y + sin_m * x
        double = float(math.prod(range(1, 2 * m, 2)))
        ladder = {}
        for l in range(m, top + 1):
            if l == m + 1:
                ladder[l] = z * float(2 * m + 1)
            elif l == m + 2:
                ladder[l] = z * ladder[l - 1] * ((2 * l - 1) / 2) - square * ((l + m - 1) / 2)
            elif l > m + 2:
                ladder[l] = z * ladder[l - 1] * ((2 * l - 1) / (l - m)) - square * ladder[l - 2] * (
                    (l + m - 1) / (l - m)
                )
            scale = y_factor(l, m) * double
            part = ladder[l] * scale if l > m else scale
            if m == 0:
                emit(l * l, part if l > m else jnp.full_like(x, part))
            else:
                emit(l * l + 2 * m - 1, cos_m * part)
                emit(l * l + 2 * m, sin_m * part)


def split3(value):
    high = value.astype(jnp.bfloat16).astype(jnp.float32)
    rest = value - high
    middle = rest.astype(jnp.bfloat16).astype(jnp.float32)
    return high, middle, rest - middle


SPACING = 27.0 / (NRAD - 1)
SHELL_ROWS = 16


def radial_values(rho, rate_ref, dtype=jnp.bfloat16):
    rows, pts = SHELL_ROWS, rho.shape[1]
    shell = lax.broadcasted_iota(jnp.int32, (rows, pts), 0).astype(jnp.float32)
    base = jnp.broadcast_to(rho, (rows, pts)) - (1.0 + SPACING * shell)
    pieces = []
    for k in range(0, NRAD, rows):
        e = base - (SPACING * k)
        power = (e * e) * rate_ref[k : k + rows, :]
        pieces.append(jnp.exp2(power.astype(dtype)))
    return jnp.concatenate(pieces, axis=0)


FARC = 8
FEATURES = 9
FEATURE_ROWS = 6 * FEATURES + 3
FAR_ROWS = 64


def far_tables(atoms_ref, moments_ref, rows_ref, table_ref):
    atoms = atoms_ref.shape[1]
    ax = atoms_ref[0:1, :] - 8.0
    ay = atoms_ref[1:2, :] - 8.0
    az = atoms_ref[2:3, :] - 8.0
    mom = [moments_ref[i : i + 1, :] for i in range(9)]
    one, nil = jnp.ones_like(ax), jnp.zeros_like(ax)
    n10, n11 = y_factor(1, 0), y_factor(1, 1)
    vx, vy, vz = mom[2] * n11, mom[3] * n11, mom[1] * n10
    f20, f21, f22 = y_factor(2, 0), 3.0 * y_factor(2, 1), 3.0 * y_factor(2, 2)
    qzz = mom[4] * f20
    qxx = mom[7] * f22 - qzz * 0.5
    qyy = -mom[7] * f22 - qzz * 0.5
    qxz, qyz, qxy = mom[5] * f21, mom[6] * f21, mom[8] * (2.0 * f22)
    gx = -(2.0 * qxx * ax + qxy * ay + qxz * az)
    gy = -(qxy * ax + 2.0 * qyy * ay + qyz * az)
    gz = -(qxz * ax + qyz * ay + 2.0 * qzz * az)
    const = -0.5 * (gx * ax + gy * ay + gz * az)
    norm = ax * ax + ay * ay + az * az + 1.0
    plans = [
        ([-2.0 * ax, -2.0 * ay, -2.0 * az, one, one, one, nil, nil, nil], norm),
        ([vx, vy, vz, nil, nil, nil, nil, nil, nil], -(vx * ax + vy * ay + vz * az)),
        ([gx, gy, gz, qxx, qyy, qzz, qxy, qxz, qyz], const),
    ]
    for q, (coefs, fixed) in enumerate(plans):
        columns = pl.ds(q * atoms, atoms)
        for f, coef in enumerate(coefs):
            high, middle, low = split3(coef)
            for r, row in enumerate((high, middle, high, low, high, middle)):
                rows_ref[6 * f + r : 6 * f + r + 1, columns] = row
        for r, row in enumerate(split3(fixed)):
            rows_ref[6 * FEATURES + r : 6 * FEATURES + r + 1, columns] = row
        rows_ref[FEATURE_ROWS:FAR_ROWS, columns] = jnp.zeros(
            (FAR_ROWS - FEATURE_ROWS, atoms), jnp.float32
        )
    table_ref[...] = rows_ref[...].astype(jnp.bfloat16)


def point_features(px, py, pz, rows_ref):
    qx, qy, qz = px - 8.0, py - 8.0, pz - 8.0
    values = [qx, qy, qz, qx * qx, qy * qy, qz * qz, qx * qy, qx * qz, qy * qz]
    for f, value in enumerate(values):
        high, middle, low = split3(value)
        for r, row in enumerate((high, high, middle, high, low, middle)):
            rows_ref[6 * f + r : 6 * f + r + 1, :] = row
    rows_ref[6 * FEATURES : FEATURE_ROWS, :] = jnp.ones((3, qx.shape[1]), jnp.float32)
    rows_ref[FEATURE_ROWS:FAR_ROWS, :] = jnp.zeros(
        (FAR_ROWS - FEATURE_ROWS, qx.shape[1]), jnp.float32
    )
    return rows_ref[...].T.astype(jnp.bfloat16)


def evaluate_kernel(
    near_smem,
    near_ref,
    points_ref,
    slot_table_ref,
    slot_pot_ref,
    atoms_ref,
    moments_ref,
    rate_ref,
    out_ref,
    far_rows,
    far_table,
    feat_rows,
    far_acc,
    y_rows,
    rho_rows,
    corr_ref,
):
    b = pl.program_id(0)
    near_count = near_ref.shape[2]
    pts = points_ref.shape[1]
    atoms = atoms_ref.shape[1]

    @pl.when(b == 0)
    def _():
        far_tables(atoms_ref, moments_ref, far_rows, far_table)
        y_rows[...] = jnp.zeros_like(y_rows)

    px, py, pz = points_ref[0:1, :], points_ref[1:2, :], points_ref[2:3, :]

    features = point_features(px, py, pz, feat_rows)
    far_acc[...] = jnp.zeros_like(far_acc)
    chunk = 256

    for c in range(FARC):
        base = c * chunk

        def table(q):
            return far_table[:, q * atoms + base : q * atoms + base + chunk]

        square = jnp.dot(features, table(0), preferred_element_type=jnp.float32)
        linear = jnp.dot(features, table(1), preferred_element_type=jnp.float32)
        quad = jnp.dot(features, table(2), preferred_element_type=jnp.float32)
        inv = lax.rsqrt(square)
        inv2 = inv * inv
        level = moments_ref[0:1, pl.ds(base, chunk)] * y_factor(0, 0)
        value = inv * (level + inv2 * (linear + inv2 * quad))
        far_acc[...] += value[:, 0:128] + value[:, 128:256]

    far_row = jnp.sum(far_acc[...].T, axis=0, keepdims=True)

    hot = (
        lax.broadcasted_iota(jnp.int32, (slot_table_ref.shape[1], near_count), 0) == near_ref[0]
    ).astype(jnp.float32)
    info = lax.dot_general(
        hot,
        slot_table_ref[...],
        (((0,), (1,)), ((), ())),
        precision=lax.Precision.HIGHEST,
        preferred_element_type=jnp.float32,
    )
    step = 8
    corr = jnp.zeros((step, pts), jnp.float32)
    for j in range(0, near_count, step):
        part = info[j : j + step, :]
        dx = px - part[:, 0:1]
        dy = py - part[:, 1:2]
        dz = pz - part[:, 2:3]
        square = dx * dx + dy * dy + dz * dz + 1.0
        inv = lax.rsqrt(square)
        rho_rows[j : j + step, :] = square * inv
        low = {}

        def emit(i, value):
            y_rows[pl.ds(j * YR + i, step, stride=YR), :] = value
            if i < 9:
                low[i] = value

        harmonic_rows(dx * inv, dy * inv, dz * inv, 6, emit)
        term = [part[:, 3 + i : 4 + i] * low[i] for i in range(9)]
        degree1 = term[1] + term[2] + term[3]
        degree2 = (term[4] + term[5]) + (term[6] + term[7]) + term[8]
        corr = corr + inv * (term[0] + inv * (degree1 + inv * degree2))
    corr_ref[...] = corr

    unroll = 32

    def pairs(g, total):
        for v in range(unroll):
            j = g * unroll + v
            coefs = slot_pot_ref[near_smem[b, j]]
            radial = radial_values(rho_rows[pl.ds(j, 1), :], rate_ref)
            values = jnp.dot(coefs, radial, preferred_element_type=jnp.float32)
            rows = y_rows[pl.ds(pl.multiple_of(j * YR, YR), YR), :]
            total = total + values[0:YR] * rows
        return total

    total = lax.fori_loop(
        0, near_count // unroll, pairs, jnp.zeros((YR, pts), jnp.float32)
    )
    near_row = jnp.sum(total, axis=0, keepdims=True)
    out_ref[0] = near_row + far_row - jnp.sum(corr_ref[...], axis=0, keepdims=True)


def evaluate(points, near_slot, slot_table, slot_pot, atom_pos, moments, rate):
    batches, near_count = near_slot.shape
    pts = points.shape[1] // batches
    atoms = atom_pos.shape[1]
    def whole(shape):
        return pl.BlockSpec(shape, lambda b, near: (0,) * len(shape))

    out = pl.pallas_call(
        evaluate_kernel,
        out_shape=jax.ShapeDtypeStruct((batches, 1, pts), jnp.float32),
        grid_spec=pltpu.PrefetchScalarGridSpec(
            num_scalar_prefetch=1,
            grid=(batches,),
            in_specs=[
                pl.BlockSpec((1, 1, near_count), lambda b, near: (b, 0, 0)),
                pl.BlockSpec((3, pts), lambda b, near: (0, b)),
                whole(slot_table.shape),
                whole(slot_pot.shape),
                whole(atom_pos.shape),
                whole(moments.shape),
                whole(rate.shape),
            ],
            out_specs=pl.BlockSpec((1, 1, pts), lambda b, near: (b, 0, 0)),
            scratch_shapes=[
                pltpu.VMEM((FAR_ROWS, 3 * atoms), jnp.float32),
                pltpu.VMEM((FAR_ROWS, 3 * atoms), jnp.bfloat16),
                pltpu.VMEM((FAR_ROWS, pts), jnp.float32),
                pltpu.VMEM((pts, 128), jnp.float32),
                pltpu.VMEM(((near_count + 1) * YR, pts), jnp.float32),
                pltpu.VMEM((near_count, pts), jnp.float32),
                pltpu.VMEM((8, pts), jnp.float32),
            ],
        ),
        compiler_params=pltpu.CompilerParams(
            dimension_semantics=("arbitrary",), vmem_limit_bytes=40 << 20
        ),
        name="evaluate",
    )(
        near_slot,
        near_slot.reshape(batches, 1, near_count),
        points,
        slot_table,
        slot_pot,
        atom_pos,
        moments,
        rate,
    )
    return out.reshape(-1)


def entry_tables(lists_ref, mine, codes_ref, plan_ref, held_ref):
    devices, listed = lists_ref.shape
    shape = (listed, listed)
    row = lax.broadcasted_iota(jnp.int32, shape, 0)
    column = lax.broadcasted_iota(jnp.int32, shape, 1)
    turned = lists_ref[...].astype(jnp.float32).T
    mine = mine.astype(jnp.float32)
    slot = (row + 1).astype(jnp.float32)
    for q in range(devices):
        same = turned[:, q : q + 1] == mine
        held_ref[q : q + 1, :] = jnp.sum(jnp.where(same, slot, 0.0), axis=0, keepdims=True)
    held = held_ref[...]
    present = jnp.where(held > 0.0, 1.0, 0.0).astype(jnp.bfloat16)
    rank = jnp.dot(
        (column < row).astype(jnp.bfloat16), present, preferred_element_type=jnp.float32
    )
    rank = jnp.where(held > 0.0, rank, 4096.0)
    none = float(devices * listed)
    code = (row * listed).astype(jnp.float32) + held - (1.0 + none)
    for r in range(codes_ref.shape[0]):
        picked = jnp.sum(jnp.where(rank == float(r), code, 0.0), axis=0, keepdims=True)
        codes_ref[r : r + 1, :] = (picked + none).astype(jnp.int32)
    counts = lax.dot_general(
        present,
        jnp.ones(shape, jnp.bfloat16),
        (((0,), (0,)), ((), ())),
        preferred_element_type=jnp.float32,
    ).astype(jnp.int32)
    needed = lax.shift_right_logical(counts + (PER - 1), 2)
    ends = jnp.dot(
        (column <= row).astype(jnp.bfloat16),
        needed.astype(jnp.float32).astype(jnp.bfloat16),
        preferred_element_type=jnp.float32,
    ).astype(jnp.int32)
    starts = ends - needed
    total = ends[listed - 1 : listed, :]
    last = plan_ref.shape[0] - 1
    for m in range(last):
        block = column + m * listed
        inside = (block >= starts) & (block < ends)
        value = jnp.sum(
            jnp.where(inside, row * 4096 + (block - starts) * PER, 0), axis=0, keepdims=True
        )
        plan_ref[m : m + 1, :] = value + jnp.where(block[0:1, :] >= total, devices, 0)
    plan_ref[last : last + 1, :] = total


def own_row(rows_ref):
    me = lax.axis_index("sx") * lax.axis_size("sy") + lax.axis_index("sy")
    return rows_ref[pl.ds(me, 1), :]


def point_blocks_kernel(
    points_from,
    density_from,
    slots_from,
    table_from,
    lists_from,
    atoms_from,
    decay_from,
    out_ref,
    codes_ref,
    plan_ref,
    places_ref,
    rate_ref,
    points_ref,
    density_ref,
    slots_ref,
    table_ref,
    lists_ref,
    atoms_ref,
    decay_ref,
    sems,
    four_ref,
    q_rows,
    held_ref,
    sorted_ref,
):
    wanted = (
        (lists_from, lists_ref),
        (atoms_from, atoms_ref),
        (slots_from, slots_ref),
        (points_from, points_ref),
        (density_from, density_ref),
        (table_from, table_ref),
        (decay_from, decay_ref),
    )
    copies = [
        pltpu.make_async_copy(source, target, sems.at[n])
        for n, (source, target) in enumerate(wanted)
    ]
    for copy in copies:
        copy.start()
    for copy in copies:
        copy.wait()
    listed = places_ref.shape[1]
    pts = rate_ref.shape[1]
    factor = decay_ref[...] * (-math.log2(math.e) / SPACING**2)
    rate_ref[...] = jnp.broadcast_to(factor, (pts, factor.shape[1])).T
    mine = own_row(lists_ref)
    wide = 256
    atom_row = lax.broadcasted_iota(jnp.int32, (wide, listed), 0)
    places = jnp.zeros(places_ref.shape, jnp.float32)
    for h in range(0, atoms_ref.shape[1], wide):
        places = places + jnp.dot(
            atoms_ref[:, h : h + wide],
            (atom_row + h == mine).astype(jnp.float32),
            precision=lax.Precision.HIGHEST,
            preferred_element_type=jnp.float32,
        )
    places_ref[...] = places
    blocks = points_ref.shape[1] // pts
    slot_rows = lax.broadcasted_iota(jnp.int32, (listed, pts), 0)
    lane = lax.broadcasted_iota(jnp.int32, (listed, pts), 1)
    earlier = (slot_rows < lane).astype(jnp.bfloat16)
    counts = jnp.zeros((listed, 1), jnp.float32)
    ranks, hots = [], []
    for g in range(blocks):
        at = pl.ds(g * pts, pts)
        same = slot_rows == slots_ref[:, at]
        hot = same.astype(jnp.float32)
        inside = jnp.dot(hot.astype(jnp.bfloat16), earlier, preferred_element_type=jnp.float32)
        ranks.append(jnp.sum(hot * (inside + counts), axis=0, keepdims=True))
        counts = counts + jnp.sum(hot, axis=1, keepdims=True)
    below = (lax.broadcasted_iota(jnp.int32, (listed, listed), 1) < lax.broadcasted_iota(
        jnp.int32, (listed, listed), 0
    )).astype(jnp.float32)
    counts_full = jnp.broadcast_to(counts, (listed, listed))
    starts_full = jnp.dot(
        below, counts_full, precision=lax.Precision.HIGHEST, preferred_element_type=jnp.float32
    )
    starts = starts_full[:, 0:1]
    packed = starts_full * 4096.0 + counts_full
    rows64 = lax.broadcasted_iota(jnp.int32, (4 * blocks, pts), 0) // 4
    sorted_rows = jnp.zeros((4 * blocks, pts), jnp.float32)
    moments = jnp.zeros((16, listed), jnp.float32)
    q_rows[...] = jnp.zeros_like(q_rows)
    for g in range(blocks):
        at = pl.ds(g * pts, pts)
        hot = (slot_rows == slots_ref[:, at]).astype(jnp.float32)
        place = ranks[g] + jnp.sum(hot * starts, axis=0, keepdims=True)
        place = place.astype(jnp.int32)
        atom = jnp.dot(
            places, hot, precision=lax.Precision.HIGHEST, preferred_element_type=jnp.float32
        )
        dx = points_ref[0:1, at] - atom[0:1]
        dy = points_ref[1:2, at] - atom[1:2]
        dz = points_ref[2:3, at] - atom[2:3]
        weight = density_ref[:, at]
        for r in range(2):
            for c, value in enumerate((dx, dy, dz, weight)):
                four_ref[4 * r + c : 4 * r + c + 1, :] = value
        tiled = jnp.concatenate([four_ref[...]] * (blocks // 2), axis=0)
        masked = jnp.where(rows64 == place // pts, tiled, 0.0)
        target = (slot_rows == place % pts).astype(jnp.bfloat16)
        for piece in split3(masked):
            sorted_rows = sorted_rows + lax.dot_general(
                piece.astype(jnp.bfloat16),
                target,
                (((1,), (1,)), ((), ())),
                preferred_element_type=jnp.float32,
            )
        square = dx * dx + dy * dy + dz * dz + 1.0
        inv = lax.rsqrt(square)
        rho = square * inv
        radial = radial_values(rho, rate_ref, jnp.float32)
        levels = jnp.dot(
            table_ref[...], radial, precision=lax.Precision.HIGHEST, preferred_element_type=jnp.float32
        )

        def emit(i, value):
            degree = (0, 1, 1, 1, 2, 2, 2, 2, 2)[i]
            q_rows[i : i + 1, :] = value * weight * levels[degree : degree + 1]

        harmonic_rows(dx * inv, dy * inv, dz * inv, 2, emit)
        moments = moments + lax.dot_general(
            q_rows[...],
            hot,
            (((1,), (1,)), ((), ())),
            precision=lax.Precision.HIGHEST,
            preferred_element_type=jnp.float32,
        )
    sorted_ref[0 : 4 * blocks, :] = sorted_rows
    sorted_ref[4 * blocks : 4 * blocks + 1, :] = packed.T[0:1, :]
    sorted_ref[4 * blocks + 1 : 4 * blocks + 10, :] = moments[0:9]
    sorted_ref[4 * blocks + 10 : 4 * blocks + 12, :] = jnp.zeros((2, listed), jnp.float32)
    for m in range(blocks + 3):
        out_ref[m] = sorted_ref[4 * m : 4 * m + 4, :]
    entry_tables(lists_ref, mine, codes_ref, plan_ref, held_ref)


def point_blocks(points, density, slots, decay_rates, moment_table, lists, atom_pos, pts):
    count = points.shape[1]
    devices, listed = lists.shape
    shells = decay_rates.shape[0]
    tiles = count // pts + 3
    plans = (listed * (devices // PER) + GROUP + listed - 1) // listed + 1
    arrays = (
        points,
        density.reshape(1, count),
        slots.reshape(1, count),
        moment_table,
        lists,
        atom_pos,
        decay_rates.reshape(1, shells),
    )
    vmem = pl.BlockSpec(memory_space=pltpu.VMEM)
    return pl.pallas_call(
        point_blocks_kernel,
        out_shape=(
            jax.ShapeDtypeStruct((tiles, 4, pts), jnp.float32),
            jax.ShapeDtypeStruct((devices + 8, listed), jnp.int32),
            jax.ShapeDtypeStruct((plans, listed), jnp.int32),
            jax.ShapeDtypeStruct((3, listed), jnp.float32),
            jax.ShapeDtypeStruct((shells, pts), jnp.float32),
        ),
        in_specs=[pl.BlockSpec(memory_space=pltpu.HBM)] * len(arrays),
        out_specs=(vmem,) * 5,
        scratch_shapes=[pltpu.VMEM(array.shape, array.dtype) for array in arrays]
        + [
            pltpu.SemaphoreType.DMA((len(arrays),)),
            pltpu.VMEM((8, pts), jnp.float32),
            pltpu.VMEM((16, pts), jnp.float32),
            pltpu.VMEM((devices, listed), jnp.float32),
            pltpu.VMEM((4 * tiles, pts), jnp.float32),
        ],
        name="point_blocks",
    )(*arrays)


MESH = pl.DeviceIdType.MESH
SIDE = 4


def gather_kernel(cuts, mine_ref, all_ref, local_sem, send_sems, recv_sems, swap_send, swap_recv):
    row, column = lax.axis_index("sx"), lax.axis_index("sy")
    core = lax.rem(row, 2)
    here = {"z": row // 2, "y": column // SIDE, "x": lax.rem(column, SIDE)}

    def device(place, on_core):
        return (place["z"] * 2 + on_core, place["y"] * SIDE + place["x"])

    def moved(axis, offset):
        place = dict(here)
        place[axis] = lax.rem(here[axis] + offset, SIDE)
        return place

    def region(place, whole, part):
        index = [pl.ds(0, SIDE) if a in whole else place[a] for a in ("z", "y", "x")]
        return all_ref.at[index[0], core, index[1], index[2], part]

    barrier = pltpu.get_barrier_semaphore()
    for axis in ("z", "y", "x"):
        for offset in range(1, SIDE):
            pl.semaphore_signal(
                barrier, inc=1, device_id=device(moved(axis, offset), core), device_id_type=MESH
            )
    pl.semaphore_signal(barrier, inc=1, device_id=device(here, 1 - core), device_id_type=MESH)
    pl.semaphore_wait(barrier, 3 * (SIDE - 1) + 1)

    local = pltpu.make_async_copy(mine_ref, region(here, "", pl.ds(0, cuts[-1])), local_sem)
    local.start()
    orders = ("xyz", "yzx", "zxy")
    parts = [pl.ds(cuts[c], cuts[c + 1] - cuts[c]) for c in range(3)]
    hops = {}
    swaps = []

    def send(c, phase):
        axis = orders[c][phase]
        whole = orders[c][:phase]
        for offset in range(1, SIDE):
            place = region(here, whole, parts[c])
            copy = pltpu.make_async_remote_copy(
                src_ref=mine_ref.at[parts[c]] if phase == 0 else place,
                dst_ref=place,
                send_sem=send_sems.at[c, phase, offset],
                recv_sem=recv_sems.at[c, phase, offset],
                device_id=device(moved(axis, offset), core),
                device_id_type=MESH,
            )
            copy.start()
            hops[c, phase, offset] = copy

    def swap(c, slot, place):
        area = region(place, orders[c][:2], parts[c])
        copy = pltpu.make_async_remote_copy(
            src_ref=area,
            dst_ref=area,
            send_sem=swap_send.at[c, slot],
            recv_sem=swap_recv.at[c, slot],
            device_id=device(here, 1 - core),
            device_id_type=MESH,
        )
        copy.start()
        swaps.append(copy)

    for c in range(3):
        send(c, 0)
    local.wait()
    for phase in (1, 2):
        for c in range(3):
            for offset in range(1, SIDE):
                hops[c, phase - 1, offset].wait_recv()
            send(c, phase)
    for c in range(3):
        swap(c, 0, here)
    for offset in range(1, SIDE):
        for c in range(3):
            hops[c, 2, offset].wait_recv()
            swap(c, offset, moved(orders[c][2], SIDE - offset))
    for copy in hops.values():
        copy.wait_send()
    for copy in swaps:
        copy.wait()


def gather_blocks(mine):
    blocks = mine.shape[0]
    cuts = (0, blocks // 3, 2 * blocks // 3, blocks)
    return pl.pallas_call(
        functools.partial(gather_kernel, cuts),
        out_shape=jax.ShapeDtypeStruct((SIDE, 2, SIDE, SIDE) + mine.shape, mine.dtype),
        in_specs=[pl.BlockSpec(memory_space=pl.ANY)],
        out_specs=pl.BlockSpec(memory_space=pl.ANY),
        scratch_shapes=[
            pltpu.SemaphoreType.DMA,
            pltpu.SemaphoreType.DMA((3, 3, SIDE)),
            pltpu.SemaphoreType.DMA((3, 3, SIDE)),
            pltpu.SemaphoreType.DMA((3, SIDE)),
            pltpu.SemaphoreType.DMA((3, SIDE)),
        ],
        compiler_params=pltpu.CompilerParams(collective_id=0, has_side_effects=True),
        name="gather_blocks",
    )(mine)


CHUNK = 32
PER = 4
LONG = 64
GROUP = 32


def project_kernel(
    lists,
    plan_ref,
    codes_ref,
    words_ref,
    runs_ref,
    blocks_ref,
    rate_ref,
    green_ref,
    pot_ref,
    buffer,
    owner_ref,
    extra_ref,
    extra_code,
    extra_owner,
    y_rows,
    rho_rows,
    coefs_ref,
):
    listed = codes_ref.shape[1]
    pts = rate_ref.shape[1]
    coefs_ref[...] = jnp.zeros_like(coefs_ref)
    y_rows[...] = jnp.zeros_like(y_rows)
    buffer[...] = jnp.zeros_like(buffer)
    for f in range(2 * GROUP):
        owner_ref[f] = 0
    extra_ref[0] = 0
    lane = lax.broadcasted_iota(jnp.int32, (4, pts), 1)
    held = blocks_ref.shape[0] // lists

    def window(tile, off, left):
        value = jnp.where(lane >= off, blocks_ref[tile], blocks_ref[tile + 1])
        return pltpu.roll(value, lax.bitwise_and(left + 128 - off, 127), 1)

    def collect(g, half):
        owners, values, codes = [], [], []
        marks = jnp.int32(0)
        for f in range(GROUP):
            plan = plan_ref[g * GROUP + f]
            j = lax.shift_right_logical(plan, 12)
            r = lax.bitwise_and(plan, 4095)
            owners.append(j)
            value = jnp.zeros((4, pts), jnp.float32)
            for v in range(PER):
                code = codes_ref[r + v, j]
                word = words_ref[code]
                left = v * CHUNK
                moved = window(
                    lax.shift_right_logical(word, 16),
                    lax.bitwise_and(lax.shift_right_logical(word, 8), 127),
                    left,
                )
                right = left + lax.bitwise_and(word, 63)
                fresh = jnp.where(lane < right, moved, 0.0)
                value = fresh if v == 0 else jnp.where(lane < left, value, fresh)
                marks = lax.bitwise_or(marks, word)
                codes.append(code)
            values.append(value)
        for f in range(GROUP):
            row = half * GROUP + f
            buffer[pl.ds(row * 4, 4), :] = values[f]
            owner_ref[row] = owners[f]
        return marks, codes, owners

    def note(fresh, marks, codes, owners):
        @pl.when(fresh & (lax.bitwise_and(marks, LONG) > 0))
        def _():
            for n, code in enumerate(codes):

                @pl.when(lax.bitwise_and(words_ref[code], LONG) > 0)
                def _():
                    at = extra_ref[0]
                    extra_code[at] = code
                    extra_owner[at] = owners[n // PER]
                    extra_ref[0] = at + 1

    def flush(half):
        def component(c):
            return buffer[pl.ds(half * (4 * GROUP) + c, GROUP, stride=4), :]

        dx, dy, dz, weight = (component(c) for c in range(4))
        square = dx * dx + dy * dy + dz * dz + 1.0
        inv = lax.rsqrt(square)
        rho_rows[...] = square * inv

        def emit(i, value):
            y_rows[pl.ds(i, GROUP, stride=HP), :] = value * weight

        harmonic_rows(dx * inv, dy * inv, dz * inv, 6, emit)
        sums = []
        for f in range(GROUP):
            radial = radial_values(rho_rows[f : f + 1, :], rate_ref)
            rows = y_rows[f * HP : (f + 1) * HP, :].astype(jnp.bfloat16)
            sums.append(
                lax.dot_general(
                    rows, radial, (((1,), (1,)), ((), ())), preferred_element_type=jnp.float32
                )
            )
        for f in range(GROUP):
            at = pl.ds(pl.multiple_of(owner_ref[half * GROUP + f] * YR, 8), YR)
            coefs_ref[at, :] = coefs_ref[at, :] + sums[f][0:YR]

    groups = (plan_ref[plan_ref.shape[0] - rate_ref.shape[1]] + (GROUP - 1)) // GROUP
    note(groups > 0, *collect(0, 0))

    @pl.loop(0, groups)
    def _(g):
        half = lax.bitwise_and(g, 1)
        later = jnp.minimum(g + 1, groups - 1)
        found = collect(later, 1 - half)
        flush(half)
        note(later > g, *found)

    @pl.when(extra_ref[0] > 0)
    def _():
        buffer[...] = jnp.zeros_like(buffer)
        extra_ref[1] = 0

        @pl.loop(0, extra_ref[0])
        def _(n):
            code = extra_code[n]
            device = lax.shift_right_logical(code, 7)
            run = runs_ref[device, lax.bitwise_and(code, 127)]
            start = lax.shift_right_logical(run, 12) + CHUNK
            length = lax.bitwise_and(run, 4095) - CHUNK

            @pl.loop(0, lax.shift_right_logical(length + (pts - 1), 7))
            def _(c):
                row = extra_ref[1]
                place = start + c * pts
                tile = device * held + lax.shift_right_logical(place, 7)
                moved = window(tile, lax.bitwise_and(place, 127), 0)
                buffer[pl.ds(row * 4, 4), :] = jnp.where(lane < length - c * pts, moved, 0.0)
                owner_ref[row] = extra_owner[n]
                extra_ref[1] = row + 1

                @pl.when(row + 1 == GROUP)
                def _():
                    flush(0)
                    buffer[...] = jnp.zeros_like(buffer)
                    extra_ref[1] = 0

        flush(0)

    for l in range(7):
        top = green_ref[l]
        high = top.astype(jnp.bfloat16)
        low = (top - high.astype(jnp.float32)).astype(jnp.bfloat16)
        half = jnp.concatenate([high, low], axis=1)
        table = jnp.concatenate([half, half], axis=0)
        for i in range(l * l, (l + 1) * (l + 1)):
            at = pl.ds(i, listed, stride=YR)
            rows = coefs_ref[at, :]
            big = rows.astype(jnp.bfloat16)
            small = (rows - big.astype(jnp.float32)).astype(jnp.bfloat16)
            both = jnp.dot(
                jnp.concatenate([big, small], axis=1), table, preferred_element_type=jnp.float32
            )
            coefs_ref[at, :] = both[:, 0:128] + both[:, 128:256]

    @pl.loop(0, listed // 8)
    def _(g):
        for v in range(8):
            j = g * 8 + v
            rows = coefs_ref[pl.ds(pl.multiple_of(j * YR, 8), YR), :]
            pot_ref[j] = jnp.concatenate(
                [rows, jnp.zeros((HP - YR, rows.shape[1]), jnp.float32)], axis=0
            ).astype(jnp.bfloat16)


def project(plan, codes, words, runs, blocks, rate, green):
    lists, listed = runs.shape
    pts = rate.shape[1]
    smem = pl.BlockSpec(memory_space=pltpu.SMEM)
    vmem = pl.BlockSpec(memory_space=pltpu.VMEM)
    return pl.pallas_call(
        functools.partial(project_kernel, lists),
        out_shape=jax.ShapeDtypeStruct((listed, HP, NRAD), jnp.bfloat16),
        in_specs=[smem] * 4 + [vmem] * 3,
        out_specs=vmem,
        scratch_shapes=[
            pltpu.VMEM((2 * GROUP * 4 + 8, pts), jnp.float32),
            pltpu.SMEM((2 * GROUP,), jnp.int32),
            pltpu.SMEM((2,), jnp.int32),
            pltpu.SMEM((codes.size,), jnp.int32),
            pltpu.SMEM((codes.size,), jnp.int32),
            pltpu.VMEM(((GROUP + 1) * HP, pts), jnp.float32),
            pltpu.VMEM((GROUP, pts), jnp.float32),
            pltpu.VMEM((YR * (listed + 1), NRAD), jnp.float32),
        ],
        compiler_params=pltpu.CompilerParams(vmem_limit_bytes=40 << 20),
        name="project",
    )(plan.reshape(-1), codes, words.reshape(-1), runs, blocks, rate, green)


def scatter_kernel(
    blocks_ref, atoms_ref, places_ref, out_ref, info_ref, words_ref, runs_ref, acc_ref
):
    devices, listed = atoms_ref.shape
    held = blocks_ref.shape[1]
    wide = 256
    mine_row = own_row(atoms_ref)
    acc_ref[...] = jnp.zeros_like(acc_ref)
    column = lax.broadcasted_iota(jnp.int32, (wide, listed), 0)
    groups = acc_ref.shape[0] // 32
    steps = 8

    @pl.loop(0, devices // steps)
    def _(g):
        total = acc_ref[...]
        packed = []
        for v in range(0, steps, 2):
            targets, parts = [], []
            for q in (g * steps + v, g * steps + v + 1):
                ids = atoms_ref[pl.ds(q, 1), :]
                targets.append(
                    (column == lax.bitwise_and(ids, wide - 1)).astype(jnp.bfloat16)
                )
                group = lax.shift_right_logical(ids, 8)
                tiles = [blocks_ref[q, held - 3 + m] for m in range(3)]
                packed.append(tiles[0][0:1])
                mom = jnp.concatenate(tiles + [jnp.zeros((4, listed), jnp.float32)], axis=0)
                top = mom.astype(jnp.bfloat16).astype(jnp.float32)
                both = [
                    jnp.where(group == h, half, 0.0)
                    for h in range(groups)
                    for half in (top, mom - top)
                ]
                parts.append(jnp.concatenate(both, axis=0).astype(jnp.bfloat16))
            total = total + lax.dot_general(
                jnp.concatenate(parts, axis=1),
                jnp.concatenate(targets, axis=1),
                (((1,), (1,)), ((), ())),
                preferred_element_type=jnp.float32,
            )
        acc_ref[...] = total
        at = pl.ds(pl.multiple_of(g * steps, steps), steps)
        run = jnp.concatenate(packed, axis=0).astype(jnp.int32)
        runs_ref[at, :] = run
        start, length = lax.shift_right_logical(run, 12), lax.bitwise_and(run, 4095)
        device = g * steps + lax.broadcasted_iota(jnp.int32, (steps, listed), 0)
        tile = device * held + lax.shift_right_logical(start, 7)
        word = tile * 65536 + lax.bitwise_and(start, 127) * 256 + jnp.minimum(length, CHUNK)
        words_ref[at, :] = word + jnp.where(length > CHUNK, LONG, 0)

    words_ref[devices : devices + 8, :] = jnp.zeros((8, listed), jnp.int32)
    mine = jnp.zeros((16, listed), jnp.float32)
    for h in range(groups):
        both = acc_ref[h * 32 : h * 32 + 16, :] + acc_ref[h * 32 + 16 : h * 32 + 32, :]
        out_ref[:, h * wide : (h + 1) * wide] = both[1:10]
        mine = mine + jnp.dot(
            both,
            (column + h * wide == mine_row).astype(jnp.float32),
            precision=lax.Precision.HIGHEST,
            preferred_element_type=jnp.float32,
        )
    info_ref[...] = jnp.zeros_like(info_ref)
    info_ref[0:3, :] = places_ref[...]
    info_ref[3:12, :] = mine[1:10]


def scatter_moments(blocks, lists, places, atoms):
    devices, listed = lists.shape
    vmem = pl.BlockSpec(memory_space=pltpu.VMEM)
    return pl.pallas_call(
        scatter_kernel,
        out_shape=(
            jax.ShapeDtypeStruct((9, atoms), jnp.float32),
            jax.ShapeDtypeStruct((16, listed), jnp.float32),
            jax.ShapeDtypeStruct((devices + 8, listed), jnp.int32),
            jax.ShapeDtypeStruct((devices, listed), jnp.int32),
        ),
        in_specs=[vmem] * 3,
        out_specs=(vmem,) * 4,
        scratch_shapes=[pltpu.VMEM((atoms // 256 * 32, 256), jnp.float32)],
        compiler_params=pltpu.CompilerParams(vmem_limit_bytes=40 << 20),
        name="scatter_moments",
    )(blocks, lists, places)


def per_device(
    grid_points,
    weighted_density,
    point_slot,
    near_slot,
    slot_atom,
    atom_pos,
    decay_rates,
    green,
    moment_table,
):
    devices = lax.axis_size("sx") * lax.axis_size("sy")
    lists = slot_atom.reshape(devices, -1)
    atoms = atom_pos.shape[1]
    pts = grid_points.shape[1] // near_slot.shape[0]
    mine, codes, plan, places, rate = point_blocks(
        grid_points, weighted_density, point_slot, decay_rates, moment_table, lists, atom_pos, pts
    )
    gathered = gather_blocks(mine)
    blocks = gathered.reshape((devices,) + mine.shape)
    moments, slot_table, words, runs = scatter_moments(blocks, lists, places, atoms)
    tiles = gathered.reshape((-1,) + mine.shape[1:])
    slot_pot = project(plan, codes, words, runs, tiles, rate, green)
    return evaluate(
        grid_points, near_slot, slot_table, slot_pot, atom_pos, moments, rate
    )


def solution(mesh):
    return jax.shard_map(
        per_device,
        mesh=mesh,
        in_specs=(
            P(None, ("sx", "sy")),
            P(("sx", "sy")),
            P(("sx", "sy")),
            P(("sx", "sy"), None),
            P(),
            P(),
            P(),
            P(),
            P(),
        ),
        out_specs=P(("sx", "sy")),
        check_vma=False,
    )
```

```python
import functools
import math

import jax
import jax.numpy as jnp
from jax import lax
from jax.experimental import pallas as pl
from jax.experimental.pallas import tpu as pltpu
from jax.sharding import PartitionSpec as P

HARM = 49
NRAD = 128


HP = 64
YR = 56


def y_factor(l, m):
    factor = math.sqrt(
        (2 * l + 1) / (4 * math.pi) * math.factorial(l - m) / math.factorial(l + m)
    )
    return factor if m == 0 else factor * math.sqrt(2.0)


def harmonic_rows(x, y, z, top, emit):
    square = x * x + y * y + z * z
    cos_m, sin_m = None, None
    for m in range(top + 1):
        if m == 1:
            cos_m, sin_m = x, y
        elif m > 1:
            cos_m, sin_m = cos_m * x - sin_m * y, cos_m * y + sin_m * x
        double = float(math.prod(range(1, 2 * m, 2)))
        ladder = {}
        for l in range(m, top + 1):
            if l == m + 1:
                ladder[l] = z * float(2 * m + 1)
            elif l == m + 2:
                ladder[l] = z * ladder[l - 1] * ((2 * l - 1) / 2) - square * ((l + m - 1) / 2)
            elif l > m + 2:
                ladder[l] = z * ladder[l - 1] * ((2 * l - 1) / (l - m)) - square * ladder[l - 2] * (
                    (l + m - 1) / (l - m)
                )
            scale = y_factor(l, m) * double
            part = ladder[l] * scale if l > m else scale
            if m == 0:
                emit(l * l, part if l > m else jnp.full_like(x, part))
            else:
                emit(l * l + 2 * m - 1, cos_m * part)
                emit(l * l + 2 * m, sin_m * part)


def split3(value):
    high = value.astype(jnp.bfloat16).astype(jnp.float32)
    rest = value - high
    middle = rest.astype(jnp.bfloat16).astype(jnp.float32)
    return high, middle, rest - middle


SPACING = 27.0 / (NRAD - 1)
SHELL_ROWS = 16


def radial_values(rho, rate_ref, dtype=jnp.bfloat16):
    rows, pts = SHELL_ROWS, rho.shape[1]
    shell = lax.broadcasted_iota(jnp.int32, (rows, pts), 0).astype(jnp.float32)
    base = jnp.broadcast_to(rho, (rows, pts)) - (1.0 + SPACING * shell)
    pieces = []
    for k in range(0, NRAD, rows):
        e = base - (SPACING * k)
        power = (e * e) * rate_ref[k : k + rows, :]
        pieces.append(jnp.exp2(power.astype(dtype)))
    return jnp.concatenate(pieces, axis=0)


FARC = 8
FEATURES = 9
FEATURE_ROWS = 6 * FEATURES + 3
FAR_ROWS = 64


def far_tables(atoms_ref, moments_ref, rows_ref, table_ref):
    atoms = atoms_ref.shape[1]
    ax = atoms_ref[0:1, :] - 8.0
    ay = atoms_ref[1:2, :] - 8.0
    az = atoms_ref[2:3, :] - 8.0
    mom = [moments_ref[i : i + 1, :] for i in range(9)]
    one, nil = jnp.ones_like(ax), jnp.zeros_like(ax)
    n10, n11 = y_factor(1, 0), y_factor(1, 1)
    vx, vy, vz = mom[2] * n11, mom[3] * n11, mom[1] * n10
    f20, f21, f22 = y_factor(2, 0), 3.0 * y_factor(2, 1), 3.0 * y_factor(2, 2)
    qzz = mom[4] * f20
    qxx = mom[7] * f22 - qzz * 0.5
    qyy = -mom[7] * f22 - qzz * 0.5
    qxz, qyz, qxy = mom[5] * f21, mom[6] * f21, mom[8] * (2.0 * f22)
    gx = -(2.0 * qxx * ax + qxy * ay + qxz * az)
    gy = -(qxy * ax + 2.0 * qyy * ay + qyz * az)
    gz = -(qxz * ax + qyz * ay + 2.0 * qzz * az)
    const = -0.5 * (gx * ax + gy * ay + gz * az)
    norm = ax * ax + ay * ay + az * az + 1.0
    plans = [
        ([-2.0 * ax, -2.0 * ay, -2.0 * az, one, one, one, nil, nil, nil], norm),
        ([vx, vy, vz, nil, nil, nil, nil, nil, nil], -(vx * ax + vy * ay + vz * az)),
        ([gx, gy, gz, qxx, qyy, qzz, qxy, qxz, qyz], const),
    ]
    for q, (coefs, fixed) in enumerate(plans):
        columns = pl.ds(q * atoms, atoms)
        for f, coef in enumerate(coefs):
            high, middle, low = split3(coef)
            for r, row in enumerate((high, middle, high, low, high, middle)):
                rows_ref[6 * f + r : 6 * f + r + 1, columns] = row
        for r, row in enumerate(split3(fixed)):
            rows_ref[6 * FEATURES + r : 6 * FEATURES + r + 1, columns] = row
        rows_ref[FEATURE_ROWS:FAR_ROWS, columns] = jnp.zeros(
            (FAR_ROWS - FEATURE_ROWS, atoms), jnp.float32
        )
    table_ref[...] = rows_ref[...].astype(jnp.bfloat16)


def point_features(px, py, pz, rows_ref):
    qx, qy, qz = px - 8.0, py - 8.0, pz - 8.0
    values = [qx, qy, qz, qx * qx, qy * qy, qz * qz, qx * qy, qx * qz, qy * qz]
    for f, value in enumerate(values):
        high, middle, low = split3(value)
        for r, row in enumerate((high, high, middle, high, low, middle)):
            rows_ref[6 * f + r : 6 * f + r + 1, :] = row
    rows_ref[6 * FEATURES : FEATURE_ROWS, :] = jnp.ones((3, qx.shape[1]), jnp.float32)
    rows_ref[FEATURE_ROWS:FAR_ROWS, :] = jnp.zeros(
        (FAR_ROWS - FEATURE_ROWS, qx.shape[1]), jnp.float32
    )
    return rows_ref[...].T.astype(jnp.bfloat16)


def evaluate_kernel(
    near_smem,
    near_ref,
    points_ref,
    slot_table_ref,
    slot_pot_ref,
    atoms_ref,
    moments_ref,
    rate_ref,
    out_ref,
    far_rows,
    far_table,
    feat_rows,
    far_acc,
    y_rows,
    rho_rows,
    corr_ref,
):
    b = pl.program_id(0)
    near_count = near_ref.shape[2]
    pts = points_ref.shape[1]
    atoms = atoms_ref.shape[1]

    @pl.when(b == 0)
    def _():
        far_tables(atoms_ref, moments_ref, far_rows, far_table)
        y_rows[...] = jnp.zeros_like(y_rows)

    px, py, pz = points_ref[0:1, :], points_ref[1:2, :], points_ref[2:3, :]

    features = point_features(px, py, pz, feat_rows)
    far_acc[...] = jnp.zeros_like(far_acc)
    chunk = 256

    for c in range(FARC):
        base = c * chunk

        def table(q):
            return far_table[:, q * atoms + base : q * atoms + base + chunk]

        square = jnp.dot(features, table(0), preferred_element_type=jnp.float32)
        linear = jnp.dot(features, table(1), preferred_element_type=jnp.float32)
        quad = jnp.dot(features, table(2), preferred_element_type=jnp.float32)
        inv = lax.rsqrt(square)
        inv2 = inv * inv
        level = moments_ref[0:1, pl.ds(base, chunk)] * y_factor(0, 0)
        value = inv * (level + inv2 * (linear + inv2 * quad))
        far_acc[...] += value[:, 0:128] + value[:, 128:256]

    far_row = jnp.sum(far_acc[...].T, axis=0, keepdims=True)

    hot = (
        lax.broadcasted_iota(jnp.int32, (slot_table_ref.shape[1], near_count), 0) == near_ref[0]
    ).astype(jnp.float32)
    info = lax.dot_general(
        hot,
        slot_table_ref[...],
        (((0,), (1,)), ((), ())),
        precision=lax.Precision.HIGHEST,
        preferred_element_type=jnp.float32,
    )
    step = 32
    corr = jnp.zeros((step, pts), jnp.float32)
    for j in range(0, near_count, step):
        part = info[j : j + step, :]
        dx = px - part[:, 0:1]
        dy = py - part[:, 1:2]
        dz = pz - part[:, 2:3]
        square = dx * dx + dy * dy + dz * dz + 1.0
        inv = lax.rsqrt(square)
        rho_rows[j : j + step, :] = square * inv
        low = {}

        def emit(i, value):
            y_rows[pl.ds(j * YR + i, step, stride=YR), :] = value
            if i < 9:
                low[i] = value

        harmonic_rows(dx * inv, dy * inv, dz * inv, 6, emit)
        term = [part[:, 3 + i : 4 + i] * low[i] for i in range(9)]
        degree1 = term[1] + term[2] + term[3]
        degree2 = (term[4] + term[5]) + (term[6] + term[7]) + term[8]
        corr = corr + inv * (term[0] + inv * (degree1 + inv * degree2))
    corr_ref[...] = corr

    unroll = 32

    def pairs(g, total):
        for v in range(unroll):
            j = g * unroll + v
            coefs = slot_pot_ref[near_smem[b, j]]
            radial = radial_values(rho_rows[pl.ds(j, 1), :], rate_ref)
            values = jnp.dot(coefs, radial, preferred_element_type=jnp.float32)
            rows = y_rows[pl.ds(pl.multiple_of(j * YR, YR), YR), :]
            total = total + values[0:YR] * rows
        return total

    total = lax.fori_loop(
        0, near_count // unroll, pairs, jnp.zeros((YR, pts), jnp.float32)
    )
    near_row = jnp.sum(total, axis=0, keepdims=True)
    out_ref[0] = near_row + far_row - jnp.sum(corr_ref[...], axis=0, keepdims=True)


def evaluate(points, near_slot, slot_table, slot_pot, atom_pos, moments, rate):
    batches, near_count = near_slot.shape
    pts = points.shape[1] // batches
    atoms = atom_pos.shape[1]
    def whole(shape):
        return pl.BlockSpec(shape, lambda b, near: (0,) * len(shape))

    out = pl.pallas_call(
        evaluate_kernel,
        out_shape=jax.ShapeDtypeStruct((batches, 1, pts), jnp.float32),
        grid_spec=pltpu.PrefetchScalarGridSpec(
            num_scalar_prefetch=1,
            grid=(batches,),
            in_specs=[
                pl.BlockSpec((1, 1, near_count), lambda b, near: (b, 0, 0)),
                pl.BlockSpec((3, pts), lambda b, near: (0, b)),
                whole(slot_table.shape),
                whole(slot_pot.shape),
                whole(atom_pos.shape),
                whole(moments.shape),
                whole(rate.shape),
            ],
            out_specs=pl.BlockSpec((1, 1, pts), lambda b, near: (b, 0, 0)),
            scratch_shapes=[
                pltpu.VMEM((FAR_ROWS, 3 * atoms), jnp.float32),
                pltpu.VMEM((FAR_ROWS, 3 * atoms), jnp.bfloat16),
                pltpu.VMEM((FAR_ROWS, pts), jnp.float32),
                pltpu.VMEM((pts, 128), jnp.float32),
                pltpu.VMEM(((near_count + 1) * YR, pts), jnp.float32),
                pltpu.VMEM((near_count, pts), jnp.float32),
                pltpu.VMEM((32, pts), jnp.float32),
            ],
        ),
        compiler_params=pltpu.CompilerParams(
            dimension_semantics=("arbitrary",), vmem_limit_bytes=40 << 20
        ),
        name="evaluate",
    )(
        near_slot,
        near_slot.reshape(batches, 1, near_count),
        points,
        slot_table,
        slot_pot,
        atom_pos,
        moments,
        rate,
    )
    return out.reshape(-1)


def entry_tables(lists_ref, mine, codes_ref, plan_ref, held_ref):
    devices, listed = lists_ref.shape
    shape = (listed, listed)
    row = lax.broadcasted_iota(jnp.int32, shape, 0)
    column = lax.broadcasted_iota(jnp.int32, shape, 1)
    turned = lists_ref[...].astype(jnp.float32).T
    mine = mine.astype(jnp.float32)
    slot = (row + 1).astype(jnp.float32)
    for q in range(devices):
        same = turned[:, q : q + 1] == mine
        held_ref[q : q + 1, :] = jnp.sum(jnp.where(same, slot, 0.0), axis=0, keepdims=True)
    held = held_ref[...]
    present = jnp.where(held > 0.0, 1.0, 0.0).astype(jnp.bfloat16)
    rank = jnp.dot(
        (column < row).astype(jnp.bfloat16), present, preferred_element_type=jnp.float32
    )
    rank = jnp.where(held > 0.0, rank, 4096.0)
    none = float(devices * listed)
    code = (row * listed).astype(jnp.float32) + held - (1.0 + none)
    for r in range(codes_ref.shape[0]):
        picked = jnp.sum(jnp.where(rank == float(r), code, 0.0), axis=0, keepdims=True)
        codes_ref[r : r + 1, :] = (picked + none).astype(jnp.int32)
    counts = lax.dot_general(
        present,
        jnp.ones(shape, jnp.bfloat16),
        (((0,), (0,)), ((), ())),
        preferred_element_type=jnp.float32,
    ).astype(jnp.int32)
    needed = lax.shift_right_logical(counts + (PER - 1), 2)
    ends = jnp.dot(
        (column <= row).astype(jnp.bfloat16),
        needed.astype(jnp.float32).astype(jnp.bfloat16),
        preferred_element_type=jnp.float32,
    ).astype(jnp.int32)
    starts = ends - needed
    total = ends[listed - 1 : listed, :]
    last = plan_ref.shape[0] - 1
    for m in range(last):
        block = column + m * listed
        inside = (block >= starts) & (block < ends)
        value = jnp.sum(
            jnp.where(inside, row * 4096 + (block - starts) * PER, 0), axis=0, keepdims=True
        )
        plan_ref[m : m + 1, :] = value + jnp.where(block[0:1, :] >= total, devices, 0)
    plan_ref[last : last + 1, :] = total


def own_row(rows_ref):
    me = lax.axis_index("sx") * lax.axis_size("sy") + lax.axis_index("sy")
    return rows_ref[pl.ds(me, 1), :]


def point_blocks_kernel(
    points_from,
    density_from,
    slots_from,
    table_from,
    lists_from,
    atoms_from,
    decay_from,
    out_ref,
    codes_ref,
    plan_ref,
    places_ref,
    rate_ref,
    points_ref,
    density_ref,
    slots_ref,
    table_ref,
    lists_ref,
    atoms_ref,
    decay_ref,
    sems,
    four_ref,
    q_rows,
    held_ref,
    sorted_ref,
):
    wanted = (
        (lists_from, lists_ref),
        (atoms_from, atoms_ref),
        (slots_from, slots_ref),
        (points_from, points_ref),
        (density_from, density_ref),
        (table_from, table_ref),
        (decay_from, decay_ref),
    )
    copies = [
        pltpu.make_async_copy(source, target, sems.at[n])
        for n, (source, target) in enumerate(wanted)
    ]
    for copy in copies:
        copy.start()
    for copy in copies:
        copy.wait()
    listed = places_ref.shape[1]
    pts = rate_ref.shape[1]
    factor = decay_ref[...] * (-math.log2(math.e) / SPACING**2)
    rate_ref[...] = jnp.broadcast_to(factor, (pts, factor.shape[1])).T
    mine = own_row(lists_ref)
    wide = 256
    atom_row = lax.broadcasted_iota(jnp.int32, (wide, listed), 0)
    places = jnp.zeros(places_ref.shape, jnp.float32)
    for h in range(0, atoms_ref.shape[1], wide):
        places = places + jnp.dot(
            atoms_ref[:, h : h + wide],
            (atom_row + h == mine).astype(jnp.float32),
            precision=lax.Precision.HIGHEST,
            preferred_element_type=jnp.float32,
        )
    places_ref[...] = places
    blocks = points_ref.shape[1] // pts
    slot_rows = lax.broadcasted_iota(jnp.int32, (listed, pts), 0)
    lane = lax.broadcasted_iota(jnp.int32, (listed, pts), 1)
    earlier = (slot_rows < lane).astype(jnp.bfloat16)
    counts = jnp.zeros((listed, 1), jnp.float32)
    ranks, hots = [], []
    for g in range(blocks):
        at = pl.ds(g * pts, pts)
        same = slot_rows == slots_ref[:, at]
        hot = same.astype(jnp.float32)
        inside = jnp.dot(hot.astype(jnp.bfloat16), earlier, preferred_element_type=jnp.float32)
        ranks.append(jnp.sum(hot * (inside + counts), axis=0, keepdims=True))
        counts = counts + jnp.sum(hot, axis=1, keepdims=True)
    below = (lax.broadcasted_iota(jnp.int32, (listed, listed), 1) < lax.broadcasted_iota(
        jnp.int32, (listed, listed), 0
    )).astype(jnp.float32)
    counts_full = jnp.broadcast_to(counts, (listed, listed))
    starts_full = jnp.dot(
        below, counts_full, precision=lax.Precision.HIGHEST, preferred_element_type=jnp.float32
    )
    starts = starts_full[:, 0:1]
    packed = starts_full * 4096.0 + counts_full
    rows64 = lax.broadcasted_iota(jnp.int32, (4 * blocks, pts), 0) // 4
    sorted_rows = jnp.zeros((4 * blocks, pts), jnp.float32)
    moments = jnp.zeros((16, listed), jnp.float32)
    q_rows[...] = jnp.zeros_like(q_rows)
    for g in range(blocks):
        at = pl.ds(g * pts, pts)
        hot = (slot_rows == slots_ref[:, at]).astype(jnp.float32)
        place = ranks[g] + jnp.sum(hot * starts, axis=0, keepdims=True)
        place = place.astype(jnp.int32)
        atom = jnp.dot(
            places, hot, precision=lax.Precision.HIGHEST, preferred_element_type=jnp.float32
        )
        dx = points_ref[0:1, at] - atom[0:1]
        dy = points_ref[1:2, at] - atom[1:2]
        dz = points_ref[2:3, at] - atom[2:3]
        weight = density_ref[:, at]
        for r in range(2):
            for c, value in enumerate((dx, dy, dz, weight)):
                four_ref[4 * r + c : 4 * r + c + 1, :] = value
        tiled = jnp.concatenate([four_ref[...]] * (blocks // 2), axis=0)
        masked = jnp.where(rows64 == place // pts, tiled, 0.0)
        target = (slot_rows == place % pts).astype(jnp.bfloat16)
        for piece in split3(masked):
            sorted_rows = sorted_rows + lax.dot_general(
                piece.astype(jnp.bfloat16),
                target,
                (((1,), (1,)), ((), ())),
                preferred_element_type=jnp.float32,
            )
        square = dx * dx + dy * dy + dz * dz + 1.0
        inv = lax.rsqrt(square)
        rho = square * inv
        radial = radial_values(rho, rate_ref, jnp.float32)
        levels = jnp.dot(
            table_ref[...], radial, precision=lax.Precision.HIGHEST, preferred_element_type=jnp.float32
        )

        def emit(i, value):
            degree = (0, 1, 1, 1, 2, 2, 2, 2, 2)[i]
            q_rows[i : i + 1, :] = value * weight * levels[degree : degree + 1]

        harmonic_rows(dx * inv, dy * inv, dz * inv, 2, emit)
        moments = moments + lax.dot_general(
            q_rows[...],
            hot,
            (((1,), (1,)), ((), ())),
            precision=lax.Precision.HIGHEST,
            preferred_element_type=jnp.float32,
        )
    sorted_ref[0 : 4 * blocks, :] = sorted_rows
    sorted_ref[4 * blocks : 4 * blocks + 1, :] = packed.T[0:1, :]
    sorted_ref[4 * blocks + 1 : 4 * blocks + 10, :] = moments[0:9]
    sorted_ref[4 * blocks + 10 : 4 * blocks + 12, :] = jnp.zeros((2, listed), jnp.float32)
    for m in range(blocks + 3):
        out_ref[m] = sorted_ref[4 * m : 4 * m + 4, :]
    entry_tables(lists_ref, mine, codes_ref, plan_ref, held_ref)


def point_blocks(points, density, slots, decay_rates, moment_table, lists, atom_pos, pts):
    count = points.shape[1]
    devices, listed = lists.shape
    shells = decay_rates.shape[0]
    tiles = count // pts + 3
    plans = (listed * (devices // PER) + GROUP + listed - 1) // listed + 1
    arrays = (
        points,
        density.reshape(1, count),
        slots.reshape(1, count),
        moment_table,
        lists,
        atom_pos,
        decay_rates.reshape(1, shells),
    )
    vmem = pl.BlockSpec(memory_space=pltpu.VMEM)
    return pl.pallas_call(
        point_blocks_kernel,
        out_shape=(
            jax.ShapeDtypeStruct((tiles, 4, pts), jnp.float32),
            jax.ShapeDtypeStruct((devices + 8, listed), jnp.int32),
            jax.ShapeDtypeStruct((plans, listed), jnp.int32),
            jax.ShapeDtypeStruct((3, listed), jnp.float32),
            jax.ShapeDtypeStruct((shells, pts), jnp.float32),
        ),
        in_specs=[pl.BlockSpec(memory_space=pltpu.HBM)] * len(arrays),
        out_specs=(vmem,) * 5,
        scratch_shapes=[pltpu.VMEM(array.shape, array.dtype) for array in arrays]
        + [
            pltpu.SemaphoreType.DMA((len(arrays),)),
            pltpu.VMEM((8, pts), jnp.float32),
            pltpu.VMEM((16, pts), jnp.float32),
            pltpu.VMEM((devices, listed), jnp.float32),
            pltpu.VMEM((4 * tiles, pts), jnp.float32),
        ],
        name="point_blocks",
    )(*arrays)


MESH = pl.DeviceIdType.MESH
SIDE = 4


def gather_kernel(cuts, mine_ref, all_ref, local_sem, send_sems, recv_sems, swap_send, swap_recv):
    row, column = lax.axis_index("sx"), lax.axis_index("sy")
    core = lax.rem(row, 2)
    here = {"z": row // 2, "y": column // SIDE, "x": lax.rem(column, SIDE)}

    def device(place, on_core):
        return (place["z"] * 2 + on_core, place["y"] * SIDE + place["x"])

    def moved(axis, offset):
        place = dict(here)
        place[axis] = lax.rem(here[axis] + offset, SIDE)
        return place

    def region(place, whole, part):
        index = [pl.ds(0, SIDE) if a in whole else place[a] for a in ("z", "y", "x")]
        return all_ref.at[index[0], core, index[1], index[2], part]

    barrier = pltpu.get_barrier_semaphore()
    for axis in ("z", "y", "x"):
        for offset in range(1, SIDE):
            pl.semaphore_signal(
                barrier, inc=1, device_id=device(moved(axis, offset), core), device_id_type=MESH
            )
    pl.semaphore_signal(barrier, inc=1, device_id=device(here, 1 - core), device_id_type=MESH)
    pl.semaphore_wait(barrier, 3 * (SIDE - 1) + 1)

    local = pltpu.make_async_copy(mine_ref, region(here, "", pl.ds(0, cuts[-1])), local_sem)
    local.start()
    orders = ("xyz", "yzx", "zxy")
    parts = [pl.ds(cuts[c], cuts[c + 1] - cuts[c]) for c in range(3)]
    hops = {}
    swaps = []

    def send(c, phase):
        axis = orders[c][phase]
        whole = orders[c][:phase]
        for offset in range(1, SIDE):
            place = region(here, whole, parts[c])
            copy = pltpu.make_async_remote_copy(
                src_ref=mine_ref.at[parts[c]] if phase == 0 else place,
                dst_ref=place,
                send_sem=send_sems.at[c, phase, offset],
                recv_sem=recv_sems.at[c, phase, offset],
                device_id=device(moved(axis, offset), core),
                device_id_type=MESH,
            )
            copy.start()
            hops[c, phase, offset] = copy

    def swap(c, slot, place):
        area = region(place, orders[c][:2], parts[c])
        copy = pltpu.make_async_remote_copy(
            src_ref=area,
            dst_ref=area,
            send_sem=swap_send.at[c, slot],
            recv_sem=swap_recv.at[c, slot],
            device_id=device(here, 1 - core),
            device_id_type=MESH,
        )
        copy.start()
        swaps.append(copy)

    for c in range(3):
        send(c, 0)
    local.wait()
    for phase in (1, 2):
        for c in range(3):
            for offset in range(1, SIDE):
                hops[c, phase - 1, offset].wait_recv()
            send(c, phase)
    for c in range(3):
        swap(c, 0, here)
    for offset in range(1, SIDE):
        for c in range(3):
            hops[c, 2, offset].wait_recv()
            swap(c, offset, moved(orders[c][2], SIDE - offset))
    for copy in hops.values():
        copy.wait_send()
    for copy in swaps:
        copy.wait()


def gather_blocks(mine):
    blocks = mine.shape[0]
    cuts = (0, blocks // 3, 2 * blocks // 3, blocks)
    return pl.pallas_call(
        functools.partial(gather_kernel, cuts),
        out_shape=jax.ShapeDtypeStruct((SIDE, 2, SIDE, SIDE) + mine.shape, mine.dtype),
        in_specs=[pl.BlockSpec(memory_space=pl.ANY)],
        out_specs=pl.BlockSpec(memory_space=pl.ANY),
        scratch_shapes=[
            pltpu.SemaphoreType.DMA,
            pltpu.SemaphoreType.DMA((3, 3, SIDE)),
            pltpu.SemaphoreType.DMA((3, 3, SIDE)),
            pltpu.SemaphoreType.DMA((3, SIDE)),
            pltpu.SemaphoreType.DMA((3, SIDE)),
        ],
        compiler_params=pltpu.CompilerParams(collective_id=0, has_side_effects=True),
        name="gather_blocks",
    )(mine)


CHUNK = 32
PER = 4
LONG = 64
GROUP = 32


def project_kernel(
    lists,
    plan_ref,
    codes_ref,
    words_ref,
    runs_ref,
    blocks_ref,
    rate_ref,
    green_ref,
    pot_ref,
    buffer,
    owner_ref,
    extra_ref,
    extra_code,
    extra_owner,
    y_rows,
    rho_rows,
    coefs_ref,
):
    listed = codes_ref.shape[1]
    pts = rate_ref.shape[1]
    coefs_ref[...] = jnp.zeros_like(coefs_ref)
    y_rows[...] = jnp.zeros_like(y_rows)
    buffer[...] = jnp.zeros_like(buffer)
    for f in range(2 * GROUP):
        owner_ref[f] = 0
    extra_ref[0] = 0
    lane = lax.broadcasted_iota(jnp.int32, (4, pts), 1)
    held = blocks_ref.shape[0] // lists

    def window(tile, off, left):
        value = jnp.where(lane >= off, blocks_ref[tile], blocks_ref[tile + 1])
        return pltpu.roll(value, lax.bitwise_and(left + 128 - off, 127), 1)

    def collect(g, half):
        owners, values, codes = [], [], []
        marks = jnp.int32(0)
        for f in range(GROUP):
            plan = plan_ref[g * GROUP + f]
            j = lax.shift_right_logical(plan, 12)
            r = lax.bitwise_and(plan, 4095)
            owners.append(j)
            value = jnp.zeros((4, pts), jnp.float32)
            for v in range(PER):
                code = codes_ref[r + v, j]
                word = words_ref[code]
                left = v * CHUNK
                moved = window(
                    lax.shift_right_logical(word, 16),
                    lax.bitwise_and(lax.shift_right_logical(word, 8), 127),
                    left,
                )
                right = left + lax.bitwise_and(word, 63)
                fresh = jnp.where(lane < right, moved, 0.0)
                value = fresh if v == 0 else jnp.where(lane < left, value, fresh)
                marks = lax.bitwise_or(marks, word)
                codes.append(code)
            values.append(value)
        for f in range(GROUP):
            row = half * GROUP + f
            buffer[pl.ds(row * 4, 4), :] = values[f]
            owner_ref[row] = owners[f]
        return marks, codes, owners

    def note(fresh, marks, codes, owners):
        @pl.when(fresh & (lax.bitwise_and(marks, LONG) > 0))
        def _():
            for n, code in enumerate(codes):

                @pl.when(lax.bitwise_and(words_ref[code], LONG) > 0)
                def _():
                    at = extra_ref[0]
                    extra_code[at] = code
                    extra_owner[at] = owners[n // PER]
                    extra_ref[0] = at + 1

    def flush(half):
        def component(c):
            return buffer[pl.ds(half * (4 * GROUP) + c, GROUP, stride=4), :]

        dx, dy, dz, weight = (component(c) for c in range(4))
        square = dx * dx + dy * dy + dz * dz + 1.0
        inv = lax.rsqrt(square)
        rho_rows[...] = square * inv

        def emit(i, value):
            y_rows[pl.ds(i, GROUP, stride=HP), :] = value * weight

        harmonic_rows(dx * inv, dy * inv, dz * inv, 6, emit)
        sums = []
        for f in range(GROUP):
            radial = radial_values(rho_rows[f : f + 1, :], rate_ref)
            rows = y_rows[f * HP : (f + 1) * HP, :].astype(jnp.bfloat16)
            sums.append(
                lax.dot_general(
                    rows, radial, (((1,), (1,)), ((), ())), preferred_element_type=jnp.float32
                )
            )
        for f in range(GROUP):
            at = pl.ds(pl.multiple_of(owner_ref[half * GROUP + f] * YR, 8), YR)
            coefs_ref[at, :] = coefs_ref[at, :] + sums[f][0:YR]

    groups = (plan_ref[plan_ref.shape[0] - rate_ref.shape[1]] + (GROUP - 1)) // GROUP
    note(groups > 0, *collect(0, 0))

    @pl.loop(0, groups)
    def _(g):
        half = lax.bitwise_and(g, 1)
        later = jnp.minimum(g + 1, groups - 1)
        found = collect(later, 1 - half)
        flush(half)
        note(later > g, *found)

    @pl.when(extra_ref[0] > 0)
    def _():
        buffer[...] = jnp.zeros_like(buffer)
        extra_ref[1] = 0

        @pl.loop(0, extra_ref[0])
        def _(n):
            code = extra_code[n]
            device = lax.shift_right_logical(code, 7)
            run = runs_ref[device, lax.bitwise_and(code, 127)]
            start = lax.shift_right_logical(run, 12) + CHUNK
            length = lax.bitwise_and(run, 4095) - CHUNK

            @pl.loop(0, lax.shift_right_logical(length + (pts - 1), 7))
            def _(c):
                row = extra_ref[1]
                place = start + c * pts
                tile = device * held + lax.shift_right_logical(place, 7)
                moved = window(tile, lax.bitwise_and(place, 127), 0)
                buffer[pl.ds(row * 4, 4), :] = jnp.where(lane < length - c * pts, moved, 0.0)
                owner_ref[row] = extra_owner[n]
                extra_ref[1] = row + 1

                @pl.when(row + 1 == GROUP)
                def _():
                    flush(0)
                    buffer[...] = jnp.zeros_like(buffer)
                    extra_ref[1] = 0

        flush(0)

    for l in range(7):
        top = green_ref[l]
        high = top.astype(jnp.bfloat16)
        low = (top - high.astype(jnp.float32)).astype(jnp.bfloat16)
        half = jnp.concatenate([high, low], axis=1)
        table = jnp.concatenate([half, half], axis=0)
        for i in range(l * l, (l + 1) * (l + 1)):
            at = pl.ds(i, listed, stride=YR)
            rows = coefs_ref[at, :]
            big = rows.astype(jnp.bfloat16)
            small = (rows - big.astype(jnp.float32)).astype(jnp.bfloat16)
            both = jnp.dot(
                jnp.concatenate([big, small], axis=1), table, preferred_element_type=jnp.float32
            )
            coefs_ref[at, :] = both[:, 0:128] + both[:, 128:256]

    @pl.loop(0, listed // 8)
    def _(g):
        for v in range(8):
            j = g * 8 + v
            rows = coefs_ref[pl.ds(pl.multiple_of(j * YR, 8), YR), :]
            pot_ref[j] = jnp.concatenate(
                [rows, jnp.zeros((HP - YR, rows.shape[1]), jnp.float32)], axis=0
            ).astype(jnp.bfloat16)


def project(plan, codes, words, runs, blocks, rate, green):
    lists, listed = runs.shape
    pts = rate.shape[1]
    smem = pl.BlockSpec(memory_space=pltpu.SMEM)
    vmem = pl.BlockSpec(memory_space=pltpu.VMEM)
    return pl.pallas_call(
        functools.partial(project_kernel, lists),
        out_shape=jax.ShapeDtypeStruct((listed, HP, NRAD), jnp.bfloat16),
        in_specs=[smem] * 4 + [vmem] * 3,
        out_specs=vmem,
        scratch_shapes=[
            pltpu.VMEM((2 * GROUP * 4 + 8, pts), jnp.float32),
            pltpu.SMEM((2 * GROUP,), jnp.int32),
            pltpu.SMEM((2,), jnp.int32),
            pltpu.SMEM((codes.size,), jnp.int32),
            pltpu.SMEM((codes.size,), jnp.int32),
            pltpu.VMEM(((GROUP + 1) * HP, pts), jnp.float32),
            pltpu.VMEM((GROUP, pts), jnp.float32),
            pltpu.VMEM((YR * (listed + 1), NRAD), jnp.float32),
        ],
        compiler_params=pltpu.CompilerParams(vmem_limit_bytes=40 << 20),
        name="project",
    )(plan.reshape(-1), codes, words.reshape(-1), runs, blocks, rate, green)


def scatter_kernel(
    blocks_ref, atoms_ref, places_ref, out_ref, info_ref, words_ref, runs_ref, acc_ref
):
    devices, listed = atoms_ref.shape
    held = blocks_ref.shape[1]
    wide = 256
    mine_row = own_row(atoms_ref)
    acc_ref[...] = jnp.zeros_like(acc_ref)
    column = lax.broadcasted_iota(jnp.int32, (wide, listed), 0)
    groups = acc_ref.shape[0] // 32
    steps = 8

    @pl.loop(0, devices // steps)
    def _(g):
        total = acc_ref[...]
        packed = []
        for v in range(0, steps, 2):
            targets, parts = [], []
            for q in (g * steps + v, g * steps + v + 1):
                ids = atoms_ref[pl.ds(q, 1), :]
                targets.append(
                    (column == lax.bitwise_and(ids, wide - 1)).astype(jnp.bfloat16)
                )
                group = lax.shift_right_logical(ids, 8)
                tiles = [blocks_ref[q, held - 3 + m] for m in range(3)]
                packed.append(tiles[0][0:1])
                mom = jnp.concatenate(tiles + [jnp.zeros((4, listed), jnp.float32)], axis=0)
                top = mom.astype(jnp.bfloat16).astype(jnp.float32)
                both = [
                    jnp.where(group == h, half, 0.0)
                    for h in range(groups)
                    for half in (top, mom - top)
                ]
                parts.append(jnp.concatenate(both, axis=0).astype(jnp.bfloat16))
            total = total + lax.dot_general(
                jnp.concatenate(parts, axis=1),
                jnp.concatenate(targets, axis=1),
                (((1,), (1,)), ((), ())),
                preferred_element_type=jnp.float32,
            )
        acc_ref[...] = total
        at = pl.ds(pl.multiple_of(g * steps, steps), steps)
        run = jnp.concatenate(packed, axis=0).astype(jnp.int32)
        runs_ref[at, :] = run
        start, length = lax.shift_right_logical(run, 12), lax.bitwise_and(run, 4095)
        device = g * steps + lax.broadcasted_iota(jnp.int32, (steps, listed), 0)
        tile = device * held + lax.shift_right_logical(start, 7)
        word = tile * 65536 + lax.bitwise_and(start, 127) * 256 + jnp.minimum(length, CHUNK)
        words_ref[at, :] = word + jnp.where(length > CHUNK, LONG, 0)

    words_ref[devices : devices + 8, :] = jnp.zeros((8, listed), jnp.int32)
    mine = jnp.zeros((16, listed), jnp.float32)
    for h in range(groups):
        both = acc_ref[h * 32 : h * 32 + 16, :] + acc_ref[h * 32 + 16 : h * 32 + 32, :]
        out_ref[:, h * wide : (h + 1) * wide] = both[1:10]
        mine = mine + jnp.dot(
            both,
            (column + h * wide == mine_row).astype(jnp.float32),
            precision=lax.Precision.HIGHEST,
            preferred_element_type=jnp.float32,
        )
    info_ref[...] = jnp.zeros_like(info_ref)
    info_ref[0:3, :] = places_ref[...]
    info_ref[3:12, :] = mine[1:10]


def scatter_moments(blocks, lists, places, atoms):
    devices, listed = lists.shape
    vmem = pl.BlockSpec(memory_space=pltpu.VMEM)
    return pl.pallas_call(
        scatter_kernel,
        out_shape=(
            jax.ShapeDtypeStruct((9, atoms), jnp.float32),
            jax.ShapeDtypeStruct((16, listed), jnp.float32),
            jax.ShapeDtypeStruct((devices + 8, listed), jnp.int32),
            jax.ShapeDtypeStruct((devices, listed), jnp.int32),
        ),
        in_specs=[vmem] * 3,
        out_specs=(vmem,) * 4,
        scratch_shapes=[pltpu.VMEM((atoms // 256 * 32, 256), jnp.float32)],
        compiler_params=pltpu.CompilerParams(vmem_limit_bytes=40 << 20),
        name="scatter_moments",
    )(blocks, lists, places)


def per_device(
    grid_points,
    weighted_density,
    point_slot,
    near_slot,
    slot_atom,
    atom_pos,
    decay_rates,
    green,
    moment_table,
):
    devices = lax.axis_size("sx") * lax.axis_size("sy")
    lists = slot_atom.reshape(devices, -1)
    atoms = atom_pos.shape[1]
    pts = grid_points.shape[1] // near_slot.shape[0]
    mine, codes, plan, places, rate = point_blocks(
        grid_points, weighted_density, point_slot, decay_rates, moment_table, lists, atom_pos, pts
    )
    gathered = gather_blocks(mine)
    blocks = gathered.reshape((devices,) + mine.shape)
    moments, slot_table, words, runs = scatter_moments(blocks, lists, places, atoms)
    tiles = gathered.reshape((-1,) + mine.shape[1:])
    slot_pot = project(plan, codes, words, runs, tiles, rate, green)
    return evaluate(
        grid_points, near_slot, slot_table, slot_pot, atom_pos, moments, rate
    )


def solution(mesh):
    return jax.shard_map(
        per_device,
        mesh=mesh,
        in_specs=(
            P(None, ("sx", "sy")),
            P(("sx", "sy")),
            P(("sx", "sy")),
            P(("sx", "sy"), None),
            P(),
            P(),
            P(),
            P(),
            P(),
        ),
        out_specs=P(("sx", "sy")),
        check_vma=False,
    )
```
